256 devices in a mesh: seq: 32 (over y, z), head: 8 (over x, core).
Axes of the slice: x: 4, y: 4, z: 8, core: 2. Of those that a mesh axis runs over, the one named last changes fastest.
Arguments:
- tokens: bfloat16 [8192, 3072], P('seq'), may hold values from -18 to 18
- w_qkv: bfloat16 [3, 3072, 2048], P(None, 'seq', 'head'), may hold values from -0.109375 to 0.109375
- gains: float32 [2, 2048], P(None, 'head'), may hold values from 0.5 to 1.5
- cotangent: bfloat16 [8192, 2048], P('seq', 'head'), may hold values from -6 to 6
- token_clip: int32 [8192], replicated, may hold values from 0 to 2, as said below
- key_live: int32 [8192], replicated, may hold values 0 or 1
- damp_mask: int32 [3072, 2048], P('seq', 'head'), may hold values 0 or 1
Outputs:
- fisher_ratio: float32 [3, 3072, 2048], P(None, 'seq', 'head')
- dampened: bfloat16 [3, 3072, 2048], P(None, 'seq', 'head')
The draws below stay inside these ranges and needn't reach their ends.
Inputs may be any that keep to these rules, and one draw needn't show every extreme that they name: token_clip never decreases along the tokens (each clip is one contiguous run of tokens); every clip has at least one token and the longest has exactly 6144.
All inputs are finite; a program needn't handle non-finite values. No bound on the sum of `damp_mask` on one device may be relied on, other than what follows from the above.
Results may differ from the reference program's by a relative error of at most 0.03.
Values may be sent and summed in bfloat16 or wider, within the bound.
A program may use at most 192 MiB of HBM per device.

```python
import math
import jax
import jax.numpy as jnp
from jax import lax

D = 3072
HD = 128
HEADS = 16
CLIPS = 3
TOK_DEV = 256
TOKENS = 8192
HID = 2048
N_SEQ = 32


def draw_tokens(key, part):
    column = jnp.arange(D, dtype=jnp.float32) / float(D - 1)
    base = jnp.clip(jax.random.normal(key, (TOKENS, D), jnp.float32), -6.0, 6.0)
    low_scale = 0.5
    high_scale = 2.0
    scales = low_scale * jnp.exp(column * jnp.log(high_scale / low_scale))
    return (base * scales[None, :]).astype(jnp.bfloat16)


def draw_token_clip(key, part):
    longest = 3 * TOKENS // 4
    remain = TOKENS - longest
    key_split = jax.random.fold_in(key, 11)
    key_place = jax.random.fold_in(key, 23)
    first_rest = jax.random.randint(key_split, (), 1, remain, dtype=jnp.int32)
    second_rest = remain - first_rest
    place = jax.random.randint(key_place, (), 0, 3, dtype=jnp.int32)
    length_zero = jnp.where(place == 0, longest, first_rest)
    length_one = jnp.where(place == 1, longest, jnp.where(place == 0, first_rest, second_rest))
    bound_one = length_zero
    bound_two = length_zero + length_one
    positions = jnp.arange(TOKENS, dtype=jnp.int32)
    return (positions >= bound_one).astype(jnp.int32) + (positions >= bound_two).astype(jnp.int32)


def touch_ends(array, key, smallest, high):
    index_at = [jax.random.randint(jax.random.fold_in(key, axis), (), 0, length) for axis, length in enumerate(array.shape)]
    widest = array.shape.index(max(array.shape))
    neighbour = index_at[:widest] + [(index_at[widest] + 1) % array.shape[widest]] + index_at[widest + 1:]
    return array.at[tuple(index_at)].set(smallest).at[tuple(neighbour)].set(high)


def block_levels(stream_key, dims, split, low, top_value):
    loudness = 1.0
    for dim, blocks in split:
        steps = jax.random.uniform(jax.random.fold_in(jax.random.fold_in(stream_key, 6), dim), (blocks,), jnp.float32, low / len(split), top_value / len(split))
        loudness = loudness * jnp.repeat(jnp.exp(steps), dims[dim] // blocks).reshape((-1,) + (1,) * (len(dims) - 1 - dim))
    return loudness


def scatter_about(rng, shape, spread, reach, pieces=(), kind=jnp.bfloat16):
    drawn = spread * jax.random.normal(rng, shape, jnp.float32)
    if pieces:
        drawn = drawn * block_levels(rng, shape, pieces, -0.22, 0.18)
    return jnp.clip(drawn, -reach, reach).astype(kind)


def setup_inputs(seed: int = 0) -> dict:
    key_list = jax.random.split(jax.random.key(seed), 8)
    return {
        "tokens": draw_tokens(jax.random.fold_in(key_list[7], 71), 0),
        "w_qkv": scatter_about(key_list[1], (3, D, HID), D ** -0.5, 0.109375, ((1, 32), (2, 8))),
        "gains": jnp.clip(1.0 + 0.1 * jax.random.normal(key_list[2], (2, HID), jnp.float32), 0.5, 1.5),
        "cotangent": scatter_about(key_list[3], (TOKENS, HID), 1.0, 6.0, ((0, 32), (1, 8))),
        "token_clip": draw_token_clip(jax.random.fold_in(key_list[7], 71), 0),
        "key_live": touch_ends((jax.random.randint(key_list[5], (TOKENS,), 0, 4) < 3).astype(jnp.int32), jax.random.fold_in(key_list[5], 1), 0, 1),
        "damp_mask": touch_ends((jax.random.randint(key_list[6], (D, HID), 0, 2) < 1).astype(jnp.int32), jax.random.fold_in(key_list[6], 1), 0, 1),
    }


def normed(values, gain_row):
    shaped = values.reshape(TOKENS, HEADS, HD)
    inverse = lax.rsqrt(lax.optimization_barrier(jnp.mean(shaped * shaped, -1, keepdims=True)) + 1e-06)
    return (shaped * inverse * gain_row.reshape(HEADS, HD), inverse, shaped)

def unnorm(upstream, shaped, inverse, gain_row):
    gain_grid = gain_row.reshape(HEADS, HD)
    cubed = inverse * inverse * inverse
    return inverse * gain_grid * upstream - shaped * cubed * lax.optimization_barrier(jnp.mean(shaped * gain_grid * upstream, -1, keepdims=True))

def reference(tokens, w_qkv, gains, cotangent, token_clip, key_live, damp_mask):
    score_scale = 1.0 / math.sqrt(HD)
    projected = [jnp.dot(tokens, w_qkv[index], preferred_element_type=jnp.float32) for index in range(3)]
    query_n, query_inv, query_raw = normed(projected[0], gains[0])
    key_n, key_inv, key_raw = normed(projected[1], gains[1])
    query_b = jnp.transpose(query_n.astype(jnp.bfloat16), (1, 0, 2))
    key_b = jnp.transpose(key_n.astype(jnp.bfloat16), (1, 0, 2))
    value_b = jnp.transpose(projected[2].astype(jnp.bfloat16).reshape(TOKENS, HEADS, HD), (1, 0, 2))
    grad_out = jnp.transpose(cotangent.reshape(TOKENS, HEADS, HD), (1, 0, 2))
    positions = jnp.arange(TOKENS, dtype=jnp.int32)
    allowed = (token_clip[:, None] == token_clip[None, :]) & ((key_live[None, :] == 1) | (positions[:, None] == positions[None, :]))

    def per_head(operands):
        head_q, head_k, head_v, head_o = operands
        scores = jnp.dot(head_q, head_k.T, preferred_element_type=jnp.float32) * score_scale
        scores = jnp.where(allowed, scores, -1e+30)
        peak = lax.optimization_barrier(jnp.max(scores, -1, keepdims=True))
        expd = jnp.exp(scores - peak)
        probs = expd / lax.optimization_barrier(jnp.sum(expd, -1, keepdims=True))
        grad_p = jnp.dot(head_o, head_v.T, preferred_element_type=jnp.float32)
        row_dot = lax.optimization_barrier(jnp.sum(probs * grad_p, -1, keepdims=True))
        ds_half = (probs * (grad_p - row_dot)).astype(jnp.bfloat16)
        probs_half = probs.astype(jnp.bfloat16)
        grad_qn = jnp.dot(ds_half, head_k, preferred_element_type=jnp.float32) * score_scale
        ds_groups = ds_half.reshape(N_SEQ, TOK_DEV, TOKENS).astype(jnp.float32)
        pr_groups = probs_half.reshape(N_SEQ, TOK_DEV, TOKENS).astype(jnp.float32)
        q_groups = head_q.reshape(N_SEQ, TOK_DEV, HD).astype(jnp.float32)
        o_groups = head_o.reshape(N_SEQ, TOK_DEV, HD).astype(jnp.float32)
        key_parts = jnp.einsum('nik,nic->nkc', ds_groups, q_groups) * score_scale
        value_parts = jnp.einsum('nik,nic->nkc', pr_groups, o_groups)
        key_sum = lax.optimization_barrier(jnp.sum(lax.optimization_barrier(key_parts.astype(jnp.bfloat16)).astype(jnp.float32), 0))
        value_sum = lax.optimization_barrier(jnp.sum(lax.optimization_barrier(value_parts.astype(jnp.bfloat16)).astype(jnp.float32), 0))
        return (grad_qn, key_sum, value_sum)
    grad_qn, grad_kn, grad_v = lax.map(per_head, (query_b, key_b, value_b, grad_out))
    grad_qn = jnp.transpose(grad_qn, (1, 0, 2))
    grad_kn = jnp.transpose(grad_kn, (1, 0, 2))
    grad_v = jnp.transpose(grad_v, (1, 0, 2))
    grad_q = unnorm(grad_qn, query_raw, query_inv, gains[0])
    grad_k = unnorm(grad_kn, key_raw, key_inv, gains[1])
    grad_proj = jnp.concatenate([grad_q.reshape(TOKENS, HID), grad_k.reshape(TOKENS, HID), grad_v.reshape(TOKENS, HID)], 1).astype(jnp.bfloat16)

    def add_group(running, slices):
        rows_x, rows_d, rows_c = slices
        masked = jnp.concatenate([rows_d * (rows_c == clip_no).astype(jnp.bfloat16)[:, None] for clip_no in range(CLIPS)], 1)
        partial_sum = jnp.dot(rows_x.T, masked, preferred_element_type=jnp.float32)
        return (running + lax.optimization_barrier(partial_sum.astype(jnp.bfloat16)).astype(jnp.float32), None)
    start_sum = jnp.zeros((D, CLIPS * 3 * HID), jnp.float32)
    per_clip, unused = lax.scan(add_group, start_sum, (tokens.reshape(N_SEQ, TOK_DEV, D), grad_proj.reshape(N_SEQ, TOK_DEV, 3 * HID), token_clip.reshape(N_SEQ, TOK_DEV)))
    fisher = lax.optimization_barrier(jnp.sum(jnp.square(per_clip.reshape(D, CLIPS, 3, HID)), 1))
    fisher = jnp.transpose(fisher, (1, 0, 2))
    fisher_mean = jnp.sum(fisher) / (3 * D * HID)
    fisher_ratio = fisher / (fisher_mean + 1e-06)
    dampened = (w_qkv.astype(jnp.float32) / (1.0 + damp_mask.astype(jnp.float32)[None] * fisher_ratio)).astype(jnp.bfloat16)
    return (fisher_ratio, dampened)
```

```python
import math

import jax
import jax.numpy as jnp
from jax import lax
from jax.experimental import pallas as pl
from jax.experimental.pallas import tpu as pltpu
from jax.sharding import Mesh, PartitionSpec as P

MESH = pl.DeviceIdType.MESH
D = 3072
HD = 128
HEADS = 16
CLIPS = 3
NY, NZ, NX, NC = 4, 8, 4, 2
ROWS = D // (NY * NZ)
BF = jnp.bfloat16
F32 = jnp.float32
BIG = 30000.0
ANY = pl.BlockSpec(memory_space=pl.ANY)
VMEM = pl.BlockSpec(memory_space=pltpu.VMEM)
SMEM = pl.BlockSpec(memory_space=pltpu.SMEM)
DMA = pltpu.SemaphoreType.DMA
MIB = 1 << 20


def place():
    return lax.axis_index("y"), lax.axis_index("z"), lax.axis_index("x"), lax.axis_index("c")


def rcopy(src, dst, send, recv, device):
    return pltpu.make_async_remote_copy(
        src_ref=src, dst_ref=dst, send_sem=send, recv_sem=recv, device_id=device, device_id_type=MESH
    )


def greet(devices):
    barrier = pltpu.get_barrier_semaphore()
    for device in devices:
        pl.semaphore_signal(barrier, inc=1, device_id=device, device_id_type=MESH)
    pl.semaphore_wait(barrier, len(devices))


class Ring:
    def __init__(self, view, sems):
        self.view = view
        self.send_r, self.recv_r, self.send_l, self.recv_l, self.send_s, self.recv_s = sems
        self.y, self.z, self.x, self.c = place()

    def right(self, k, at):
        v = self.view(self.c, lax.rem(at + NZ, NZ), None if k < 3 else 0)
        return rcopy(v, v, self.send_r.at[k], self.recv_r.at[k], (self.y, lax.rem(self.z + 1, NZ), self.x, self.c))

    def left(self, k, at):
        v = self.view(self.c, lax.rem(at, NZ), None if k < 3 else 1)
        return rcopy(
            v, v, self.send_l.at[k], self.recv_l.at[k], (self.y, lax.rem(self.z + NZ - 1, NZ), self.x, self.c)
        )

    def sib(self, i, core):
        if i == 0:
            at, half = self.z, None
        elif i < 5:
            at, half = self.z - i, (None if i < 4 else 0)
        else:
            at, half = self.z + i - 4, (None if i < 8 else 1)
        v = self.view(core, lax.rem(at + NZ, NZ), half)
        return rcopy(v, v, self.send_s.at[i], self.recv_s.at[i], (self.y, self.z, self.x, 1 - self.c))

    def start(self):
        self.right(0, self.z).start()
        self.left(0, self.z).start()
        self.sib(0, self.c).start()

    def step(self, k):
        self.right(k, self.z - 1 - k).wait_recv()
        if k < 3:
            self.right(k + 1, self.z - 1 - k).start()
        self.sib(1 + k, self.c).start()
        self.left(k, self.z + 1 + k).wait_recv()
        if k < 3:
            self.left(k + 1, self.z + 1 + k).start()
        self.sib(5 + k, self.c).start()

    def finish(self):
        for k in range(4):
            self.right(k, self.z - k).wait_send()
            self.left(k, self.z + k).wait_send()
        for i in range(9):
            self.sib(i, self.c).wait_send()
            self.sib(i, 1 - self.c).wait_recv()


RING_SEMS = [DMA((4,)), DMA((4,)), DMA((4,)), DMA((4,)), DMA((9,)), DMA((9,))]


def half_view(ref, lead=False):
    def view(core, z, half):
        if half is None:
            where = pl.ds(2 * core, 2)
        else:
            where = 2 * core + half
        return ref.at[:, where, z] if lead else ref.at[where, z]

    return view


def gather_inputs(
    tok, w, cot, gains, xout, wout, dout, gout, zout,
    tin, tt, sl, sw, rw, sd, rd, sg, rg, sx, rx, sxx, rxx, sz, rz, *ring_sems,
):
    y, z, x, c = place()
    h = lax.rem(x, 2)
    up, down = lax.rem(y + 1, NY), lax.rem(y + NY - 1, NY)
    xr, xl = lax.rem(x + 1, NX), lax.rem(x + NX - 1, NX)
    home = y // 2
    slot = lax.rem(y, 2)
    here, there = 128 * h, 128 * (1 - h)
    others = []
    for dy in range(NY):
        for dc in range(NC):
            if dy or dc:
                others.append((lax.rem(y + dy, NY), z, x, lax.rem(c + dc, NC)))
    for other in (xr, xl):
        others.append((y, z, other, c))
    for dz in range(1, NZ):
        others.append((y, lax.rem(z + dz, NZ), x, c))
    mine_t = lax.eq(x // 2, c)
    load_t = pltpu.make_async_copy(tok.at[:, pl.ds(pl.multiple_of(768 * x, 768), 768)], tin, sl.at[0])

    @pl.when(mine_t)
    def _():
        load_t.start()

    greet(others)

    def rows(base, piece, count):
        return pl.ds(pl.multiple_of(base + 64 * piece, 64), count)

    def hand_w(j, target, src_y, sem_at, recv_at):
        return rcopy(
            w.at[:, :, pl.ds(128 * j, 128)], wout.at[:, src_y, z], sw.at[sem_at], rw.at[recv_at], (target, z, x, home)
        )

    def hand_d(j, target, dst_slot, sem_at, recv_at):
        return rcopy(
            cot.at[:, pl.ds(128 * j, 128)], dout.at[dst_slot], sd.at[sem_at], rd.at[recv_at], (target, z, x, home)
        )

    def own_w(j):
        return pltpu.make_async_copy(w.at[:, :, pl.ds(128 * j, 128)], wout.at[:, y, z], sl.at[1])

    def own_d(j):
        return pltpu.make_async_copy(cot.at[:, pl.ds(128 * j, 128)], dout.at[slot], sl.at[2])

    own_x = pltpu.make_async_copy(tok, xout.at[slot], sl.at[3])
    for j in range(2):
        target = 2 * c + j
        is_self = lax.eq(target, y)

        @pl.when(is_self)
        def _(j=j):
            own_w(j).start()
            own_d(j).start()

        @pl.when(jnp.logical_not(is_self))
        def _(j=j, target=target):
            hand_w(j, target, y, j, slot).start()

    def x_own(direction):
        ref, dev = tok.at[rows(here, 0, 128)], (up if direction == 0 else down, z, x, c)
        return rcopy(ref, xout.at[slot, rows(here, 0, 128)], sx.at[direction], rx.at[direction], dev)

    @pl.when(lax.eq(home, c))
    def _():
        x_own(0).start()
        x_own(1).start()
        own_x.start()

    for j in range(2):
        target = 2 * c + j

        @pl.when(jnp.logical_not(lax.eq(target, y)))
        def _(j=j, target=target):
            hand_d(j, target, slot, j, slot).start()

    g_src = gains.at[:, pl.ds(pl.multiple_of(128 * slot, 128), 128)]
    own_g = pltpu.make_async_copy(g_src, gout, sl.at[4])
    give_g = rcopy(g_src, gout, sg.at[0], rg.at[0], (y, z, x, 1 - c))

    @pl.when(lax.eq(home, c))
    def _():
        own_g.start()
        give_g.start()

    def give_t(dz, dst_z):
        return rcopy(
            tt.at[dst_z], zout.at[z], sz.at[dz - 1], rz.at[dz - 1], (y, dst_z, x, c)
        )

    own_t = pltpu.make_async_copy(tt.at[z], zout.at[z], sl.at[5])

    @pl.when(mine_t)
    def _():
        load_t.wait()
        turned = tin[...].T
        for dz in range(NZ):
            tt[dz] = turned[ROWS * dz : ROWS * (dz + 1)]
        own_t.start()
        for dz in range(1, NZ):
            give_t(dz, lax.rem(z + dz, NZ)).start()

    for j in range(2):
        src_y = 2 * c + j
        is_self = lax.eq(src_y, y)

        @pl.when(is_self)
        def _(j=j):
            own_w(j).wait()

        @pl.when(jnp.logical_not(is_self))
        def _(j=j, src_y=src_y):
            hand_w(j, src_y, src_y, j, j).wait_recv()

    ring = Ring(half_view(wout, lead=True), ring_sems)
    ring.start()
    ring.step(0)
    ring.step(1)

    def piece(block, base, i):
        return xout.at[lax.rem(block, 2), rows(base, i, 64)]

    def relay(block, i):
        ref = piece(block, here, i)
        return rcopy(ref, ref, sx.at[2 + i], rx.at[2 + i], (up if i == 0 else down, z, x, c))

    def across(d, block, i):
        ref = piece(block, here, i)
        return rcopy(ref, ref, sxx.at[d - 1, i], rxx.at[d - 1, i], (y, z, xr if i == 0 else xl, c))

    def from_across(d, block, i):
        ref = piece(block, there, i)
        return rcopy(ref, ref, sxx.at[d - 1, i], rxx.at[d - 1, i], (y, z, xr if i == 0 else xl, c))

    blocks = {d: lax.rem(y + NY - d, NY) for d in (1, 2, 3)}
    near = {1: 0, 3: 1}
    for d in (1, 3):
        block = blocks[d]

        @pl.when(lax.eq(block // 2, c))
        def _(d=d, block=block):
            ref = xout.at[lax.rem(block, 2), rows(here, 0, 128)]
            rcopy(
                ref, ref, sx.at[near[d]], rx.at[near[d]], (up if d == 1 else down, z, x, c)
            ).wait_recv()
            relay(block, near[d]).start()
            across(d, block, 0).start()
            across(d, block, 1).start()

    ring.step(2)
    block = blocks[2]

    @pl.when(lax.eq(block // 2, c))
    def _():
        for i in range(2):
            relay(block, i).wait_recv()
            across(2, block, i).start()

    ring.step(3)
    for d in (1, 3, 2):
        block = blocks[d]

        @pl.when(lax.eq(block // 2, c))
        def _(d=d, block=block):
            for i in range(2):
                from_across(d, block, i).wait_recv()
                across(d, block, i).wait_send()
            if d != 2:
                relay(block, near[d]).wait_send()

    @pl.when(lax.eq(home, c))
    def _():
        x_own(0).wait_send()
        x_own(1).wait_send()
        own_x.wait()
        own_g.wait()
        give_g.wait_send()

    @pl.when(jnp.logical_not(lax.eq(home, c)))
    def _():
        give_g.wait_recv()

    @pl.when(mine_t)
    def _():
        own_t.wait()
        for dz in range(1, NZ):
            src_z = lax.rem(z + NZ - dz, NZ)
            rcopy(
                tt.at[z], zout.at[src_z], sz.at[dz - 1], rz.at[dz - 1], (y, src_z, x, c)
            ).wait_recv()
            give_t(dz, lax.rem(z + dz, NZ)).wait_send()

    for j in range(2):
        src_y = 2 * c + j
        is_self = lax.eq(src_y, y)

        @pl.when(is_self)
        def _(j=j):
            own_d(j).wait()

        @pl.when(jnp.logical_not(is_self))
        def _(j=j, src_y=src_y):
            hand_w(j, src_y, src_y, j, j).wait_send()
            hand_d(j, src_y, j, j, j).wait_send()
            hand_d(j, src_y, j, j, j).wait_recv()

    ring.finish()


def project(x_ref, w_ref, g_ref, q_ref, kv_ref, norm_ref, inv_ref):
    rows = x_ref[0]
    for j in range(3):
        raw = jnp.dot(rows, w_ref[j], preferred_element_type=F32)
        if j == 2:
            kv_ref[0, :, 128:] = raw.astype(BF)
        else:
            inv = lax.rsqrt(jnp.mean(raw * raw, -1, keepdims=True) + 1e-06)
            hat = raw * inv
            norm_ref[0, j] = hat
            inv_ref[0, j] = jnp.broadcast_to(inv, hat.shape)
            out = (hat * g_ref[j : j + 1]).astype(BF)
            if j == 0:
                q_ref[0] = out
            else:
                kv_ref[0, :, :128] = out


def gather_kv(kv, zin, kv_all, xx, sl, sx, rx, *ring_sems):
    y, z, x, c = place()
    others = [(y, z, x, 1 - c), (y, lax.rem(z + 1, NZ), x, c), (y, lax.rem(z + NZ - 1, NZ), x, c)]
    for dx in range(1, NX):
        others.append((y, z, lax.rem(x + dx, NX), c))
    own = pltpu.make_async_copy(kv, kv_all.at[pl.ds(2 * c, 2), z], sl.at[0])
    own.start()
    greet(others)
    mine_t = lax.eq(x // 2, c)
    own_t = pltpu.make_async_copy(zin, xx.at[lax.rem(x, 2)], sl.at[1])

    def give(dx):
        return rcopy(
            zin, xx.at[lax.rem(x, 2)], sx.at[dx - 1], rx.at[dx - 1], (y, z, lax.rem(x + dx, NX), c)
        )

    own.wait()
    ring = Ring(half_view(kv_all), ring_sems)
    ring.start()

    @pl.when(mine_t)
    def _():
        own_t.start()
        for dx in (1, 3, 2):
            give(dx).start()

    for k in range(4):
        ring.step(k)

    @pl.when(mine_t)
    def _():
        own_t.wait()
        for dx in range(1, NX):
            give(dx).wait_send()

    for dx in range(1, NX):
        src = lax.rem(x + NX - dx, NX)

        @pl.when(lax.eq(src // 2, c))
        def _(dx=dx, src=src):
            rcopy(zin, xx.at[lax.rem(src, 2)], sx.at[dx - 1], rx.at[dx - 1], (y, z, src, c)).wait_recv()

    ring.finish()


KB = 256


def attend(q_ref, own_ref, do_ref, qc_ref, kv_ref, kc_ref, live_ref, dq_ref, dkv_ref, diag_ref, e_ref, dp_ref):
    tokens, queries = kv_ref.shape[0], q_ref.shape[0]
    scale = 1.0 / math.sqrt(HD)
    to_exp2 = scale * math.log2(math.e)
    q = q_ref[...]
    do = do_ref[...]
    q_cat = jnp.concatenate([q, qc_ref[...]], 1)
    nt = (((1,), (1,)), ((), ()))

    def fold(v):
        return jnp.sum(v.reshape(KB // 8, 8, queries), 0)

    def first(i, sums):
        total, dot = sums
        at = pl.ds(pl.multiple_of(i * KB, KB), KB)
        k_cat = jnp.concatenate([kv_ref[at, :HD], kc_ref[at, :]], 1)
        e = jnp.exp2(lax.dot_general(k_cat, q_cat, nt, preferred_element_type=F32) * to_exp2)
        dp = lax.dot_general(kv_ref[at, HD:], do, nt, preferred_element_type=F32)
        e_ref[at, :] = e
        dp_ref[at, :] = dp
        return total + fold(e), dot + fold(e * dp)

    zero = jnp.zeros((8, queries), F32)
    total, dot = lax.fori_loop(0, tokens // KB, first, (zero, zero))
    total = jnp.sum(total, 0, keepdims=True)
    dot = jnp.sum(dot, 0, keepdims=True)
    own_k = own_ref[:, :HD].astype(F32)
    own_v = own_ref[:, HD:].astype(F32)
    qf, dof = q.astype(F32), do.astype(F32)
    dead = 1.0 - live_ref[...]
    own_e = dead * jnp.exp2(jnp.sum((qf * own_k).T, 0, keepdims=True) * to_exp2)
    own_dp = jnp.sum((dof * own_v).T, 0, keepdims=True)
    total = total + own_e
    dot = dot + own_e * own_dp
    inv = 1.0 / total
    row_dot = dot * inv
    own_p = own_e * inv
    own_ds = own_p * (own_dp - row_dot)
    column = lambda v: jnp.broadcast_to(v, (HD, queries)).T.astype(BF).astype(F32)
    p_col, ds_col = column(own_p), column(own_ds)
    diag_ref[:, :HD] = ds_col * qf * scale
    diag_ref[:, HD:] = p_col * dof

    def second(i, acc):
        at = pl.ds(pl.multiple_of(i * KB, KB), KB)
        p = e_ref[at, :] * inv
        ds = (p * (dp_ref[at, :] - row_dot)).astype(BF)
        dkv_ref[at, HD:] = jnp.dot(p.astype(BF), do, preferred_element_type=F32).astype(BF)
        dkv_ref[at, :HD] = (jnp.dot(ds, q, preferred_element_type=F32) * scale).astype(BF)
        return acc + lax.dot_general(
            kv_ref[at, :HD], ds, (((0,), (0,)), ((), ())), preferred_element_type=F32
        )

    acc = lax.fori_loop(0, tokens // KB, second, jnp.zeros((HD, queries), F32))
    dq_ref[...] = (acc.T + ds_col * own_k) * scale


def scatter_kv(part, xx, summed, xn, mine, sib, snd_r, snd_l, got_r, got_l, sl, ss, rs, sr, rr, sq, rq, sx, rx):
    y, z, x, c = place()
    right, left = (y, lax.rem(z + 1, NZ), x, c), (y, lax.rem(z + NZ - 1, NZ), x, c)
    up, down = (lax.rem(y + 1, NY), z, x, c), (lax.rem(y + NY - 1, NY), z, x, c)
    load = pltpu.make_async_copy(part.at[pl.ds(2 * c, 2)], mine, sl.at[0])
    load.start()
    greet([(y, z, x, 1 - c), right, left, up, down])

    def at(offset):
        return lax.rem(z + offset + NZ, NZ)

    def swap(i, offset):
        return rcopy(
            part.at[pl.ds(2 * (1 - c), 2), at(offset)], sib.at[:, at(offset)], ss.at[i], rs.at[i], (y, z, x, 1 - c)
        )

    order = (4, 3, -3, 2, -2, 1, -1, 0)
    for i, offset in enumerate(order):
        swap(i, offset).start()

    give_up = rcopy(xx, xn.at[0], sx.at[0], rx.at[0], up)
    give_down = rcopy(xx, xn.at[1], sx.at[1], rx.at[1], down)
    give_up.start()
    give_down.start()
    load.wait()

    def chip(offset, half):
        return mine[half, at(offset)].astype(F32) + sib[half, at(offset)].astype(F32)

    def send_r(t):
        if t == 0:
            return rcopy(snd_r.at[0, 0], got_r.at[0, 0], sr.at[0], rr.at[0], right)
        return rcopy(snd_r.at[t], got_r.at[t], sr.at[t], rr.at[t], right)

    def send_l(t):
        if t == 0:
            return rcopy(snd_l.at[0, 1], got_l.at[0, 1], sq.at[0], rq.at[0], left)
        return rcopy(snd_l.at[t], got_l.at[t], sq.at[t], rq.at[t], left)

    swap(0, 4).wait_recv()
    snd_r[0, 0] = chip(4, 0).astype(BF)
    send_r(0).start()
    snd_l[0, 1] = chip(4, 1).astype(BF)
    send_l(0).start()
    for t in range(1, 4):
        swap(2 * t - 1, 4 - t).wait_recv()
        send_r(t - 1).wait_recv()
        snd_r[t, 0] = (chip(4 - t, 0) + got_r[t - 1, 0].astype(F32)).astype(BF)
        own = chip(4 - t, 1)
        snd_r[t, 1] = (own if t == 1 else own + got_r[t - 1, 1].astype(F32)).astype(BF)
        send_r(t).start()
        swap(2 * t, t - 4).wait_recv()
        send_l(t - 1).wait_recv()
        snd_l[t, 1] = (chip(t - 4, 1) + got_l[t - 1, 1].astype(F32)).astype(BF)
        own = chip(t - 4, 0)
        snd_l[t, 0] = (own if t == 1 else own + got_l[t - 1, 0].astype(F32)).astype(BF)
        send_l(t).start()
    swap(7, 0).wait_recv()
    send_r(3).wait_recv()
    send_l(3).wait_recv()
    for half in range(2):
        summed[half] = chip(0, half) + got_r[3, half].astype(F32) + got_l[3, half].astype(F32)
    for t in range(4):
        send_r(t).wait_send()
        send_l(t).wait_send()
    for i, offset in enumerate(order):
        swap(i, offset).wait_send()
    give_up.wait()
    give_down.wait()


def norm_back(dq_ref, dkv_ref, diag_ref, norm_ref, inv_ref, g_ref, out_ref):
    dkv = dkv_ref[0] + diag_ref[...]
    for j in range(2):
        up = (dq_ref[...] if j == 0 else dkv[:, :HD]) * g_ref[j : j + 1]
        hat = norm_ref[0, j]
        back = inv_ref[0, j] * (up - hat * jnp.mean(hat * up, -1, keepdims=True))
        out_ref[0, :, HD * j : HD * (j + 1)] = back.astype(BF)
    out_ref[0, :, 2 * HD :] = dkv[:, HD:].astype(BF)


def gather_grads(dproj, xn, all_d, xo, sl, sx, rx, *ring_sems):
    y, z, x, c = place()
    up, down = (lax.rem(y + 1, NY), z, x, c), (lax.rem(y + NY - 1, NY), z, x, c)
    own = pltpu.make_async_copy(dproj, all_d.at[pl.ds(2 * c, 2), z], sl.at[0])
    own.start()
    greet([(y, z, x, 1 - c), (y, lax.rem(z + 1, NZ), x, c), (y, lax.rem(z + NZ - 1, NZ), x, c), up, down])
    own.wait()
    ring = Ring(half_view(all_d), ring_sems)
    ring.start()
    give_up = rcopy(xn.at[0, 0], xo.at[0], sx.at[0], rx.at[0], up)
    give_down = rcopy(xn.at[1, 1], xo.at[1], sx.at[1], rx.at[1], down)
    give_up.start()
    give_down.start()
    for k in range(4):
        ring.step(k)
    ring.finish()
    give_up.wait()
    give_down.wait()


def weight_grads(clip_ref, xx, xn, xo, d_ref, mask_ref, f_ref, sum_ref, acc):
    y = lax.axis_index("y")
    acc[...] = jnp.zeros_like(acc)
    for rel, block in ((0, xx), (NY - 1, xn.at[0]), (1, xn.at[1]), (2, xo)):
        yb = lax.rem(y + rel, NY)
        for z in range(NZ):
            s = yb * NZ + z
            low, high = clip_ref[256 * s], clip_ref[256 * s + 255]
            lhs = jnp.concatenate([block[0, z], block[1, z]], 0)
            for clip in range(CLIPS):

                @pl.when(jnp.logical_and(low <= clip, clip <= high))
                def _(lhs=lhs, yb=yb, z=z, s=s, clip=clip):
                    keep = (mask_ref[s] == clip).astype(BF)
                    rhs = d_ref[yb, z] * jnp.concatenate([keep] * 3, 1)
                    acc[clip] += jnp.dot(lhs, rhs, preferred_element_type=F32)

    fisher = acc[0] * acc[0] + acc[1] * acc[1] + acc[2] * acc[2]
    for j in range(2):
        f_ref[j] = fisher[ROWS * j : ROWS * (j + 1)]
    rows = jnp.sum(fisher.reshape(2 * ROWS // 8, 8, 3 * HD), 0)
    sum_ref[...] = rows[:, :HD] + rows[:, HD : 2 * HD] + rows[:, 2 * HD :]


def exchange(f, part, own, total, tile, box, box2, sl, sf, rf, s1, r1, s2, r2):
    y, z, x, c = place()
    first = []
    for dz in range(NZ):
        for dc in range(NC):
            if dz or dc:
                first.append((y, lax.rem(z + dz, NZ), x, lax.rem(c + dc, NC)))
    second = []
    for dy in range(NY):
        for dx in range(NX):
            if dy or dx:
                second.append((lax.rem(y + dy, NY), z, lax.rem(x + dx, NX), c))
    third = []
    for dy in range(1, NY):
        third.append((lax.rem(y + dy, NY), z, x, 1 - c))
    greet(first + second + third)
    for i, device in enumerate(first):
        rcopy(part, box.at[i], s1.at[i], r1.at[i], device).start()
    home, slot = y // 2, lax.rem(y, 2)

    def give(j, target, dst_slot, recv_at):
        return rcopy(f.at[j], own.at[dst_slot], sf.at[j], rf.at[recv_at], (target, z, x, home))

    def keep(j):
        return pltpu.make_async_copy(f.at[j], own.at[slot], sl.at[0])

    for j in range(2):
        target = 2 * c + j

        @pl.when(lax.eq(target, y))
        def _(j=j):
            keep(j).start()

        @pl.when(jnp.logical_not(lax.eq(target, y)))
        def _(j=j, target=target):
            give(j, target, slot, slot).start()

    for i, device in enumerate(first):
        rcopy(part, box.at[i], s1.at[i], r1.at[i], device).wait_recv()
    tile[...] = part[...] + jnp.sum(box[...], 0)
    for i, device in enumerate(second):
        rcopy(tile, box2.at[i], s2.at[i], r2.at[i], device).start()
    for i, device in enumerate(second):
        rcopy(tile, box2.at[i], s2.at[i], r2.at[i], device).wait_recv()
    total[...] = tile[...] + jnp.sum(box2[...], 0)
    for j in range(2):
        target = 2 * c + j

        @pl.when(lax.eq(target, y))
        def _(j=j):
            keep(j).wait()

        @pl.when(jnp.logical_not(lax.eq(target, y)))
        def _(j=j, target=target):
            give(j, target, j, j).wait_recv()
            give(j, target, j, j).wait_send()

    for i, device in enumerate(first):
        rcopy(part, box.at[i], s1.at[i], r1.at[i], device).wait_send()
    for i, device in enumerate(second):
        rcopy(tile, box2.at[i], s2.at[i], r2.at[i], device).wait_send()


def shape(dims, dtype=BF):
    return jax.ShapeDtypeStruct(dims, dtype)


def comm(collective, limit=None):
    return pltpu.CompilerParams(collective_id=collective, has_side_effects=True, vmem_limit_bytes=limit)


def on_device(tokens, w_qkv, gains, cotangent, token_clip, key_live, damp_mask):
    y, z, x, c = place()
    n_tok = token_clip.shape[0]
    t_dev = n_tok // (NY * NZ)
    xout, wout, dout, gout, zout = pl.pallas_call(
        gather_inputs,
        out_shape=(
            shape((2, t_dev, D)),
            shape((3, NY, NZ, ROWS, HD)),
            shape((2, t_dev, HD)),
            shape((2, HD), F32),
            shape((NZ, ROWS, t_dev)),
        ),
        in_specs=[ANY] * 4,
        out_specs=(ANY,) * 5,
        scratch_shapes=[
            pltpu.VMEM((t_dev, NZ * ROWS), BF),
            pltpu.VMEM((NZ, ROWS, t_dev), BF),
            DMA((6,)),
            DMA((2,)), DMA((2,)), DMA((2,)), DMA((2,)), DMA((1,)), DMA((1,)),
            DMA((4,)), DMA((4,)), DMA((3, 2)), DMA((3, 2)), DMA((7,)), DMA((7,)),
            *RING_SEMS,
        ],
        compiler_params=comm(0),
        name="gather_inputs",
    )(tokens, w_qkv, cotangent, gains)

    q, kv, hat, inv = pl.pallas_call(
        project,
        grid=(2,),
        out_shape=(
            shape((2, t_dev, HD)),
            shape((2, t_dev, 2 * HD)),
            shape((2, 2, t_dev, HD), F32),
            shape((2, 2, t_dev, HD), F32),
        ),
        in_specs=[
            pl.BlockSpec((1, t_dev, D), lambda i: (i, 0, 0)),
            pl.BlockSpec((3, D, HD), lambda i: (0, 0, 0)),
            pl.BlockSpec((2, HD), lambda i: (0, 0)),
        ],
        out_specs=(
            pl.BlockSpec((1, t_dev, HD), lambda i: (i, 0, 0)),
            pl.BlockSpec((1, t_dev, 2 * HD), lambda i: (i, 0, 0)),
            pl.BlockSpec((1, 2, t_dev, HD), lambda i: (i, 0, 0, 0)),
            pl.BlockSpec((1, 2, t_dev, HD), lambda i: (i, 0, 0, 0)),
        ),
        compiler_params=pltpu.CompilerParams(vmem_limit_bytes=32 * MIB),
        name="project",
    )(xout, wout.reshape(3, D, HD), gout)

    kv_all, xx = pl.pallas_call(
        gather_kv,
        out_shape=(shape((NY, NZ, t_dev, 2 * HD)), shape((2, NZ, ROWS, t_dev))),
        in_specs=[ANY] * 2,
        out_specs=(ANY,) * 2,
        scratch_shapes=[DMA((2,)), DMA((3,)), DMA((3,)), *RING_SEMS],
        compiler_params=comm(1),
        name="gather_kv",
    )(kv, zout)

    lanes = jnp.arange(HD, dtype=jnp.int32)[None, :]
    key_code = jnp.where(
        (lanes == token_clip[:, None]) & (key_live[:, None] == 1), 0.0, jnp.where(lanes < CLIPS, -BIG, 0.0)
    ).astype(BF)
    grid_clip = lax.dynamic_slice(token_clip.reshape(NY, NZ, t_dev), (2 * c, z, 0), (2, 1, t_dev)).reshape(2 * t_dev)
    grid_live = lax.dynamic_slice(key_live.reshape(NY, NZ, t_dev), (2 * c, z, 0), (2, 1, t_dev)).reshape(1, 2 * t_dev)
    query_code = (lanes == grid_clip[:, None]).astype(BF)
    dq, dkv, diag = pl.pallas_call(
        attend,
        out_shape=(shape((2 * t_dev, HD), F32), shape((n_tok, 2 * HD)), shape((2 * t_dev, 2 * HD), F32)),
        in_specs=[VMEM] * 7,
        out_specs=(VMEM,) * 3,
        scratch_shapes=[pltpu.VMEM((n_tok, 2 * t_dev), F32), pltpu.VMEM((n_tok, 2 * t_dev), F32)],
        compiler_params=pltpu.CompilerParams(vmem_limit_bytes=60 * MIB),
        name="attend",
    )(
        q.reshape(2 * t_dev, HD),
        kv.reshape(2 * t_dev, 2 * HD),
        dout.reshape(2 * t_dev, HD),
        query_code,
        kv_all.reshape(n_tok, 2 * HD),
        key_code,
        grid_live.astype(F32),
    )

    pair = (2, t_dev, 2 * HD)
    summed, xn = pl.pallas_call(
        scatter_kv,
        out_shape=(shape(pair, F32), shape((2, 2, NZ, ROWS, t_dev))),
        in_specs=[ANY] * 2,
        out_specs=(VMEM, ANY),
        scratch_shapes=[
            pltpu.VMEM((2, NZ, t_dev, 2 * HD), BF),
            pltpu.VMEM((2, NZ, t_dev, 2 * HD), BF),
            pltpu.VMEM((4, *pair), BF), pltpu.VMEM((4, *pair), BF),
            pltpu.VMEM((4, *pair), BF), pltpu.VMEM((4, *pair), BF),
            DMA((1,)), DMA((8,)), DMA((8,)),
            DMA((4,)), DMA((4,)), DMA((4,)), DMA((4,)), DMA((2,)), DMA((2,)),
        ],
        compiler_params=comm(2, 40 * MIB),
        name="scatter_kv",
    )(dkv.reshape(NY, NZ, t_dev, 2 * HD), xx)

    dproj = pl.pallas_call(
        norm_back,
        grid=(2,),
        out_shape=shape((2, t_dev, 3 * HD)),
        in_specs=[
            pl.BlockSpec((t_dev, HD), lambda i: (i, 0)),
            pl.BlockSpec((1, t_dev, 2 * HD), lambda i: (i, 0, 0)),
            pl.BlockSpec((t_dev, 2 * HD), lambda i: (i, 0)),
            pl.BlockSpec((1, 2, t_dev, HD), lambda i: (i, 0, 0, 0)),
            pl.BlockSpec((1, 2, t_dev, HD), lambda i: (i, 0, 0, 0)),
            pl.BlockSpec((2, HD), lambda i: (0, 0)),
        ],
        out_specs=pl.BlockSpec((1, t_dev, 3 * HD), lambda i: (i, 0, 0)),
        name="norm_back",
    )(dq, summed, diag, hat, inv, gout)

    all_d, xo = pl.pallas_call(
        gather_grads,
        out_shape=(shape((NY, NZ, t_dev, 3 * HD)), shape((2, NZ, ROWS, t_dev))),
        in_specs=[ANY] * 2,
        out_specs=(ANY,) * 2,
        scratch_shapes=[DMA((1,)), DMA((2,)), DMA((2,)), *RING_SEMS],
        compiler_params=comm(3),
        name="gather_grads",
    )(dproj, xn)

    clip_cols = jnp.broadcast_to(token_clip.reshape(NY * NZ, t_dev, 1), (NY * NZ, t_dev, HD))
    fisher, part = pl.pallas_call(
        weight_grads,
        out_shape=(shape((2, ROWS, 3 * HD), F32), shape((8, HD), F32)),
        in_specs=[SMEM] + [VMEM] * 5,
        out_specs=(VMEM, VMEM),
        scratch_shapes=[pltpu.VMEM((CLIPS, 2 * ROWS, 3 * HD), F32)],
        compiler_params=pltpu.CompilerParams(vmem_limit_bytes=48 * MIB),
        name="weight_grads",
    )(token_clip, xx, xn, xo, all_d, clip_cols)

    own, total = pl.pallas_call(
        exchange,
        out_shape=(shape((2, ROWS, 3 * HD), F32), shape((8, HD), F32)),
        in_specs=[ANY, VMEM],
        out_specs=(ANY, VMEM),
        scratch_shapes=[
            pltpu.VMEM((8, HD), F32),
            pltpu.VMEM((15, 8, HD), F32),
            pltpu.VMEM((15, 8, HD), F32),
            DMA((1,)), DMA((2,)), DMA((2,)), DMA((15,)), DMA((15,)), DMA((15,)), DMA((15,)),
        ],
        compiler_params=comm(4),
        name="exchange",
    )(fisher, part)

    fisher_mean = jnp.sum(total) / (3 * D * HEADS * HD)
    ratio = own.reshape(2, ROWS, 3, HD).transpose(2, 1, 0, 3).reshape(3, ROWS, 2 * HD) / (fisher_mean + 1e-06)
    dampened = (w_qkv.astype(F32) / (1.0 + damp_mask.astype(F32)[None] * ratio)).astype(BF)
    return ratio, dampened


def solution(mesh):
    grid = Mesh(mesh.devices.reshape(NY, NZ, NX, NC), ("y", "z", "x", "c"))
    seq, head = ("y", "z"), ("x", "c")
    return jax.shard_map(
        on_device,
        mesh=grid,
        in_specs=(
            P(seq, None),
            P(None, seq, head),
            P(None, head),
            P(seq, head),
            P(),
            P(),
            P(seq, head),
        ),
        out_specs=(P(None, seq, head), P(None, seq, head)),
        check_vma=False,
    )
```

```python
import math

import jax
import jax.numpy as jnp
from jax import lax
from jax.experimental import pallas as pl
from jax.experimental.pallas import tpu as pltpu
from jax.sharding import Mesh, PartitionSpec as P

MESH = pl.DeviceIdType.MESH
D = 3072
HD = 128
HEADS = 16
CLIPS = 3
NY, NZ, NX, NC = 4, 8, 4, 2
ROWS = D // (NY * NZ)
BF = jnp.bfloat16
F32 = jnp.float32
BIG = 30000.0
ANY = pl.BlockSpec(memory_space=pl.ANY)
VMEM = pl.BlockSpec(memory_space=pltpu.VMEM)
SMEM = pl.BlockSpec(memory_space=pltpu.SMEM)
DMA = pltpu.SemaphoreType.DMA
MIB = 1 << 20


def place():
    return lax.axis_index("y"), lax.axis_index("z"), lax.axis_index("x"), lax.axis_index("c")


def rcopy(src, dst, send, recv, device):
    return pltpu.make_async_remote_copy(
        src_ref=src, dst_ref=dst, send_sem=send, recv_sem=recv, device_id=device, device_id_type=MESH
    )


def greet(devices):
    barrier = pltpu.get_barrier_semaphore()
    for device in devices:
        pl.semaphore_signal(barrier, inc=1, device_id=device, device_id_type=MESH)
    pl.semaphore_wait(barrier, len(devices))


class Ring:
    def __init__(self, view, sems):
        self.view = view
        self.send_r, self.recv_r, self.send_l, self.recv_l, self.send_s, self.recv_s = sems
        self.y, self.z, self.x, self.c = place()

    def right(self, k, at):
        v = self.view(self.c, lax.rem(at + NZ, NZ), None if k < 3 else 0)
        return rcopy(v, v, self.send_r.at[k], self.recv_r.at[k], (self.y, lax.rem(self.z + 1, NZ), self.x, self.c))

    def left(self, k, at):
        v = self.view(self.c, lax.rem(at, NZ), None if k < 3 else 1)
        return rcopy(
            v, v, self.send_l.at[k], self.recv_l.at[k], (self.y, lax.rem(self.z + NZ - 1, NZ), self.x, self.c)
        )

    def sib(self, i, core):
        if i == 0:
            at, half = self.z, None
        elif i < 5:
            at, half = self.z - i, (None if i < 4 else 0)
        else:
            at, half = self.z + i - 4, (None if i < 8 else 1)
        v = self.view(core, lax.rem(at + NZ, NZ), half)
        return rcopy(v, v, self.send_s.at[i], self.recv_s.at[i], (self.y, self.z, self.x, 1 - self.c))

    def start(self):
        self.right(0, self.z).start()
        self.left(0, self.z).start()
        self.sib(0, self.c).start()

    def step(self, k):
        self.right(k, self.z - 1 - k).wait_recv()
        if k < 3:
            self.right(k + 1, self.z - 1 - k).start()
        self.sib(1 + k, self.c).start()
        self.left(k, self.z + 1 + k).wait_recv()
        if k < 3:
            self.left(k + 1, self.z + 1 + k).start()
        self.sib(5 + k, self.c).start()

    def finish(self):
        for k in range(4):
            self.right(k, self.z - k).wait_send()
            self.left(k, self.z + k).wait_send()
        for i in range(9):
            self.sib(i, self.c).wait_send()
            self.sib(i, 1 - self.c).wait_recv()


RING_SEMS = [DMA((4,)), DMA((4,)), DMA((4,)), DMA((4,)), DMA((9,)), DMA((9,))]


def half_view(ref, lead=False):
    def view(core, z, half):
        if half is None:
            where = pl.ds(2 * core, 2)
        else:
            where = 2 * core + half
        return ref.at[:, where, z] if lead else ref.at[where, z]

    return view


class Chunks:
    def __init__(self, buf, sems):
        self.buf = buf
        self.send_r, self.recv_r, self.send_l, self.recv_l, self.send_s, self.recv_s = sems
        self.y, self.z, self.x, self.c = place()

    def at(self, core, z, b):
        return self.buf.at[2 * core + b, lax.rem(z + NZ, NZ)]

    def right(self, k, b, z):
        v = self.at(self.c, z, b)
        return rcopy(
            v, v, self.send_r.at[k, b], self.recv_r.at[k, b], (self.y, lax.rem(self.z + 1, NZ), self.x, self.c)
        )

    def left(self, k, b, z):
        v = self.at(self.c, z, b)
        return rcopy(
            v, v, self.send_l.at[k, b], self.recv_l.at[k, b], (self.y, lax.rem(self.z + NZ - 1, NZ), self.x, self.c)
        )

    def sib(self, i, b, core, z):
        v = self.at(core, z, b)
        return rcopy(v, v, self.send_s.at[i, b], self.recv_s.at[i, b], (self.y, self.z, self.x, 1 - self.c))

    def start(self, b):
        self.right(0, b, self.z).start()
        self.left(0, b, self.z).start()
        self.sib(0, b, self.c, self.z).start()

    def start_wait(self):
        for b in range(2):
            self.sib(0, b, 1 - self.c, self.z).wait_recv()

    def step(self, k):
        zr, zl = self.z - 1 - k, self.z + 1 + k
        for b in range(2):
            self.right(k, b, zr).wait_recv()
            if b == 0:
                self.right(k + 1, b, zr).start()
            else:
                pl.when(k < 2)(lambda: self.right(k + 1, 1, zr).start())
            self.sib(1 + k, b, self.c, zr).start()
            self.left(k, b, zl).wait_recv()
            if b == 1:
                self.left(k + 1, b, zl).start()
            else:
                pl.when(k < 2)(lambda: self.left(k + 1, 0, zl).start())
            self.sib(5 + k, b, self.c, zl).start()
        for b in range(2):
            self.sib(1 + k, b, 1 - self.c, zr).wait_recv()
            self.sib(5 + k, b, 1 - self.c, zl).wait_recv()

    def last(self):
        far = self.z + 4
        self.right(3, 0, far).wait_recv()
        self.sib(4, 0, self.c, far).start()
        self.left(3, 1, far).wait_recv()
        self.sib(8, 1, self.c, far).start()
        self.sib(4, 0, 1 - self.c, far).wait_recv()
        self.sib(8, 1, 1 - self.c, far).wait_recv()

    def finish(self):
        for k in range(4):
            for b in range(2):
                if k < 3 or b == 0:
                    self.right(k, b, self.z - k).wait_send()
                    self.sib(1 + k, b, self.c, self.z).wait_send()
                if k < 3 or b == 1:
                    self.left(k, b, self.z + k).wait_send()
                    self.sib(5 + k, b, self.c, self.z).wait_send()
        for b in range(2):
            self.sib(0, b, self.c, self.z).wait_send()


CHUNK_SEMS = [DMA((4, 2)), DMA((4, 2)), DMA((4, 2)), DMA((4, 2)), DMA((9, 2)), DMA((9, 2))]


def gather_inputs(
    tok, w, cot, gains, xout, wout, dout, gout, zout,
    tin, tt, sl, sw, rw, sd, rd, sg, rg, sx, rx, sxx, rxx, sz, rz, *ring_sems,
):
    y, z, x, c = place()
    h = lax.rem(x, 2)
    up, down = lax.rem(y + 1, NY), lax.rem(y + NY - 1, NY)
    xr, xl = lax.rem(x + 1, NX), lax.rem(x + NX - 1, NX)
    home = y // 2
    slot = lax.rem(y, 2)
    here, there = 128 * h, 128 * (1 - h)
    others = []
    for dy in range(NY):
        for dc in range(NC):
            if dy or dc:
                others.append((lax.rem(y + dy, NY), z, x, lax.rem(c + dc, NC)))
    for other in (xr, xl):
        others.append((y, z, other, c))
    for dz in range(1, NZ):
        others.append((y, lax.rem(z + dz, NZ), x, c))
    mine_t = lax.eq(x // 2, c)
    load_t = pltpu.make_async_copy(tok.at[:, pl.ds(pl.multiple_of(768 * x, 768), 768)], tin, sl.at[0])

    @pl.when(mine_t)
    def _():
        load_t.start()

    greet(others)

    def rows(base, piece, count):
        return pl.ds(pl.multiple_of(base + 64 * piece, 64), count)

    def hand_w(j, target, src_y, sem_at, recv_at):
        return rcopy(
            w.at[:, :, pl.ds(128 * j, 128)], wout.at[:, src_y, z], sw.at[sem_at], rw.at[recv_at], (target, z, x, home)
        )

    def hand_d(j, target, dst_slot, sem_at, recv_at):
        return rcopy(
            cot.at[:, pl.ds(128 * j, 128)], dout.at[dst_slot], sd.at[sem_at], rd.at[recv_at], (target, z, x, home)
        )

    def own_w(j):
        return pltpu.make_async_copy(w.at[:, :, pl.ds(128 * j, 128)], wout.at[:, y, z], sl.at[1])

    def own_d(j):
        return pltpu.make_async_copy(cot.at[:, pl.ds(128 * j, 128)], dout.at[slot], sl.at[2])

    own_x = pltpu.make_async_copy(tok, xout.at[slot], sl.at[3])
    for j in range(2):
        target = 2 * c + j
        is_self = lax.eq(target, y)

        @pl.when(is_self)
        def _(j=j):
            own_w(j).start()
            own_d(j).start()

        @pl.when(jnp.logical_not(is_self))
        def _(j=j, target=target):
            hand_w(j, target, y, j, slot).start()

    def x_own(direction):
        ref, dev = tok.at[rows(here, 0, 128)], (up if direction == 0 else down, z, x, c)
        return rcopy(ref, xout.at[slot, rows(here, 0, 128)], sx.at[direction], rx.at[direction], dev)

    @pl.when(lax.eq(home, c))
    def _():
        x_own(0).start()
        x_own(1).start()
        own_x.start()

    for j in range(2):
        target = 2 * c + j

        @pl.when(jnp.logical_not(lax.eq(target, y)))
        def _(j=j, target=target):
            hand_d(j, target, slot, j, slot).start()

    g_src = gains.at[:, pl.ds(pl.multiple_of(128 * slot, 128), 128)]
    own_g = pltpu.make_async_copy(g_src, gout, sl.at[4])
    give_g = rcopy(g_src, gout, sg.at[0], rg.at[0], (y, z, x, 1 - c))

    @pl.when(lax.eq(home, c))
    def _():
        own_g.start()
        give_g.start()

    def give_t(dz, dst_z):
        return rcopy(
            tt.at[dst_z], zout.at[z], sz.at[dz - 1], rz.at[dz - 1], (y, dst_z, x, c)
        )

    own_t = pltpu.make_async_copy(tt.at[z], zout.at[z], sl.at[5])

    @pl.when(mine_t)
    def _():
        load_t.wait()
        turned = tin[...].T
        for dz in range(NZ):
            tt[dz] = turned[ROWS * dz : ROWS * (dz + 1)]
        own_t.start()
        for dz in range(1, NZ):
            give_t(dz, lax.rem(z + dz, NZ)).start()

    for j in range(2):
        src_y = 2 * c + j
        is_self = lax.eq(src_y, y)

        @pl.when(is_self)
        def _(j=j):
            own_w(j).wait()

        @pl.when(jnp.logical_not(is_self))
        def _(j=j, src_y=src_y):
            hand_w(j, src_y, src_y, j, j).wait_recv()

    ring = Ring(half_view(wout, lead=True), ring_sems)
    ring.start()
    ring.step(0)
    ring.step(1)

    def piece(block, base, i):
        return xout.at[lax.rem(block, 2), rows(base, i, 64)]

    def relay(block, i):
        ref = piece(block, here, i)
        return rcopy(ref, ref, sx.at[2 + i], rx.at[2 + i], (up if i == 0 else down, z, x, c))

    def across(d, block, i):
        ref = piece(block, here, i)
        return rcopy(ref, ref, sxx.at[d - 1, i], rxx.at[d - 1, i], (y, z, xr if i == 0 else xl, c))

    def from_across(d, block, i):
        ref = piece(block, there, i)
        return rcopy(ref, ref, sxx.at[d - 1, i], rxx.at[d - 1, i], (y, z, xr if i == 0 else xl, c))

    blocks = {d: lax.rem(y + NY - d, NY) for d in (1, 2, 3)}
    near = {1: 0, 3: 1}
    for d in (1, 3):
        block = blocks[d]

        @pl.when(lax.eq(block // 2, c))
        def _(d=d, block=block):
            ref = xout.at[lax.rem(block, 2), rows(here, 0, 128)]
            rcopy(
                ref, ref, sx.at[near[d]], rx.at[near[d]], (up if d == 1 else down, z, x, c)
            ).wait_recv()
            relay(block, near[d]).start()
            across(d, block, 0).start()
            across(d, block, 1).start()

    ring.step(2)
    block = blocks[2]

    @pl.when(lax.eq(block // 2, c))
    def _():
        for i in range(2):
            relay(block, i).wait_recv()
            across(2, block, i).start()

    ring.step(3)
    for d in (1, 3, 2):
        block = blocks[d]

        @pl.when(lax.eq(block // 2, c))
        def _(d=d, block=block):
            for i in range(2):
                from_across(d, block, i).wait_recv()
                across(d, block, i).wait_send()
            if d != 2:
                relay(block, near[d]).wait_send()

    @pl.when(lax.eq(home, c))
    def _():
        x_own(0).wait_send()
        x_own(1).wait_send()
        own_x.wait()
        own_g.wait()
        give_g.wait_send()

    @pl.when(jnp.logical_not(lax.eq(home, c)))
    def _():
        give_g.wait_recv()

    @pl.when(mine_t)
    def _():
        own_t.wait()
        for dz in range(1, NZ):
            src_z = lax.rem(z + NZ - dz, NZ)
            rcopy(
                tt.at[z], zout.at[src_z], sz.at[dz - 1], rz.at[dz - 1], (y, src_z, x, c)
            ).wait_recv()
            give_t(dz, lax.rem(z + dz, NZ)).wait_send()

    for j in range(2):
        src_y = 2 * c + j
        is_self = lax.eq(src_y, y)

        @pl.when(is_self)
        def _(j=j):
            own_d(j).wait()

        @pl.when(jnp.logical_not(is_self))
        def _(j=j, src_y=src_y):
            hand_w(j, src_y, src_y, j, j).wait_send()
            hand_d(j, src_y, j, j, j).wait_send()
            hand_d(j, src_y, j, j, j).wait_recv()

    ring.finish()


def over_chunks(z, k, body):
    def one(i, carry):
        zb = jnp.where(lax.rem(i, 2) == 0, z - 1 - k, z + 1 + k)
        body(i // 2, lax.rem(zb + NZ, NZ))
        return carry

    lax.fori_loop(0, 8, one, 0)


def over_four(zb, body):
    def one(i, carry):
        body(i, lax.rem(zb + NZ, NZ))
        return carry

    lax.fori_loop(0, 4, one, 0)


NT = (((1,), (1,)), ((), ()))
TN = (((0,), (0,)), ((), ()))


def main_kernel(
    xin, win, gain, do_ref, zin, clip_ref, live_ref, w_own, damp,
    ratio_ref, damp_ref,
    xv, wv, kvb, kc, e_s, dp_s, qv, qcat, sums, mine, oth, sib, snd_r, snd_l, got_r, got_l,
    hat, inv, diag, dqt, qn_s, don_s, rows_s, alld, x3, acc, fish, own, part, tile, box, box2,
    sl, s_sw, r_sw, sr, rr, sq, rq, s3x, r3x, s3y, r3y, s3f, r3f, sf, rf, s1, r1, s2, r2, *ring_sems,
):
    y, z, x, c = place()
    t_dev = xin.shape[1]
    queries = 2 * t_dev
    scale = 1.0 / math.sqrt(HD)
    to_exp2 = scale * math.log2(math.e)
    load_w = pltpu.make_async_copy(win, wv, sl.at[0])
    load_x = [pltpu.make_async_copy(xin.at[b], xv.at[b], sl.at[1 + b]) for b in range(2)]
    load_w.start()
    load_x[0].start()
    load_x[1].start()
    first = []
    for dz in range(NZ):
        for dc in range(NC):
            if dz or dc:
                first.append((y, lax.rem(z + dz, NZ), x, lax.rem(c + dc, NC)))
    second = []
    for dy in range(NY):
        for dx in range(NX):
            if dy or dx:
                second.append((lax.rem(y + dy, NY), z, lax.rem(x + dx, NX), c))
    third = []
    for dy in range(1, NY):
        third.append((lax.rem(y + dy, NY), z, x, 1 - c))
    greet(first + second + third)
    right, left = (y, lax.rem(z + 1, NZ), x, c), (y, lax.rem(z + NZ - 1, NZ), x, c)
    yu, yd, yf = lax.rem(y + 1, NY), lax.rem(y + NY - 1, NY), lax.rem(y + 2, NY)
    up, down = (yu, z, x, c), (yd, z, x, c)

    mine_t = lax.eq(x // 2, c)
    own_t = pltpu.make_async_copy(zin, x3.at[y, lax.rem(x, 2)], sl.at[3])

    def give_x(dx):
        return rcopy(
            zin, x3.at[y, lax.rem(x, 2)], s3x.at[dx - 1], r3x.at[dx - 1], (y, z, lax.rem(x + dx, NX), c)
        )

    @pl.when(mine_t)
    def _():
        own_t.start()
        for dx in (1, 3, 2):
            give_x(dx).start()

    def take_x():
        @pl.when(mine_t)
        def _():
            own_t.wait()

        for dx in range(1, NX):
            src = lax.rem(x + NX - dx, NX)

            @pl.when(lax.eq(src // 2, c))
            def _(dx=dx, src=src):
                rcopy(
                    zin, x3.at[y, lax.rem(src, 2)], s3x.at[dx - 1], r3x.at[dx - 1], (y, z, src, c)
                ).wait_recv()

    def give_y(direction):
        return rcopy(x3.at[y], x3.at[y], s3y.at[direction], r3y.at[direction], up if direction == 0 else down)

    def take_y(direction):
        ref = x3.at[yd if direction == 0 else yu]
        return rcopy(ref, ref, s3y.at[direction], r3y.at[direction], up if direction == 0 else down)

    def give_far(direction):
        ref = x3.at[yd if direction == 0 else yu, direction]
        return rcopy(ref, ref, s3f.at[direction], r3f.at[direction], up if direction == 0 else down)

    def take_far(direction):
        ref = x3.at[yf, direction]
        return rcopy(ref, ref, s3f.at[direction], r3f.at[direction], up if direction == 0 else down)

    kv_ring = Chunks(kvb, ring_sems[:6])
    load_w.wait()
    for b in range(2):
        load_x[b].wait()
        rows = xv[b]
        at = pl.ds(t_dev * b, t_dev)
        for j in (1, 2, 0):
            raw = jnp.dot(rows, wv[j], preferred_element_type=F32)
            if j == 2:
                kvb[2 * c + b, z, :, HD:] = raw.astype(BF)
                kv_ring.start(b)
            else:
                scale_back = lax.rsqrt(jnp.mean(raw * raw, -1, keepdims=True) + 1e-06)
                normed = raw * scale_back
                hat[b, j] = normed
                inv[b, j] = jnp.broadcast_to(scale_back, normed.shape)
                out = (normed * gain[j : j + 1]).astype(BF)
                if j == 0:
                    qv[at, :] = out
                    qcat[at, :HD] = out
                else:
                    kvb[2 * c + b, z, :, :HD] = out

    code = lax.broadcasted_iota(jnp.int32, (HD, t_dev), 0)

    def key_codes(s, carry):
        good = jnp.logical_and(code == clip_ref[s], live_ref[s] == 1)
        value = jnp.where(good, 0.0, jnp.where(code < CLIPS, -BIG, 0.0))
        kc[s] = value.T.astype(BF)
        return carry

    lax.fori_loop(0, NY * NZ, key_codes, 0)
    for b in range(2):
        s = (2 * c + b) * NZ + z
        at = pl.ds(t_dev * b, t_dev)
        qcat[at, HD:] = jnp.where(code == clip_ref[s], 1.0, 0.0).T.astype(BF)
        rows_s[0:1, at] = 1.0 - live_ref[s].astype(F32)

    sums[...] = jnp.zeros_like(sums)

    def fold(v):
        return jnp.sum(v.reshape(t_dev // 8, 8, queries), 0)

    def pass_one(yb, zb):
        s = yb * NZ + zb
        k_cat = jnp.concatenate([kvb[yb, zb, :, :HD], kc[s]], 1)
        e = jnp.exp2(lax.dot_general(k_cat, qcat[...], NT, preferred_element_type=F32) * to_exp2)
        dp = lax.dot_general(kvb[yb, zb, :, HD:], do_ref[...], NT, preferred_element_type=F32)
        e_s[s] = e.astype(BF)
        dp_s[s] = dp.astype(BF)
        sums[0] += fold(e)
        sums[1] += fold(e * dp)

    kv_ring.start_wait()
    over_four(z, pass_one)

    def gather_step(k, carry):
        kv_ring.step(k)

        @pl.when(k == 1)
        def _():
            take_x()
            give_y(0).start()
            give_y(1).start()

        over_chunks(z, k, pass_one)
        return carry

    lax.fori_loop(0, 3, gather_step, 0)
    kv_ring.last()
    over_four(z + 4, pass_one)

    total = jnp.sum(sums[0], 0, keepdims=True)
    dot = jnp.sum(sums[1], 0, keepdims=True)
    qf, dof = qv[...].astype(F32), do_ref[...].astype(F32)
    own_k = kvb[pl.ds(2 * c, 2), z, :, :HD].reshape(queries, HD).astype(F32)
    own_v = kvb[pl.ds(2 * c, 2), z, :, HD:].reshape(queries, HD).astype(F32)
    own_e = rows_s[0:1, :] * jnp.exp2(jnp.sum((qf * own_k).T, 0, keepdims=True) * to_exp2)
    own_dp = jnp.sum((dof * own_v).T, 0, keepdims=True)
    total = total + own_e
    dot = dot + own_e * own_dp
    inv_row = 1.0 / total
    row_dot = dot * inv_row
    own_p = own_e * inv_row
    own_ds = own_p * (own_dp - row_dot)
    column = lambda v: jnp.broadcast_to(v, (HD, queries)).T
    p_col = column(own_p).astype(BF).astype(F32)
    ds_col = column(own_ds).astype(BF).astype(F32)
    inv_col = column(inv_row)
    diag[:, :HD] = ds_col * qf * scale
    diag[:, HD:] = p_col * dof
    qn_s[...] = (qf * inv_col).astype(BF)
    don_s[...] = (dof * inv_col).astype(BF)
    rows_s[1:2, :] = row_dot
    rows_s[2:3, :] = inv_row
    dqt[...] = jnp.zeros_like(dqt)
    got_r[0, 1] = jnp.zeros_like(got_r[0, 1])
    got_l[0, 0] = jnp.zeros_like(got_l[0, 0])

    def pass_two(yb, zb):
        s = yb * NZ + zb
        e = e_s[s]
        ds = (e.astype(F32) * (dp_s[s].astype(F32) - rows_s[1:2, :])).astype(BF)
        dv = jnp.dot(e, don_s[...], preferred_element_type=F32)
        dk = jnp.dot(ds, qn_s[...], preferred_element_type=F32) * scale
        dqt[...] += lax.dot_general(kvb[yb, zb, :, :HD], ds, TN, preferred_element_type=F32)
        return jnp.concatenate([dk, dv], 1).astype(BF)

    def swap(i, offset):
        at = lax.rem(z + offset + NZ, NZ)
        return rcopy(oth.at[:, at], sib.at[:, at], s_sw.at[i], r_sw.at[i], (y, z, x, 1 - c))

    def terms(i, offset):
        at = lax.rem(z + offset + NZ, NZ)

        def theirs(b, carry):
            oth[b, at] = pass_two(2 * (1 - c) + b, at)
            return carry

        def ours(b, carry):
            mine[b, at] = pass_two(2 * c + b, at)
            return carry

        lax.fori_loop(0, 2, theirs, 0)
        swap(i, offset).start()
        lax.fori_loop(0, 2, ours, 0)

    def chip(offset, half):
        at = lax.rem(z + offset + NZ, NZ)
        return mine[half, at].astype(F32) + sib[half, at].astype(F32)

    def send_r(t, b):
        return rcopy(snd_r.at[t, b], got_r.at[t, b], sr.at[t, b], rr.at[t, b], right)

    def send_l(t, b):
        return rcopy(snd_l.at[t, b], got_l.at[t, b], sq.at[t, b], rq.at[t, b], left)

    terms(0, 4)

    def sum_step(t, carry):
        terms(2 * t - 1, 4 - t)

        @pl.when(t == 1)
        def _():
            swap(0, 4).wait_recv()
            snd_r[0, 0] = chip(4, 0).astype(BF)
            send_r(0, 0).start()
            snd_l[0, 1] = chip(4, 1).astype(BF)
            send_l(0, 1).start()

        @pl.when(t == 2)
        def _():
            for direction in range(2):
                take_y(direction).wait_recv()
                give_far(direction).start()

        terms(2 * t, t - 4)
        swap(2 * t - 1, 4 - t).wait_recv()
        swap(2 * t, t - 4).wait_recv()
        for b in range(2):
            if b == 0:
                send_r(t - 1, 0).wait_recv()
            else:
                pl.when(t > 1)(lambda: send_r(t - 1, 1).wait_recv())
            snd_r[t, b] = (chip(4 - t, b) + got_r[t - 1, b].astype(F32)).astype(BF)
            send_r(t, b).start()
            if b == 1:
                send_l(t - 1, 1).wait_recv()
            else:
                pl.when(t > 1)(lambda: send_l(t - 1, 0).wait_recv())
            snd_l[t, b] = (chip(t - 4, b) + got_l[t - 1, b].astype(F32)).astype(BF)
            send_l(t, b).start()
        return carry

    lax.fori_loop(1, 4, sum_step, 0)
    terms(7, 0)
    dq = (dqt[...] * rows_s[2:3, :]).T
    swap(7, 0).wait_recv()
    d_ring = Chunks(alld, ring_sems[6:])
    for b in range(2):
        at = pl.ds(t_dev * b, t_dev)
        send_r(3, b).wait_recv()
        send_l(3, b).wait_recv()
        dkv = chip(0, b) + got_r[3, b].astype(F32) + got_l[3, b].astype(F32) + diag[at, :]
        own_kb = kvb[2 * c + b, z, :, :HD].astype(F32)
        dqn = (dq[t_dev * b : t_dev * (b + 1)] + ds_col[t_dev * b : t_dev * (b + 1)] * own_kb) * scale
        for j in range(2):
            upstream = (dqn if j == 0 else dkv[:, :HD]) * gain[j : j + 1]
            normed = hat[b, j]
            back = inv[b, j] * (upstream - normed * jnp.mean(normed * upstream, -1, keepdims=True))
            alld[2 * c + b, z, :, HD * j : HD * (j + 1)] = back.astype(BF)
        alld[2 * c + b, z, :, 2 * HD :] = dkv[:, HD:].astype(BF)
        d_ring.start(b)

    acc[...] = jnp.zeros_like(acc)
    for direction in range(2):
        take_far(direction).wait_recv()

    def grads(yb, zb):
        s = yb * NZ + zb
        rows = jnp.concatenate([x3[yb, 0, zb], x3[yb, 1, zb]], 0)
        parts = []
        for clip in range(CLIPS):
            keep = jnp.broadcast_to(jnp.where(clip_ref[s] == clip, 1.0, 0.0), rows.shape).astype(BF)
            parts.append(rows * keep)
        acc[...] += jnp.dot(jnp.concatenate(parts, 0), alld[yb, zb], preferred_element_type=F32)

    d_ring.start_wait()
    over_four(z, grads)

    def grad_step(k, carry):
        d_ring.step(k)
        over_chunks(z, k, grads)
        return carry

    lax.fori_loop(0, 3, grad_step, 0)
    d_ring.last()
    over_four(z + 4, grads)
    two = 2 * ROWS
    fisher = jnp.square(acc[0:two]) + jnp.square(acc[two : 2 * two]) + jnp.square(acc[2 * two :])
    for j in range(2):
        fish[j] = fisher[ROWS * j : ROWS * (j + 1)]
    rows = jnp.sum(fisher.reshape(two // 8, 8, 3 * HD), 0)
    part[...] = rows[:, :HD] + rows[:, HD : 2 * HD] + rows[:, 2 * HD :]

    for i, device in enumerate(first):
        rcopy(part, box.at[i], s1.at[i], r1.at[i], device).start()
    home, slot = y // 2, lax.rem(y, 2)

    def give(j, target, dst_slot, recv_at):
        return rcopy(fish.at[j], own.at[dst_slot], sf.at[j], rf.at[recv_at], (target, z, x, home))

    def keep_own(j):
        return pltpu.make_async_copy(fish.at[j], own.at[slot], sl.at[4])

    for j in range(2):
        target = 2 * c + j

        @pl.when(lax.eq(target, y))
        def _(j=j):
            keep_own(j).start()

        @pl.when(jnp.logical_not(lax.eq(target, y)))
        def _(j=j, target=target):
            give(j, target, slot, slot).start()

    for i, device in enumerate(first):
        rcopy(part, box.at[i], s1.at[i], r1.at[i], device).wait_recv()
    tile[...] = part[...] + jnp.sum(box[...], 0)
    for i, device in enumerate(second):
        rcopy(tile, box2.at[i], s2.at[i], r2.at[i], device).start()

    kv_ring.finish()
    d_ring.finish()
    for i, offset in enumerate((4, 3, -3, 2, -2, 1, -1, 0)):
        swap(i, offset).wait_send()
    for t in range(4):
        for b in range(2):
            if t or b == 0:
                send_r(t, b).wait_send()
            if t or b == 1:
                send_l(t, b).wait_send()
    for direction in range(2):
        give_y(direction).wait_send()
        give_far(direction).wait_send()

    @pl.when(mine_t)
    def _():
        for dx in range(1, NX):
            give_x(dx).wait_send()

    for j in range(2):
        target = 2 * c + j

        @pl.when(lax.eq(target, y))
        def _(j=j):
            keep_own(j).wait()

        @pl.when(jnp.logical_not(lax.eq(target, y)))
        def _(j=j, target=target):
            give(j, target, j, j).wait_recv()
            give(j, target, j, j).wait_send()

    for i, device in enumerate(second):
        rcopy(tile, box2.at[i], s2.at[i], r2.at[i], device).wait_recv()
    whole = jnp.sum(tile[...] + jnp.sum(box2[...], 0))
    divisor = whole / (3 * D * HEADS * HD) + 1e-06
    for j in range(3):
        for h in range(2):
            lanes = pl.ds(HD * h, HD)
            ratio = own[h, :, HD * j : HD * (j + 1)] / divisor
            ratio_ref[j, :, lanes] = ratio
            damp_ref[j, :, lanes] = (
                w_own[j, :, lanes].astype(F32) / (1.0 + damp[:, lanes].astype(F32) * ratio)
            ).astype(BF)
    for i, device in enumerate(first):
        rcopy(part, box.at[i], s1.at[i], r1.at[i], device).wait_send()
    for i, device in enumerate(second):
        rcopy(tile, box2.at[i], s2.at[i], r2.at[i], device).wait_send()


def shape(dims, dtype=BF):
    return jax.ShapeDtypeStruct(dims, dtype)


def comm(collective, limit=None):
    return pltpu.CompilerParams(collective_id=collective, has_side_effects=True, vmem_limit_bytes=limit)


def on_device(tokens, w_qkv, gains, cotangent, token_clip, key_live, damp_mask):
    y, z, x, c = place()
    n_tok = token_clip.shape[0]
    t_dev = n_tok // (NY * NZ)
    xout, wout, dout, gout, zout = pl.pallas_call(
        gather_inputs,
        out_shape=(
            shape((2, t_dev, D)),
            shape((3, NY, NZ, ROWS, HD)),
            shape((2, t_dev, HD)),
            shape((2, HD), F32),
            shape((NZ, ROWS, t_dev)),
        ),
        in_specs=[ANY] * 4,
        out_specs=(ANY,) * 5,
        scratch_shapes=[
            pltpu.VMEM((t_dev, NZ * ROWS), BF),
            pltpu.VMEM((NZ, ROWS, t_dev), BF),
            DMA((6,)),
            DMA((2,)), DMA((2,)), DMA((2,)), DMA((2,)), DMA((1,)), DMA((1,)),
            DMA((4,)), DMA((4,)), DMA((3, 2)), DMA((3, 2)), DMA((7,)), DMA((7,)),
            *RING_SEMS,
        ],
        compiler_params=comm(0),
        name="gather_inputs",
    )(tokens, w_qkv, cotangent, gains)

    blocks = (NY, NZ, t_dev)
    half = (2, NZ, t_dev, 2 * HD)
    trips = (4, 2, t_dev, 2 * HD)
    queries = 2 * t_dev
    return pl.pallas_call(
        main_kernel,
        out_shape=(shape((3, ROWS, 2 * HD), F32), shape((3, ROWS, 2 * HD))),
        in_specs=[ANY, ANY, VMEM, VMEM, ANY, VMEM, VMEM, VMEM, VMEM],
        out_specs=(VMEM, VMEM),
        scratch_shapes=[
            pltpu.VMEM((2, t_dev, D), BF),
            pltpu.VMEM((3, D, HD), BF),
            pltpu.VMEM((*blocks, 2 * HD), BF),
            pltpu.VMEM((NY * NZ, t_dev, HD), BF),
            pltpu.VMEM((NY * NZ, t_dev, queries), BF),
            pltpu.VMEM((NY * NZ, t_dev, queries), BF),
            pltpu.VMEM((queries, HD), BF),
            pltpu.VMEM((queries, 2 * HD), BF),
            pltpu.VMEM((2, 8, queries), F32),
            pltpu.VMEM(half, BF), pltpu.VMEM(half, BF), pltpu.VMEM(half, BF),
            pltpu.VMEM(trips, BF), pltpu.VMEM(trips, BF), pltpu.VMEM(trips, BF), pltpu.VMEM(trips, BF),
            pltpu.VMEM((2, 2, t_dev, HD), F32), pltpu.VMEM((2, 2, t_dev, HD), F32),
            pltpu.VMEM((queries, 2 * HD), F32),
            pltpu.VMEM((HD, queries), F32),
            pltpu.VMEM((queries, HD), BF), pltpu.VMEM((queries, HD), BF),
            pltpu.VMEM((8, queries), F32),
            pltpu.VMEM((*blocks, 3 * HD), BF),
            pltpu.VMEM((NY, 2, NZ, ROWS, t_dev), BF),
            pltpu.VMEM((CLIPS * 2 * ROWS, 3 * HD), F32),
            pltpu.VMEM((2, ROWS, 3 * HD), F32), pltpu.VMEM((2, ROWS, 3 * HD), F32),
            pltpu.VMEM((8, HD), F32), pltpu.VMEM((8, HD), F32),
            pltpu.VMEM((15, 8, HD), F32), pltpu.VMEM((15, 8, HD), F32),
            DMA((5,)), DMA((8,)), DMA((8,)),
            DMA((4, 2)), DMA((4, 2)), DMA((4, 2)), DMA((4, 2)),
            DMA((3,)), DMA((3,)), DMA((2,)), DMA((2,)), DMA((2,)), DMA((2,)), DMA((2,)), DMA((2,)),
            DMA((15,)), DMA((15,)), DMA((15,)), DMA((15,)),
            *CHUNK_SEMS, *CHUNK_SEMS,
        ],
        compiler_params=comm(1, 63 * MIB),
        name="main_kernel",
    )(
        xout, wout.reshape(3, D, HD), gout, dout.reshape(queries, HD), zout,
        token_clip.reshape(NY * NZ, 1, t_dev), key_live.reshape(NY * NZ, 1, t_dev), w_qkv, damp_mask,
    )


def solution(mesh):
    grid = Mesh(mesh.devices.reshape(NY, NZ, NX, NC), ("y", "z", "x", "c"))
    seq, head = ("y", "z"), ("x", "c")
    return jax.shard_map(
        on_device,
        mesh=grid,
        in_specs=(
            P(seq, None),
            P(None, seq, head),
            P(None, head),
            P(seq, head),
            P(),
            P(),
            P(seq, head),
        ),
        out_specs=(P(None, seq, head), P(None, seq, head)),
        check_vma=False,
    )
```

```python
import math

import jax
import jax.numpy as jnp
from jax import lax
from jax.experimental import pallas as pl
from jax.experimental.pallas import tpu as pltpu
from jax.sharding import Mesh, PartitionSpec as P

MESH = pl.DeviceIdType.MESH
D = 3072
HD = 128
HEADS = 16
CLIPS = 3
NY, NZ, NX, NC = 4, 8, 4, 2
ROWS = D // (NY * NZ)
BF = jnp.bfloat16
F32 = jnp.float32
BIG = 30000.0
ANY = pl.BlockSpec(memory_space=pl.ANY)
VMEM = pl.BlockSpec(memory_space=pltpu.VMEM)
SMEM = pl.BlockSpec(memory_space=pltpu.SMEM)
DMA = pltpu.SemaphoreType.DMA
MIB = 1 << 20


def place():
    return lax.axis_index("y"), lax.axis_index("z"), lax.axis_index("x"), lax.axis_index("c")


def rcopy(src, dst, send, recv, device):
    return pltpu.make_async_remote_copy(
        src_ref=src, dst_ref=dst, send_sem=send, recv_sem=recv, device_id=device, device_id_type=MESH
    )


def greet(devices):
    barrier = pltpu.get_barrier_semaphore()
    for device in devices:
        pl.semaphore_signal(barrier, inc=1, device_id=device, device_id_type=MESH)
    pl.semaphore_wait(barrier, len(devices))


class Ring:
    def __init__(self, view, sems):
        self.view = view
        self.send_r, self.recv_r, self.send_l, self.recv_l, self.send_s, self.recv_s = sems
        self.y, self.z, self.x, self.c = place()

    def right(self, k, at):
        v = self.view(self.c, lax.rem(at + NZ, NZ), None if k < 3 else 0)
        return rcopy(v, v, self.send_r.at[k], self.recv_r.at[k], (self.y, lax.rem(self.z + 1, NZ), self.x, self.c))

    def left(self, k, at):
        v = self.view(self.c, lax.rem(at, NZ), None if k < 3 else 1)
        return rcopy(
            v, v, self.send_l.at[k], self.recv_l.at[k], (self.y, lax.rem(self.z + NZ - 1, NZ), self.x, self.c)
        )

    def sib(self, i, core):
        if i == 0:
            at, half = self.z, None
        elif i < 5:
            at, half = self.z - i, (None if i < 4 else 0)
        else:
            at, half = self.z + i - 4, (None if i < 8 else 1)
        v = self.view(core, lax.rem(at + NZ, NZ), half)
        return rcopy(v, v, self.send_s.at[i], self.recv_s.at[i], (self.y, self.z, self.x, 1 - self.c))

    def start(self):
        self.right(0, self.z).start()
        self.left(0, self.z).start()
        self.sib(0, self.c).start()

    def step(self, k):
        self.right(k, self.z - 1 - k).wait_recv()
        if k < 3:
            self.right(k + 1, self.z - 1 - k).start()
        self.sib(1 + k, self.c).start()
        self.left(k, self.z + 1 + k).wait_recv()
        if k < 3:
            self.left(k + 1, self.z + 1 + k).start()
        self.sib(5 + k, self.c).start()

    def finish(self):
        for k in range(4):
            self.right(k, self.z - k).wait_send()
            self.left(k, self.z + k).wait_send()
        for i in range(9):
            self.sib(i, self.c).wait_send()


RING_SEMS = [DMA((4,)), DMA((4,)), DMA((4,)), DMA((4,)), DMA((9,)), DMA((9,))]


def half_view(ref, lead=False):
    def view(core, z, half):
        if half is None:
            where = pl.ds(2 * core, 2)
        else:
            where = 2 * core + half
        return ref.at[:, where, z] if lead else ref.at[where, z]

    return view


class Chunks:
    def __init__(self, buf, sems):
        self.buf = buf
        self.send_r, self.recv_r, self.send_l, self.recv_l, self.send_s, self.recv_s = sems
        self.y, self.z, self.x, self.c = place()

    def at(self, core, z, b):
        return self.buf.at[2 * core + b, lax.rem(z + NZ, NZ)]

    def right(self, k, b, z):
        v = self.at(self.c, z, b)
        return rcopy(
            v, v, self.send_r.at[k, b], self.recv_r.at[k, b], (self.y, lax.rem(self.z + 1, NZ), self.x, self.c)
        )

    def left(self, k, b, z):
        v = self.at(self.c, z, b)
        return rcopy(
            v, v, self.send_l.at[k, b], self.recv_l.at[k, b], (self.y, lax.rem(self.z + NZ - 1, NZ), self.x, self.c)
        )

    def sib(self, i, b, core, z):
        v = self.at(core, z, b)
        return rcopy(v, v, self.send_s.at[i, b], self.recv_s.at[i, b], (self.y, self.z, self.x, 1 - self.c))

    def start(self, b):
        self.right(0, b, self.z).start()
        self.left(0, b, self.z).start()
        self.sib(0, b, self.c, self.z).start()

    def step(self, k, b):
        zr, zl = self.z - 1 - k, self.z + 1 + k
        self.right(k, b, zr).wait_recv()
        pl.when(jnp.logical_or(b == 0, k < 2))(lambda: self.right(k + 1, b, zr).start())
        self.sib(1 + k, b, self.c, zr).start()
        self.left(k, b, zl).wait_recv()
        pl.when(jnp.logical_or(b == 1, k < 2))(lambda: self.left(k + 1, b, zl).start())
        self.sib(5 + k, b, self.c, zl).start()

    def step_sib(self, k, b):
        self.sib(1 + k, b, 1 - self.c, self.z - 1 - k).wait_recv()
        self.sib(5 + k, b, 1 - self.c, self.z + 1 + k).wait_recv()

    def far(self, b):
        far = self.z + 4
        pl.when(b == 0)(lambda: self.right(3, 0, far).wait_recv())
        pl.when(b == 1)(lambda: self.left(3, 1, far).wait_recv())
        self.sib(4, b, self.c, far).start()

    def finish(self):
        for b in range(2):
            for k in range(4):
                if k < 3 or b == 0:
                    self.right(k, b, self.z - k).wait_send()
                if k < 3 or b == 1:
                    self.left(k, b, self.z + k).wait_send()
            for i in range(8):
                self.sib(i, b, self.c, self.z).wait_send()


CHUNK_SEMS = [DMA((4, 2)), DMA((4, 2)), DMA((4, 2)), DMA((4, 2)), DMA((8, 2)), DMA((8, 2))]


def four_blocks(z1, y1, z2, y2, body):
    def one(i, carry):
        zb = jnp.where(lax.rem(i, 2) == 0, z1, z2)
        yb = jnp.where(i < 2, y1, y2)
        body(yb, lax.rem(zb + NZ, NZ))
        return carry

    lax.fori_loop(0, 4, one, 0)


def two_blocks(zb, y1, y2, body):
    def one(i, carry):
        body(jnp.where(i == 0, y1, y2), lax.rem(zb + NZ, NZ))
        return carry

    lax.fori_loop(0, 2, one, 0)


NT = (((1,), (1,)), ((), ()))
TN = (((0,), (0,)), ((), ()))


def main_kernel(
    tok, w, cot, gains, clip_ref, live_ref, w_own, damp,
    ratio_ref, damp_ref,
    xv, wv, kvb, kc, e_s, dp_s, qv, qcat, sums, mine, oth, sib, snd_r, snd_l, got_r, got_l,
    hat, inv, diag, dqt, qn_s, don_s, rows_s, alld, x3, acc, fish, own, part, tile, box, box2,
    do_v, gain, tin, tt,
    sl, s_sw, r_sw, sr, rr, sq, rq, s3x, r3x, s3y, r3y, s3f, r3f, sf, rf, s1, r1, s2, r2,
    sw, rw, sd, rd, sg, rg, sx, rx, sxx, rxx, sz, rz, *ring_sems,
):
    y, z, x, c = place()
    t_dev = tok.shape[0]
    queries = 2 * t_dev
    scale = 1.0 / math.sqrt(HD)
    to_exp2 = scale * math.log2(math.e)
    sems_w, sems_kv, sems_d = ring_sems[:6], ring_sems[6:12], ring_sems[12:]
    h = lax.rem(x, 2)
    xr, xl = lax.rem(x + 1, NX), lax.rem(x + NX - 1, NX)
    home, slot = y // 2, lax.rem(y, 2)
    at_home = lax.eq(home, c)
    here, there = 128 * h, 128 * (1 - h)
    right, left = (y, lax.rem(z + 1, NZ), x, c), (y, lax.rem(z + NZ - 1, NZ), x, c)
    yu, yd, yf = lax.rem(y + 1, NY), lax.rem(y + NY - 1, NY), lax.rem(y + 2, NY)
    up, down = (yu, z, x, c), (yd, z, x, c)
    mine_t = lax.eq(x // 2, c)
    load_t = pltpu.make_async_copy(tok.at[:, pl.ds(pl.multiple_of(768 * x, 768), 768)], tin, sl.at[0])
    own_x = pltpu.make_async_copy(tok, xv.at[slot], sl.at[3])
    g_src = gains.at[:, pl.ds(pl.multiple_of(128 * slot, 128), 128)]
    own_g = pltpu.make_async_copy(g_src, gain, sl.at[5])

    @pl.when(mine_t)
    def _():
        load_t.start()

    @pl.when(at_home)
    def _():
        own_x.start()
        own_g.start()

    first = []
    for dz in range(NZ):
        for dc in range(NC):
            if dz or dc:
                first.append((y, lax.rem(z + dz, NZ), x, lax.rem(c + dc, NC)))
    second = []
    for dy in range(NY):
        for dx in range(NX):
            if dy or dx:
                second.append((lax.rem(y + dy, NY), z, lax.rem(x + dx, NX), c))
    third = []
    for dy in range(1, NY):
        third.append((lax.rem(y + dy, NY), z, x, 1 - c))
    greet(first + second + third)

    def span(base, piece, count):
        return pl.ds(pl.multiple_of(base + 64 * piece, 64), count)

    def hand_w(j, target, src_y, sem_at, recv_at):
        return rcopy(
            w.at[:, :, pl.ds(128 * j, 128)], wv.at[:, src_y, z], sw.at[sem_at], rw.at[recv_at], (target, z, x, home)
        )

    def hand_d(j, target, dst_slot, sem_at, recv_at):
        return rcopy(
            cot.at[:, pl.ds(128 * j, 128)], do_v.at[dst_slot], sd.at[sem_at], rd.at[recv_at], (target, z, x, home)
        )

    def own_w(j):
        return pltpu.make_async_copy(w.at[:, :, pl.ds(128 * j, 128)], wv.at[:, y, z], sl.at[1])

    def own_d(j):
        return pltpu.make_async_copy(cot.at[:, pl.ds(128 * j, 128)], do_v.at[slot], sl.at[2])

    for j in range(2):
        target = 2 * c + j
        is_self = lax.eq(target, y)

        @pl.when(is_self)
        def _(j=j):
            own_w(j).start()
            own_d(j).start()

        @pl.when(jnp.logical_not(is_self))
        def _(j=j, target=target):
            hand_w(j, target, y, j, slot).start()

    def x_own(direction):
        ref, dev = tok.at[span(here, 0, 128)], (up if direction == 0 else down)
        return rcopy(ref, xv.at[slot, span(here, 0, 128)], sx.at[direction], rx.at[direction], dev)

    give_g = rcopy(g_src, gain, sg.at[0], rg.at[0], (y, z, x, 1 - c))

    @pl.when(at_home)
    def _():
        x_own(0).start()
        x_own(1).start()
        give_g.start()

    for j in range(2):
        target = 2 * c + j

        @pl.when(jnp.logical_not(lax.eq(target, y)))
        def _(j=j, target=target):
            hand_d(j, target, slot, j, slot).start()

    def give_t(dz, dst_z):
        return rcopy(
            tt.at[dst_z], x3.at[y, lax.rem(x, 2), z], sz.at[dz - 1], rz.at[dz - 1], (y, dst_z, x, c)
        )

    def take_t(dz, src_z):
        return rcopy(
            tt.at[z], x3.at[y, lax.rem(x, 2), src_z], sz.at[dz - 1], rz.at[dz - 1], (y, src_z, x, c)
        )

    @pl.when(mine_t)
    def _():
        load_t.wait()
        turned = tin[...].T
        for dz in range(NZ):
            tt[dz] = turned[ROWS * dz : ROWS * (dz + 1)]
        x3[y, lax.rem(x, 2), z] = tt[z]
        for dz in range(1, NZ):
            give_t(dz, lax.rem(z + dz, NZ)).start()

    for j in range(2):
        src_y = 2 * c + j
        is_self = lax.eq(src_y, y)

        @pl.when(is_self)
        def _(j=j):
            own_w(j).wait()

        @pl.when(jnp.logical_not(is_self))
        def _(j=j, src_y=src_y):
            hand_w(j, src_y, src_y, j, j).wait_recv()

    w_ring = Ring(half_view(wv, lead=True), sems_w)
    w_ring.start()
    w_ring.step(0)

    def piece(block, base, i):
        return xv.at[lax.rem(block, 2), span(base, i, 64)]

    def relay(block, i):
        ref = piece(block, here, i)
        return rcopy(ref, ref, sx.at[2 + i], rx.at[2 + i], up if i == 0 else down)

    def across(d, block, i):
        ref = piece(block, here, i)
        return rcopy(ref, ref, sxx.at[d - 1, i], rxx.at[d - 1, i], (y, z, xr if i == 0 else xl, c))

    def from_across(d, block, i):
        ref = piece(block, there, i)
        return rcopy(ref, ref, sxx.at[d - 1, i], rxx.at[d - 1, i], (y, z, xr if i == 0 else xl, c))

    blocks = {d: lax.rem(y + NY - d, NY) for d in (1, 2, 3)}
    near = {1: 0, 3: 1}
    for d in (1, 3):
        block = blocks[d]

        @pl.when(lax.eq(block // 2, c))
        def _(d=d, block=block):
            ref = xv.at[lax.rem(block, 2), span(here, 0, 128)]
            rcopy(ref, ref, sx.at[near[d]], rx.at[near[d]], up if d == 1 else down).wait_recv()
            relay(block, near[d]).start()
            across(d, block, 0).start()
            across(d, block, 1).start()

    w_ring.step(1)
    w_ring.step(2)
    block = blocks[2]

    @pl.when(lax.eq(block // 2, c))
    def _():
        for i in range(2):
            relay(block, i).wait_recv()
            across(2, block, i).start()

    w_ring.step(3)
    for i in range(9):
        w_ring.sib(i, 1 - c).wait_recv()

    def take_block(d):
        block = blocks[d]

        @pl.when(lax.eq(block // 2, c))
        def _():
            for i in range(2):
                from_across(d, block, i).wait_recv()

    @pl.when(at_home)
    def _():
        own_x.wait()
        own_g.wait()

    @pl.when(jnp.logical_not(at_home))
    def _():
        give_g.wait_recv()
        take_block(1)
        take_block(3)

    kv_ring = Chunks(kvb, sems_kv)
    b_first = jnp.where(at_home, slot, 1 - slot)

    def project(b):
        block_rows = xv[b]
        at = pl.ds(pl.multiple_of(t_dev * b, t_dev), t_dev)
        for j in (1, 2, 0):
            raw = jnp.dot(block_rows, wv[j].reshape(D, HD), preferred_element_type=F32)
            if j == 2:
                kvb[2 * c + b, z, :, HD:] = raw.astype(BF)
                kv_ring.start(b)
            else:
                scale_back = lax.rsqrt(jnp.mean(raw * raw, -1, keepdims=True) + 1e-06)
                normed = raw * scale_back
                hat[b, j] = normed
                inv[b, j] = jnp.broadcast_to(scale_back, normed.shape)
                out = (normed * gain[j : j + 1, :]).astype(BF)
                if j == 0:
                    qv[at, :] = out
                    qcat[at, :HD] = out
                else:
                    kvb[2 * c + b, z, :, :HD] = out

    project(b_first)

    code = lax.broadcasted_iota(jnp.int32, (HD, t_dev), 0)

    def key_codes(s, carry):
        good = jnp.logical_and(code == clip_ref[s], live_ref[s] == 1)
        value = jnp.where(good, 0.0, jnp.where(code < CLIPS, -BIG, 0.0))
        kc[s] = value.T.astype(BF)
        return carry

    lax.fori_loop(0, NY * NZ, key_codes, 0)
    for b in range(2):
        s = (2 * c + b) * NZ + z
        at = pl.ds(t_dev * b, t_dev)
        qcat[at, HD:] = jnp.where(code == clip_ref[s], 1.0, 0.0).T.astype(BF)
        rows_s[0:1, at] = 1.0 - live_ref[s].astype(F32)

    kv_ring.step(0, b_first)

    @pl.when(at_home)
    def _():
        take_block(1)
        take_block(3)

    @pl.when(jnp.logical_not(at_home))
    def _():
        take_block(2)

    b_second = 1 - b_first
    project(b_second)

    def give_x(dx):
        ref = x3.at[y, lax.rem(x, 2)]
        return rcopy(ref, ref, s3x.at[dx - 1], r3x.at[dx - 1], (y, z, lax.rem(x + dx, NX), c))

    @pl.when(mine_t)
    def _():
        for dz in range(1, NZ):
            take_t(dz, lax.rem(z + NZ - dz, NZ)).wait_recv()
        for dx in (1, 3, 2):
            give_x(dx).start()

    def take_x():
        for dx in range(1, NX):
            src = lax.rem(x + NX - dx, NX)

            @pl.when(lax.eq(src // 2, c))
            def _(dx=dx, src=src):
                ref = x3.at[y, lax.rem(src, 2)]
                rcopy(ref, ref, s3x.at[dx - 1], r3x.at[dx - 1], (y, z, src, c)).wait_recv()

    def give_y(direction):
        return rcopy(x3.at[y], x3.at[y], s3y.at[direction], r3y.at[direction], up if direction == 0 else down)

    def take_y(direction):
        ref = x3.at[yd if direction == 0 else yu]
        return rcopy(ref, ref, s3y.at[direction], r3y.at[direction], up if direction == 0 else down)

    def give_far(direction):
        ref = x3.at[yd if direction == 0 else yu, direction]
        return rcopy(ref, ref, s3f.at[direction], r3f.at[direction], up if direction == 0 else down)

    def take_far(direction):
        ref = x3.at[yf, direction]
        return rcopy(ref, ref, s3f.at[direction], r3f.at[direction], up if direction == 0 else down)

    for j in range(2):
        src_y = 2 * c + j
        is_self = lax.eq(src_y, y)

        @pl.when(is_self)
        def _(j=j):
            own_d(j).wait()

        @pl.when(jnp.logical_not(is_self))
        def _(j=j, src_y=src_y):
            hand_d(j, src_y, j, j, j).wait_recv()

    sums[...] = jnp.zeros_like(sums)

    def fold(v):
        return jnp.sum(v.reshape(t_dev // 8, 8, queries), 0)

    def pass_one(yb, zb):
        s = yb * NZ + zb
        k_cat = jnp.concatenate([kvb[yb, zb, :, :HD], kc[s]], 1)
        e = jnp.exp2(lax.dot_general(k_cat, qcat[...], NT, preferred_element_type=F32) * to_exp2)
        dp = lax.dot_general(kvb[yb, zb, :, HD:], do_v[...].reshape(queries, HD), NT, preferred_element_type=F32)
        e_s[s] = e.astype(BF)
        dp_s[s] = dp.astype(BF)
        sums[0] += fold(e)
        sums[1] += fold(e * dp)

    def blocks_of(k, b):
        kv_ring.step_sib(k, 1 - b)
        four_blocks(z - 1 - k, 2 * c + b, z + 1 + k, 2 * (1 - c) + 1 - b, pass_one)

    kv_ring.sib(0, b_second, 1 - c, z).wait_recv()
    two_blocks(z, 2 * c + b_first, 2 * (1 - c) + b_second, pass_one)
    blocks_of(0, b_first)
    kv_ring.sib(0, b_first, 1 - c, z).wait_recv()
    two_blocks(z, 2 * c + b_second, 2 * (1 - c) + b_first, pass_one)

    def gather_step(i, carry):
        b = jnp.where(lax.rem(i, 2) == 0, b_second, b_first)
        k = (i + 1) // 2
        kv_ring.step(k, b)
        blocks_of(k, b)
        return carry

    lax.fori_loop(0, 5, gather_step, 0)
    kv_ring.far(b_first)
    kv_ring.far(b_second)
    take_x()
    give_y(0).start()
    give_y(1).start()
    for b in range(2):
        kv_ring.sib(4, b, 1 - c, z + 4).wait_recv()
    two_blocks(z + 4, 2 * c, 2 * c + 1, pass_one)
    two_blocks(z + 4, 2 * (1 - c), 2 * (1 - c) + 1, pass_one)

    total = jnp.sum(sums[0], 0, keepdims=True)
    dot = jnp.sum(sums[1], 0, keepdims=True)
    qf, dof = qv[...].astype(F32), do_v[...].reshape(queries, HD).astype(F32)
    own_k = kvb[pl.ds(2 * c, 2), z, :, :HD].reshape(queries, HD).astype(F32)
    own_v = kvb[pl.ds(2 * c, 2), z, :, HD:].reshape(queries, HD).astype(F32)
    own_e = rows_s[0:1, :] * jnp.exp2(jnp.sum((qf * own_k).T, 0, keepdims=True) * to_exp2)
    own_dp = jnp.sum((dof * own_v).T, 0, keepdims=True)
    total = total + own_e
    dot = dot + own_e * own_dp
    inv_row = 1.0 / total
    row_dot = dot * inv_row
    own_p = own_e * inv_row
    own_ds = own_p * (own_dp - row_dot)
    column = lambda v: jnp.broadcast_to(v, (HD, queries)).T
    p_col = column(own_p).astype(BF).astype(F32)
    ds_col = column(own_ds).astype(BF).astype(F32)
    inv_col = column(inv_row)
    diag[:, :HD] = ds_col * qf * scale
    diag[:, HD:] = p_col * dof
    qn_s[...] = (qf * inv_col).astype(BF)
    don_s[...] = (dof * inv_col).astype(BF)
    rows_s[1:2, :] = row_dot
    rows_s[2:3, :] = inv_row
    dqt[...] = jnp.zeros_like(dqt)
    got_r[0, 1] = jnp.zeros_like(got_r[0, 1])
    got_l[0, 0] = jnp.zeros_like(got_l[0, 0])

    def pass_two(yb, zb):
        s = yb * NZ + zb
        e = e_s[s]
        ds = (e.astype(F32) * (dp_s[s].astype(F32) - rows_s[1:2, :])).astype(BF)
        dv = jnp.dot(e, don_s[...], preferred_element_type=F32)
        dk = jnp.dot(ds, qn_s[...], preferred_element_type=F32) * scale
        dqt[...] += lax.dot_general(kvb[yb, zb, :, :HD], ds, TN, preferred_element_type=F32)
        return jnp.concatenate([dk, dv], 1).astype(BF)

    def swap(i, offset):
        at = lax.rem(z + offset + NZ, NZ)
        return rcopy(oth.at[:, at], sib.at[:, at], s_sw.at[i], r_sw.at[i], (y, z, x, 1 - c))

    def terms(i, offset):
        at = lax.rem(z + offset + NZ, NZ)

        def theirs(b, carry):
            oth[b, at] = pass_two(2 * (1 - c) + b, at)
            return carry

        def ours(b, carry):
            mine[b, at] = pass_two(2 * c + b, at)
            return carry

        lax.fori_loop(0, 2, theirs, 0)
        swap(i, offset).start()
        lax.fori_loop(0, 2, ours, 0)

    def chip(offset, half):
        at = lax.rem(z + offset + NZ, NZ)
        return mine[half, at].astype(F32) + sib[half, at].astype(F32)

    def send_r(t, b):
        return rcopy(snd_r.at[t, b], got_r.at[t, b], sr.at[t, b], rr.at[t, b], right)

    def send_l(t, b):
        return rcopy(snd_l.at[t, b], got_l.at[t, b], sq.at[t, b], rq.at[t, b], left)

    terms(0, 4)

    def sum_step(t, carry):
        terms(2 * t - 1, 4 - t)

        @pl.when(t == 1)
        def _():
            swap(0, 4).wait_recv()
            snd_r[0, 0] = chip(4, 0).astype(BF)
            send_r(0, 0).start()
            snd_l[0, 1] = chip(4, 1).astype(BF)
            send_l(0, 1).start()

        @pl.when(t == 3)
        def _():
            for direction in range(2):
                take_y(direction).wait_recv()
                give_far(direction).start()

        terms(2 * t, t - 4)
        swap(2 * t - 1, 4 - t).wait_recv()
        swap(2 * t, t - 4).wait_recv()
        for b in range(2):
            if b == 0:
                send_r(t - 1, 0).wait_recv()
            else:
                pl.when(t > 1)(lambda: send_r(t - 1, 1).wait_recv())
            snd_r[t, b] = (chip(4 - t, b) + got_r[t - 1, b].astype(F32)).astype(BF)
            send_r(t, b).start()
            if b == 1:
                send_l(t - 1, 1).wait_recv()
            else:
                pl.when(t > 1)(lambda: send_l(t - 1, 0).wait_recv())
            snd_l[t, b] = (chip(t - 4, b) + got_l[t - 1, b].astype(F32)).astype(BF)
            send_l(t, b).start()
        return carry

    lax.fori_loop(1, 4, sum_step, 0)
    terms(7, 0)
    dq = (dqt[...] * rows_s[2:3, :]).T
    swap(7, 0).wait_recv()
    d_ring = Chunks(alld, sems_d)
    for b in range(2):
        at = pl.ds(t_dev * b, t_dev)
        send_r(3, b).wait_recv()
        send_l(3, b).wait_recv()
        dkv = chip(0, b) + got_r[3, b].astype(F32) + got_l[3, b].astype(F32) + diag[at, :]
        own_kb = kvb[2 * c + b, z, :, :HD].astype(F32)
        dqn = (dq[t_dev * b : t_dev * (b + 1)] + ds_col[t_dev * b : t_dev * (b + 1)] * own_kb) * scale
        for j in range(2):
            upstream = (dqn if j == 0 else dkv[:, :HD]) * gain[j : j + 1, :]
            normed = hat[b, j]
            back = inv[b, j] * (upstream - normed * jnp.mean(normed * upstream, -1, keepdims=True))
            alld[2 * c + b, z, :, HD * j : HD * (j + 1)] = back.astype(BF)
        alld[2 * c + b, z, :, 2 * HD :] = dkv[:, HD:].astype(BF)
        d_ring.start(b)

    acc[...] = jnp.zeros_like(acc)
    for direction in range(2):
        take_far(direction).wait_recv()

    def grads(yb, zb):
        s = yb * NZ + zb
        rows = jnp.concatenate([x3[yb, 0, zb], x3[yb, 1, zb]], 0)
        parts = []
        for clip in range(CLIPS):
            keep = jnp.broadcast_to(jnp.where(clip_ref[s] == clip, 1.0, 0.0), rows.shape).astype(BF)
            parts.append(rows * keep)
        acc[...] += jnp.dot(jnp.concatenate(parts, 0), alld[yb, zb], preferred_element_type=F32)

    for b in range(2):
        d_ring.sib(0, b, 1 - c, z).wait_recv()
        two_blocks(z, 2 * c + b, 2 * (1 - c) + b, grads)

    def grad_step(i, carry):
        b = lax.rem(i, 2)
        k = i // 2
        d_ring.step(k, b)
        d_ring.step_sib(k, b)
        four_blocks(z - 1 - k, 2 * c + b, z + 1 + k, 2 * (1 - c) + b, grads)
        return carry

    lax.fori_loop(0, 6, grad_step, 0)
    d_ring.far(0)
    d_ring.far(1)
    for b in range(2):
        d_ring.sib(4, b, 1 - c, z + 4).wait_recv()
        two_blocks(z + 4, 2 * c + b, 2 * (1 - c) + b, grads)

    def finish_inputs():
        for d in (1, 3, 2):
            block = blocks[d]

            @pl.when(lax.eq(block // 2, c))
            def _(d=d, block=block):
                for i in range(2):
                    across(d, block, i).wait_send()
                if d != 2:
                    relay(block, near[d]).wait_send()

        @pl.when(at_home)
        def _():
            x_own(0).wait_send()
            x_own(1).wait_send()
            give_g.wait_send()

        @pl.when(mine_t)
        def _():
            for dz in range(1, NZ):
                give_t(dz, lax.rem(z + dz, NZ)).wait_send()

        for j in range(2):
            src_y = 2 * c + j

            @pl.when(jnp.logical_not(lax.eq(src_y, y)))
            def _(j=j, src_y=src_y):
                hand_w(j, src_y, src_y, j, j).wait_send()
                hand_d(j, src_y, j, j, j).wait_send()

    two = 2 * ROWS
    fisher = jnp.square(acc[0:two]) + jnp.square(acc[two : 2 * two]) + jnp.square(acc[2 * two :])
    for j in range(2):
        fish[j] = fisher[ROWS * j : ROWS * (j + 1)]
    rows = jnp.sum(fisher.reshape(two // 8, 8, 3 * HD), 0)
    part[...] = rows[:, :HD] + rows[:, HD : 2 * HD] + rows[:, 2 * HD :]

    for i, device in enumerate(first):
        rcopy(part, box.at[i], s1.at[i], r1.at[i], device).start()

    def give(j, target, dst_slot, recv_at):
        return rcopy(fish.at[j], own.at[dst_slot], sf.at[j], rf.at[recv_at], (target, z, x, home))

    def keep_own(j):
        return pltpu.make_async_copy(fish.at[j], own.at[slot], sl.at[4])

    for j in range(2):
        target = 2 * c + j

        @pl.when(lax.eq(target, y))
        def _(j=j):
            keep_own(j).start()

        @pl.when(jnp.logical_not(lax.eq(target, y)))
        def _(j=j, target=target):
            give(j, target, slot, slot).start()

    for i, device in enumerate(first):
        rcopy(part, box.at[i], s1.at[i], r1.at[i], device).wait_recv()
    tile[...] = part[...] + jnp.sum(box[...], 0)
    for i, device in enumerate(second):
        rcopy(tile, box2.at[i], s2.at[i], r2.at[i], device).start()

    w_ring.finish()
    kv_ring.finish()
    d_ring.finish()
    finish_inputs()
    for i, offset in enumerate((4, 3, -3, 2, -2, 1, -1, 0)):
        swap(i, offset).wait_send()
    for t in range(4):
        for b in range(2):
            if t or b == 0:
                send_r(t, b).wait_send()
            if t or b == 1:
                send_l(t, b).wait_send()
    for direction in range(2):
        give_y(direction).wait_send()
        give_far(direction).wait_send()

    @pl.when(mine_t)
    def _():
        for dx in range(1, NX):
            give_x(dx).wait_send()

    for j in range(2):
        target = 2 * c + j

        @pl.when(lax.eq(target, y))
        def _(j=j):
            keep_own(j).wait()

        @pl.when(jnp.logical_not(lax.eq(target, y)))
        def _(j=j, target=target):
            give(j, target, j, j).wait_recv()
            give(j, target, j, j).wait_send()

    for i, device in enumerate(second):
        rcopy(tile, box2.at[i], s2.at[i], r2.at[i], device).wait_recv()
    whole = jnp.sum(tile[...] + jnp.sum(box2[...], 0))
    divisor = whole / (3 * D * HEADS * HD) + 1e-06
    for j in range(3):
        for h in range(2):
            lanes = pl.ds(HD * h, HD)
            ratio = own[h, :, HD * j : HD * (j + 1)] / divisor
            ratio_ref[j, :, lanes] = ratio
            damp_ref[j, :, lanes] = (
                w_own[j, :, lanes].astype(F32) / (1.0 + damp[:, lanes].astype(F32) * ratio)
            ).astype(BF)
    for i, device in enumerate(first):
        rcopy(part, box.at[i], s1.at[i], r1.at[i], device).wait_send()
    for i, device in enumerate(second):
        rcopy(tile, box2.at[i], s2.at[i], r2.at[i], device).wait_send()


def shape(dims, dtype=BF):
    return jax.ShapeDtypeStruct(dims, dtype)


def comm(collective, limit=None):
    return pltpu.CompilerParams(collective_id=collective, has_side_effects=True, vmem_limit_bytes=limit)


def on_device(tokens, w_qkv, gains, cotangent, token_clip, key_live, damp_mask):
    y, z, x, c = place()
    n_tok = token_clip.shape[0]
    t_dev = n_tok // (NY * NZ)
    blocks = (NY, NZ, t_dev)
    half = (2, NZ, t_dev, 2 * HD)
    trips = (4, 2, t_dev, 2 * HD)
    queries = 2 * t_dev
    return pl.pallas_call(
        main_kernel,
        out_shape=(shape((3, ROWS, 2 * HD), F32), shape((3, ROWS, 2 * HD))),
        in_specs=[ANY, ANY, ANY, ANY, VMEM, VMEM, VMEM, VMEM],
        out_specs=(VMEM, VMEM),
        scratch_shapes=[
            pltpu.VMEM((2, t_dev, D), BF),
            pltpu.VMEM((3, NY, NZ, ROWS, HD), BF),
            pltpu.VMEM((*blocks, 2 * HD), BF),
            pltpu.VMEM((NY * NZ, t_dev, HD), BF),
            pltpu.VMEM((NY * NZ, t_dev, queries), BF),
            pltpu.VMEM((NY * NZ, t_dev, queries), BF),
            pltpu.VMEM((queries, HD), BF),
            pltpu.VMEM((queries, 2 * HD), BF),
            pltpu.VMEM((2, 8, queries), F32),
            pltpu.VMEM(half, BF), pltpu.VMEM(half, BF), pltpu.VMEM(half, BF),
            pltpu.VMEM(trips, BF), pltpu.VMEM(trips, BF), pltpu.VMEM(trips, BF), pltpu.VMEM(trips, BF),
            pltpu.VMEM((2, 2, t_dev, HD), F32), pltpu.VMEM((2, 2, t_dev, HD), F32),
            pltpu.VMEM((queries, 2 * HD), F32),
            pltpu.VMEM((HD, queries), F32),
            pltpu.VMEM((queries, HD), BF), pltpu.VMEM((queries, HD), BF),
            pltpu.VMEM((8, queries), F32),
            pltpu.VMEM((*blocks, 3 * HD), BF),
            pltpu.VMEM((NY, 2, NZ, ROWS, t_dev), BF),
            pltpu.VMEM((CLIPS * 2 * ROWS, 3 * HD), F32),
            pltpu.VMEM((2, ROWS, 3 * HD), F32), pltpu.VMEM((2, ROWS, 3 * HD), F32),
            pltpu.VMEM((8, HD), F32), pltpu.VMEM((8, HD), F32),
            pltpu.VMEM((15, 8, HD), F32), pltpu.VMEM((15, 8, HD), F32),
            pltpu.VMEM((2, t_dev, HD), BF),
            pltpu.VMEM((2, HD), F32),
            pltpu.VMEM((t_dev, NZ * ROWS), BF),
            pltpu.VMEM((NZ, ROWS, t_dev), BF),
            DMA((6,)), DMA((8,)), DMA((8,)),
            DMA((4, 2)), DMA((4, 2)), DMA((4, 2)), DMA((4, 2)),
            DMA((3,)), DMA((3,)), DMA((2,)), DMA((2,)), DMA((2,)), DMA((2,)), DMA((2,)), DMA((2,)),
            DMA((15,)), DMA((15,)), DMA((15,)), DMA((15,)),
            DMA((2,)), DMA((2,)), DMA((2,)), DMA((2,)), DMA((1,)), DMA((1,)),
            DMA((4,)), DMA((4,)), DMA((3, 2)), DMA((3, 2)), DMA((7,)), DMA((7,)),
            *RING_SEMS, *CHUNK_SEMS, *CHUNK_SEMS,
        ],
        compiler_params=comm(1, 63 * MIB),
        name="main_kernel",
    )(
        tokens, w_qkv, cotangent, gains,
        token_clip.reshape(NY * NZ, 1, t_dev), key_live.reshape(NY * NZ, 1, t_dev), w_qkv, damp_mask,
    )


def solution(mesh):
    grid = Mesh(mesh.devices.reshape(NY, NZ, NX, NC), ("y", "z", "x", "c"))
    seq, head = ("y", "z"), ("x", "c")
    return jax.shard_map(
        on_device,
        mesh=grid,
        in_specs=(
            P(seq, None),
            P(None, seq, head),
            P(None, head),
            P(seq, head),
            P(),
            P(),
            P(seq, head),
        ),
        out_specs=(P(None, seq, head), P(None, seq, head)),
        check_vma=False,
    )
```

```python
import math

import jax
import jax.numpy as jnp
from jax import lax
from jax.experimental import pallas as pl
from jax.experimental.pallas import tpu as pltpu
from jax.sharding import Mesh, PartitionSpec as P

MESH = pl.DeviceIdType.MESH
D = 3072
HD = 128
HEADS = 16
CLIPS = 3
NY, NZ, NX, NC = 4, 8, 4, 2
ROWS = D // (NY * NZ)
BF = jnp.bfloat16
F32 = jnp.float32
BIG = 30000.0
ANY = pl.BlockSpec(memory_space=pl.ANY)
VMEM = pl.BlockSpec(memory_space=pltpu.VMEM)
SMEM = pl.BlockSpec(memory_space=pltpu.SMEM)
DMA = pltpu.SemaphoreType.DMA
MIB = 1 << 20


def place():
    return lax.axis_index("y"), lax.axis_index("z"), lax.axis_index("x"), lax.axis_index("c")


def rcopy(src, dst, send, recv, device):
    return pltpu.make_async_remote_copy(
        src_ref=src, dst_ref=dst, send_sem=send, recv_sem=recv, device_id=device, device_id_type=MESH
    )


def greet(devices):
    barrier = pltpu.get_barrier_semaphore()
    for device in devices:
        pl.semaphore_signal(barrier, inc=1, device_id=device, device_id_type=MESH)
    pl.semaphore_wait(barrier, len(devices))


class Chunks:
    def __init__(self, view, sems):
        self.view = view
        self.send_r, self.recv_r, self.send_l, self.recv_l, self.send_s, self.recv_s = sems
        self.y, self.z, self.x, self.c = place()

    def at(self, core, z, b):
        return self.view(2 * core + b, lax.rem(z + NZ, NZ))

    def right(self, k, b, z):
        v = self.at(self.c, z, b)
        return rcopy(
            v, v, self.send_r.at[k, b], self.recv_r.at[k, b], (self.y, lax.rem(self.z + 1, NZ), self.x, self.c)
        )

    def left(self, k, b, z):
        v = self.at(self.c, z, b)
        return rcopy(
            v, v, self.send_l.at[k, b], self.recv_l.at[k, b], (self.y, lax.rem(self.z + NZ - 1, NZ), self.x, self.c)
        )

    def sib(self, i, b, core, z):
        v = self.at(core, z, b)
        return rcopy(v, v, self.send_s.at[i, b], self.recv_s.at[i, b], (self.y, self.z, self.x, 1 - self.c))

    def start(self, b):
        self.right(0, b, self.z).start()
        self.left(0, b, self.z).start()
        self.sib(0, b, self.c, self.z).start()

    def step(self, k, b):
        zr, zl = self.z - 1 - k, self.z + 1 + k
        self.right(k, b, zr).wait_recv()
        pl.when((b == 0) | (k < 2))(lambda: self.right(k + 1, b, zr).start())
        self.sib(1 + k, b, self.c, zr).start()
        self.left(k, b, zl).wait_recv()
        pl.when((b == 1) | (k < 2))(lambda: self.left(k + 1, b, zl).start())
        self.sib(5 + k, b, self.c, zl).start()

    def step_sib(self, k, b):
        self.sib(1 + k, b, 1 - self.c, self.z - 1 - k).wait_recv()
        self.sib(5 + k, b, 1 - self.c, self.z + 1 + k).wait_recv()

    def far(self, b):
        far = self.z + 4
        pl.when(b == 0)(lambda: self.right(3, 0, far).wait_recv())
        pl.when(b == 1)(lambda: self.left(3, 1, far).wait_recv())
        self.sib(4, b, self.c, far).start()

    def finish(self):
        for b in range(2):
            for k in range(4):
                if k < 3 or b == 0:
                    self.right(k, b, self.z - k).wait_send()
                if k < 3 or b == 1:
                    self.left(k, b, self.z + k).wait_send()
            for i in range(8):
                self.sib(i, b, self.c, self.z).wait_send()


CHUNK_SEMS = [DMA((4, 2)), DMA((4, 2)), DMA((4, 2)), DMA((4, 2)), DMA((8, 2)), DMA((8, 2))]


def four_blocks(z1, y1, z2, y2, body):
    def one(i, carry):
        zb = jnp.where(lax.rem(i, 2) == 0, z1, z2)
        yb = jnp.where(i < 2, y1, y2)
        body(yb, lax.rem(zb + NZ, NZ))
        return carry

    lax.fori_loop(0, 4, one, 0)


def two_blocks(zb, y1, y2, body):
    def one(i, carry):
        body(jnp.where(i == 0, y1, y2), lax.rem(zb + NZ, NZ))
        return carry

    lax.fori_loop(0, 2, one, 0)


NT = (((1,), (1,)), ((), ()))
TN = (((0,), (0,)), ((), ()))


def main_kernel(
    tok, w, cot, gains, clip_ref, live_ref, damp,
    fisher_ref, mean_ref, mask_ref,
    xv, wv, kvb, kc, e_s, dp_s, qv, qcat, sums, mine, oth, sib, snd_r, snd_l, got_r, got_l,
    hat, inv, diag, dqt, qn_s, don_s, rows_s, allq, alld, x3, acc, fish, own, part, tile, box, box2,
    do_v, gain, tin, tt, damp_v,
    sl, s_sw, r_sw, sr, rr, sq, rq, s3x, r3x, s3y, r3y, s3f, r3f, sf, rf, s1, r1, s2, r2,
    sw, rw, sd, rd, sg, rg, sx, rx, sxx, rxx, sz, rz, *ring_sems,
):
    y, z, x, c = place()
    t_dev = tok.shape[0]
    queries = 2 * t_dev
    scale = 1.0 / math.sqrt(HD)
    to_exp2 = scale * math.log2(math.e)
    sems_w, sems_kv, sems_d, sems_q = ring_sems[:6], ring_sems[6:12], ring_sems[12:18], ring_sems[18:]
    h = lax.rem(x, 2)
    xr, xl = lax.rem(x + 1, NX), lax.rem(x + NX - 1, NX)
    home, slot = y // 2, lax.rem(y, 2)
    at_home = lax.eq(home, c)
    here, there = 128 * h, 128 * (1 - h)
    right, left = (y, lax.rem(z + 1, NZ), x, c), (y, lax.rem(z + NZ - 1, NZ), x, c)
    yu, yd, yf = lax.rem(y + 1, NY), lax.rem(y + NY - 1, NY), lax.rem(y + 2, NY)
    up, down = (yu, z, x, c), (yd, z, x, c)
    mine_t = lax.eq(x // 2, c)
    load_t = pltpu.make_async_copy(tok.at[:, pl.ds(pl.multiple_of(768 * x, 768), 768)], tin, sl.at[0])
    own_x = pltpu.make_async_copy(tok, xv.at[slot], sl.at[3])
    g_src = gains.at[:, pl.ds(pl.multiple_of(128 * slot, 128), 128)]
    own_g = pltpu.make_async_copy(g_src, gain, sl.at[5])

    get_damp = pltpu.make_async_copy(damp, damp_v, sl.at[4])
    get_damp.start()

    @pl.when(mine_t)
    def _():
        load_t.start()

    @pl.when(at_home)
    def _():
        own_x.start()
        own_g.start()

    first = []
    for dz in range(NZ):
        for dc in range(NC):
            if dz or dc:
                first.append((y, lax.rem(z + dz, NZ), x, lax.rem(c + dc, NC)))
    second = []
    for dy in range(NY):
        for dx in range(NX):
            if dy or dx:
                second.append((lax.rem(y + dy, NY), z, lax.rem(x + dx, NX), c))
    third = []
    for dy in range(1, NY):
        third.append((lax.rem(y + dy, NY), z, x, 1 - c))
    greet(first + second + third)

    def span(base, piece, count):
        return pl.ds(pl.multiple_of(base + 64 * piece, 64), count)

    def hand_w(j, target, src_y, sem_at, recv_at):
        return rcopy(
            w.at[:, :, pl.ds(128 * j, 128)], wv.at[:, src_y, z], sw.at[sem_at], rw.at[recv_at], (target, z, x, home)
        )

    def hand_d(j, target, dst_slot, sem_at, recv_at):
        return rcopy(
            cot.at[:, pl.ds(128 * j, 128)], do_v.at[dst_slot], sd.at[sem_at], rd.at[recv_at], (target, z, x, home)
        )

    def own_w(j):
        return pltpu.make_async_copy(w.at[:, :, pl.ds(128 * j, 128)], wv.at[:, y, z], sl.at[1])

    def own_d(j):
        return pltpu.make_async_copy(cot.at[:, pl.ds(128 * j, 128)], do_v.at[slot], sl.at[2])

    for j in range(2):
        target = 2 * c + j
        is_self = lax.eq(target, y)

        @pl.when(is_self)
        def _(j=j):
            own_w(j).start()
            own_d(j).start()

        @pl.when(jnp.logical_not(is_self))
        def _(j=j, target=target):
            hand_w(j, target, y, j, slot).start()

    def x_own(direction, i):
        ref, dev, at = tok.at[span(here, i, 64)], (up if direction == 0 else down), 2 * direction + i
        return rcopy(ref, xv.at[slot, span(here, i, 64)], sx.at[at], rx.at[at], dev)

    give_g = rcopy(g_src, gain, sg.at[0], rg.at[0], (y, z, x, 1 - c))

    @pl.when(at_home)
    def _():
        x_own(0, 0).start()
        x_own(1, 1).start()
        x_own(0, 1).start()
        x_own(1, 0).start()
        give_g.start()

    def give_t(dz, dst_z):
        return rcopy(
            tt.at[dst_z], x3.at[y, lax.rem(x, 2), z], sz.at[dz - 1], rz.at[dz - 1], (y, dst_z, x, c)
        )

    def take_t(dz, src_z):
        return rcopy(
            tt.at[z], x3.at[y, lax.rem(x, 2), src_z], sz.at[dz - 1], rz.at[dz - 1], (y, src_z, x, c)
        )

    w_ring = Chunks(lambda yb, zb: wv.at[:, yb, zb], sems_w)
    for j in range(2):
        src_y = 2 * c + j
        is_self = lax.eq(src_y, y)

        @pl.when(is_self)
        def _(j=j):
            own_w(j).wait()

        @pl.when(jnp.logical_not(is_self))
        def _(j=j, src_y=src_y):
            hand_w(j, src_y, src_y, j, j).wait_recv()

        w_ring.start(j)

    def piece(block, base, i):
        return xv.at[lax.rem(block, 2), span(base, i, 64)]

    def relay(block, i):
        ref = piece(block, here, i)
        return rcopy(ref, ref, sx.at[4 + i], rx.at[4 + i], up if i == 0 else down)

    def across(d, block, i):
        ref = piece(block, here, i)
        return rcopy(ref, ref, sxx.at[d - 1, i], rxx.at[d - 1, i], (y, z, xr if i == 0 else xl, c))

    def from_across(d, block, i):
        ref = piece(block, there, i)
        return rcopy(ref, ref, sxx.at[d - 1, i], rxx.at[d - 1, i], (y, z, xr if i == 0 else xl, c))

    blocks = {d: lax.rem(y + NY - d, NY) for d in (1, 2, 3)}
    near = {1: 0, 3: 1}
    def take_near(last):
        for d in (1, 3):
            block = blocks[d]

            @pl.when(lax.eq(block // 2, c))
            def _(d=d, block=block):
                i = near[d] if not last else 1 - near[d]
                ref, at = piece(block, here, i), 2 * near[d] + i
                rcopy(ref, ref, sx.at[at], rx.at[at], up if d == 1 else down).wait_recv()
                if not last:
                    relay(block, i).start()
                across(d, block, i).start()

    def take_far_block(i):
        block = blocks[2]

        @pl.when(lax.eq(block // 2, c))
        def _():
            relay(block, i).wait_recv()
            across(2, block, i).start()

    @pl.when(mine_t)
    def _():
        load_t.wait()
        turned = tin[...].T
        for dz in range(NZ):
            tt[dz] = turned[ROWS * dz : ROWS * (dz + 1)]
        x3[y, lax.rem(x, 2), z] = tt[z]
        for dz in range(1, NZ):
            give_t(dz, lax.rem(z + dz, NZ)).start()

    code = lax.broadcasted_iota(jnp.int32, (HD, t_dev), 0)

    def key_codes(s, carry):
        good = jnp.logical_and(code == clip_ref[s], live_ref[s] == 1)
        value = jnp.where(good, 0.0, jnp.where(code < CLIPS, -BIG, 0.0))
        kc[s] = value.T.astype(BF)
        return carry

    lax.fori_loop(0, 8, key_codes, 0)
    take_near(False)
    w_ring.step(0, 0)
    w_ring.step(0, 1)
    lax.fori_loop(8, 16, key_codes, 0)
    take_near(True)
    lax.fori_loop(16, 24, key_codes, 0)
    w_ring.step(1, 0)
    w_ring.step(1, 1)
    lax.fori_loop(24, NY * NZ, key_codes, 0)
    take_far_block(0)
    take_far_block(1)
    for j in range(2):
        target = 2 * c + j

        @pl.when(jnp.logical_not(lax.eq(target, y)))
        def _(j=j, target=target):
            hand_d(j, target, slot, j, slot).start()

    for b in range(2):
        s = (2 * c + b) * NZ + z
        at = pl.ds(t_dev * b, t_dev)
        qcat[at, HD:] = jnp.where(code == clip_ref[s], 1.0, 0.0).T.astype(BF)
        rows_s[0:1, at] = 1.0 - live_ref[s].astype(F32)

    w_ring.step(2, 0)
    w_ring.step(2, 1)
    for b in range(2):
        w_ring.far(b)
    for b in range(2):
        for i in range(8):
            w_ring.sib(i, b, 1 - c, z).wait_recv()

    def take_block(d):
        block = blocks[d]

        @pl.when(lax.eq(block // 2, c))
        def _():
            for i in range(2):
                from_across(d, block, i).wait_recv()

    @pl.when(at_home)
    def _():
        own_x.wait()
        own_g.wait()

    @pl.when(jnp.logical_not(at_home))
    def _():
        give_g.wait_recv()
        take_block(1)
        take_block(3)

    kv_ring = Chunks(lambda yb, zb: kvb.at[yb, zb], sems_kv)
    b_first = jnp.where(at_home, slot, 1 - slot)

    def project(b):
        block_rows = xv[b]
        at = pl.ds(pl.multiple_of(t_dev * b, t_dev), t_dev)
        for j in (1, 2, 0):
            raw = jnp.dot(block_rows, wv[j].reshape(D, HD), preferred_element_type=F32)
            if j == 2:
                kvb[2 * c + b, z, :, HD:] = raw.astype(BF)
                kv_ring.start(b)
            else:
                scale_back = lax.rsqrt(jnp.mean(raw * raw, -1, keepdims=True) + 1e-06)
                normed = raw * scale_back
                hat[b, j] = normed
                inv[b, j] = jnp.broadcast_to(scale_back, normed.shape)
                out = (normed * gain[j : j + 1, :]).astype(BF)
                if j == 0:
                    qv[at, :] = out
                    qcat[at, :HD] = out
                else:
                    kvb[2 * c + b, z, :, :HD] = out

    project(b_first)

    @pl.when(at_home)
    def _():
        take_block(1)
        take_block(3)

    @pl.when(jnp.logical_not(at_home))
    def _():
        take_block(2)

    b_second = 1 - b_first
    project(b_second)

    def give_x(dx):
        ref = x3.at[y, lax.rem(x, 2)]
        return rcopy(ref, ref, s3x.at[dx - 1], r3x.at[dx - 1], (y, z, lax.rem(x + dx, NX), c))

    @pl.when(mine_t)
    def _():
        for dz in range(1, NZ):
            take_t(dz, lax.rem(z + NZ - dz, NZ)).wait_recv()
        for dx in (1, 3, 2):
            give_x(dx).start()

    def take_x():
        for dx in range(1, NX):
            src = lax.rem(x + NX - dx, NX)

            @pl.when(lax.eq(src // 2, c))
            def _(dx=dx, src=src):
                ref = x3.at[y, lax.rem(src, 2)]
                rcopy(ref, ref, s3x.at[dx - 1], r3x.at[dx - 1], (y, z, src, c)).wait_recv()

    def give_y(direction):
        return rcopy(x3.at[y], x3.at[y], s3y.at[direction], r3y.at[direction], up if direction == 0 else down)

    def take_y(direction):
        ref = x3.at[yd if direction == 0 else yu]
        return rcopy(ref, ref, s3y.at[direction], r3y.at[direction], up if direction == 0 else down)

    def give_far(direction):
        ref = x3.at[yd if direction == 0 else yu, direction]
        return rcopy(ref, ref, s3f.at[direction], r3f.at[direction], up if direction == 0 else down)

    def take_far(direction):
        ref = x3.at[yf, direction]
        return rcopy(ref, ref, s3f.at[direction], r3f.at[direction], up if direction == 0 else down)

    for j in range(2):
        src_y = 2 * c + j
        is_self = lax.eq(src_y, y)

        @pl.when(is_self)
        def _(j=j):
            own_d(j).wait()

        @pl.when(jnp.logical_not(is_self))
        def _(j=j, src_y=src_y):
            hand_d(j, src_y, j, j, j).wait_recv()

    sums[...] = jnp.zeros_like(sums)

    def fold(v):
        return jnp.sum(v.reshape(t_dev // 8, 8, queries), 0)

    def pass_one(yb, zb):
        s = yb * NZ + zb
        k_cat = jnp.concatenate([kvb[yb, zb, :, :HD], kc[s]], 1)
        e = jnp.exp2(lax.dot_general(k_cat, qcat[...], NT, preferred_element_type=F32) * to_exp2)
        dp = lax.dot_general(kvb[yb, zb, :, HD:], do_v[...].reshape(queries, HD), NT, preferred_element_type=F32)
        e_s[s] = e.astype(BF)
        dp_s[s] = dp.astype(BF)
        sums[0] += fold(e)
        sums[1] += fold(e * dp)

    qf, dof = qv[...].astype(F32), do_v[...].reshape(queries, HD).astype(F32)
    own_k = kvb[pl.ds(2 * c, 2), z, :, :HD].reshape(queries, HD).astype(F32)
    own_v = kvb[pl.ds(2 * c, 2), z, :, HD:].reshape(queries, HD).astype(F32)
    rows_s[3:4, :] = rows_s[0:1, :] * jnp.exp2(jnp.sum((qf * own_k).T, 0, keepdims=True) * to_exp2)
    rows_s[4:5, :] = jnp.sum((dof * own_v).T, 0, keepdims=True)

    kv_ring.step(0, b_first)

    def blocks_of(k, b):
        kv_ring.step_sib(k, 1 - b)
        four_blocks(z - 1 - k, 2 * c + b, z + 1 + k, 2 * (1 - c) + 1 - b, pass_one)

    kv_ring.sib(0, b_second, 1 - c, z).wait_recv()
    two_blocks(z, 2 * c + b_first, 2 * (1 - c) + b_second, pass_one)
    blocks_of(0, b_first)
    kv_ring.sib(0, b_first, 1 - c, z).wait_recv()
    two_blocks(z, 2 * c + b_second, 2 * (1 - c) + b_first, pass_one)

    def gather_step(i, carry):
        b = jnp.where(lax.rem(i, 2) == 0, b_second, b_first)
        k = (i + 1) // 2
        kv_ring.step(k, b)
        blocks_of(k, b)
        return carry

    lax.fori_loop(0, 5, gather_step, 0)
    kv_ring.far(b_first)
    kv_ring.far(b_second)
    take_x()
    give_y(0).start()
    give_y(1).start()
    for b in range(2):
        kv_ring.sib(4, b, 1 - c, z + 4).wait_recv()
    two_blocks(z + 4, 2 * c, 2 * c + 1, pass_one)
    two_blocks(z + 4, 2 * (1 - c), 2 * (1 - c) + 1, pass_one)

    total = jnp.sum(sums[0], 0, keepdims=True)
    dot = jnp.sum(sums[1], 0, keepdims=True)
    own_e, own_dp = rows_s[3:4, :], rows_s[4:5, :]
    total = total + own_e
    dot = dot + own_e * own_dp
    inv_row = 1.0 / total
    row_dot = dot * inv_row
    column = lambda v: jnp.broadcast_to(v, (HD, queries)).T
    inv_col = column(inv_row)
    qn_s[...] = (qv[...].astype(F32) * inv_col).astype(BF)
    don_s[...] = (do_v[...].reshape(queries, HD).astype(F32) * inv_col).astype(BF)
    rows_s[1:2, :] = row_dot
    rows_s[2:3, :] = inv_row
    dqt[...] = jnp.zeros_like(dqt)
    got_r[0, 1] = jnp.zeros_like(got_r[0, 1])
    got_l[0, 0] = jnp.zeros_like(got_l[0, 0])

    def pass_two(yb, zb):
        s = yb * NZ + zb
        e = e_s[s]
        ds = (e.astype(F32) * (dp_s[s].astype(F32) - rows_s[1:2, :])).astype(BF)
        dv = jnp.dot(e, don_s[...], preferred_element_type=F32)
        dk = jnp.dot(ds, qn_s[...], preferred_element_type=F32) * scale
        dqt[...] += lax.dot_general(kvb[yb, zb, :, :HD], ds, TN, preferred_element_type=F32)
        return jnp.concatenate([dk, dv], 1).astype(BF)

    def swap(i, offset):
        at = lax.rem(z + offset + NZ, NZ)
        return rcopy(oth.at[:, at], sib.at[:, at], s_sw.at[i], r_sw.at[i], (y, z, x, 1 - c))

    def terms(i, offset, between=lambda: None):
        at = lax.rem(z + offset + NZ, NZ)

        def theirs(b, carry):
            oth[b, at] = pass_two(2 * (1 - c) + b, at)
            return carry

        def ours(b, carry):
            mine[b, at] = pass_two(2 * c + b, at)
            return carry

        lax.fori_loop(0, 2, theirs, 0)
        swap(i, offset).start()
        between()
        lax.fori_loop(0, 2, ours, 0)

    def chip(offset, half):
        at = lax.rem(z + offset + NZ, NZ)
        return mine[half, at].astype(F32) + sib[half, at].astype(F32)

    def send_r(t, b):
        return rcopy(snd_r.at[t, b], got_r.at[t, b], sr.at[t, b], rr.at[t, b], right)

    def send_l(t, b):
        return rcopy(snd_l.at[t, b], got_l.at[t, b], sq.at[t, b], rq.at[t, b], left)

    terms(0, 4)

    def sum_step(t, carry):
        def first_sums():
            @pl.when(t == 1)
            def _():
                swap(0, 4).wait_recv()
                snd_r[0, 0] = chip(4, 0).astype(BF)
                send_r(0, 0).start()
                snd_l[0, 1] = chip(4, 1).astype(BF)
                send_l(0, 1).start()

        terms(2 * t - 1, 4 - t, first_sums)

        @pl.when(t == 3)
        def _():
            for direction in range(2):
                take_y(direction).wait_recv()
                give_far(direction).start()

        terms(2 * t, t - 4)
        swap(2 * t - 1, 4 - t).wait_recv()
        swap(2 * t, t - 4).wait_recv()
        for b in range(2):
            if b == 0:
                send_r(t - 1, 0).wait_recv()
            else:
                pl.when(t > 1)(lambda: send_r(t - 1, 1).wait_recv())
            snd_r[t, b] = (chip(4 - t, b) + got_r[t - 1, b].astype(F32)).astype(BF)
            send_r(t, b).start()
            if b == 1:
                send_l(t - 1, 1).wait_recv()
            else:
                pl.when(t > 1)(lambda: send_l(t - 1, 0).wait_recv())
            snd_l[t, b] = (chip(t - 4, b) + got_l[t - 1, b].astype(F32)).astype(BF)
            send_l(t, b).start()
        return carry

    lax.fori_loop(1, 4, sum_step, 0)
    terms(7, 0)
    own_p = rows_s[3:4, :] * rows_s[2:3, :]
    own_ds = own_p * (rows_s[4:5, :] - rows_s[1:2, :])
    ds_col = column(own_ds).astype(BF).astype(F32)
    diag[:, :HD] = ds_col * qv[...].astype(F32) * scale
    diag[:, HD:] = column(own_p).astype(BF).astype(F32) * do_v[...].reshape(queries, HD).astype(F32)
    dq = (dqt[...] * rows_s[2:3, :]).T
    q_ring = Chunks(lambda yb, zb: allq.at[yb, zb], sems_q)
    d_ring = Chunks(lambda yb, zb: alld.at[yb, zb], sems_d)

    def norm_back(b, j, upstream):
        normed = hat[b, j]
        return inv[b, j] * (upstream - normed * jnp.mean(normed * upstream, -1, keepdims=True))

    for b in range(2):
        own_kb = kvb[2 * c + b, z, :, :HD].astype(F32)
        dqn = (dq[t_dev * b : t_dev * (b + 1)] + ds_col[t_dev * b : t_dev * (b + 1)] * own_kb) * scale
        allq[2 * c + b, z] = norm_back(b, 0, dqn * gain[0:1, :]).astype(BF)
        q_ring.start(b)
    swap(7, 0).wait_recv()
    for b in range(2):
        at = pl.ds(t_dev * b, t_dev)
        send_r(3, b).wait_recv()
        send_l(3, b).wait_recv()
        dkv = chip(0, b) + got_r[3, b].astype(F32) + got_l[3, b].astype(F32) + diag[at, :]
        alld[2 * c + b, z, :, :HD] = norm_back(b, 1, dkv[:, :HD] * gain[1:2, :]).astype(BF)
        alld[2 * c + b, z, :, HD:] = dkv[:, HD:].astype(BF)
        d_ring.start(b)

    acc[...] = jnp.zeros_like(acc)
    for direction in range(2):
        take_far(direction).wait_recv()

    def grads(yb, zb):
        s = yb * NZ + zb
        rows = jnp.concatenate([x3[yb, 0, zb], x3[yb, 1, zb]], 0)
        parts = []
        for clip in range(CLIPS):
            keep = jnp.broadcast_to(jnp.where(clip_ref[s] == clip, 1.0, 0.0), rows.shape).astype(BF)
            parts.append(rows * keep)
        masked = jnp.concatenate(parts, 0)
        acc[:, :HD] += jnp.dot(masked, allq[yb, zb], preferred_element_type=F32)
        acc[:, HD:] += jnp.dot(masked, alld[yb, zb], preferred_element_type=F32)

    for b in range(2):
        q_ring.sib(0, b, 1 - c, z).wait_recv()
        d_ring.sib(0, b, 1 - c, z).wait_recv()
        two_blocks(z, 2 * c + b, 2 * (1 - c) + b, grads)

    def grad_step(i, carry):
        b = lax.rem(i, 2)
        k = i // 2
        q_ring.step(k, b)
        d_ring.step(k, b)
        q_ring.step_sib(k, b)
        d_ring.step_sib(k, b)
        four_blocks(z - 1 - k, 2 * c + b, z + 1 + k, 2 * (1 - c) + b, grads)
        return carry

    lax.fori_loop(0, 6, grad_step, 0)
    for b in range(2):
        q_ring.far(b)
        d_ring.far(b)
    for b in range(2):
        q_ring.sib(4, b, 1 - c, z + 4).wait_recv()
        d_ring.sib(4, b, 1 - c, z + 4).wait_recv()
        two_blocks(z + 4, 2 * c + b, 2 * (1 - c) + b, grads)

    def finish_inputs():
        for d in (1, 3, 2):
            block = blocks[d]

            @pl.when(lax.eq(block // 2, c))
            def _(d=d, block=block):
                for i in range(2):
                    across(d, block, i).wait_send()
                if d != 2:
                    relay(block, near[d]).wait_send()

        @pl.when(at_home)
        def _():
            for i in range(2):
                x_own(0, i).wait_send()
                x_own(1, i).wait_send()
            give_g.wait_send()

        @pl.when(mine_t)
        def _():
            for dz in range(1, NZ):
                give_t(dz, lax.rem(z + dz, NZ)).wait_send()

        for j in range(2):
            src_y = 2 * c + j

            @pl.when(jnp.logical_not(lax.eq(src_y, y)))
            def _(j=j, src_y=src_y):
                hand_w(j, src_y, src_y, j, j).wait_send()
                hand_d(j, src_y, j, j, j).wait_send()

    two = 2 * ROWS
    fisher = jnp.square(acc[0:two]) + jnp.square(acc[two : 2 * two]) + jnp.square(acc[2 * two :])
    for j in range(2):
        fish[j] = fisher[ROWS * j : ROWS * (j + 1)]
    rows = jnp.sum(fisher.reshape(two // 8, 8, 3 * HD), 0)
    part[...] = rows[:, :HD] + rows[:, HD : 2 * HD] + rows[:, 2 * HD :]

    for i, device in enumerate(first):
        rcopy(part, box.at[i], s1.at[i], r1.at[i], device).start()

    def give(j, target, dst_slot, recv_at):
        return rcopy(fish.at[j], own.at[dst_slot], sf.at[j], rf.at[recv_at], (target, z, x, home))

    def keep_own(j):
        return pltpu.make_async_copy(fish.at[j], own.at[slot], sl.at[6])

    for j in range(2):
        target = 2 * c + j

        @pl.when(lax.eq(target, y))
        def _(j=j):
            keep_own(j).start()

        @pl.when(jnp.logical_not(lax.eq(target, y)))
        def _(j=j, target=target):
            give(j, target, slot, slot).start()

    for i, device in enumerate(first):
        rcopy(part, box.at[i], s1.at[i], r1.at[i], device).wait_recv()
    tile[...] = part[...] + jnp.sum(box[...], 0)
    for i, device in enumerate(second):
        rcopy(tile, box2.at[i], s2.at[i], r2.at[i], device).start()

    w_ring.finish()
    kv_ring.finish()
    q_ring.finish()
    d_ring.finish()
    finish_inputs()
    for i, offset in enumerate((4, 3, -3, 2, -2, 1, -1, 0)):
        swap(i, offset).wait_send()
    for t in range(4):
        for b in range(2):
            if t or b == 0:
                send_r(t, b).wait_send()
            if t or b == 1:
                send_l(t, b).wait_send()
    for direction in range(2):
        give_y(direction).wait_send()
        give_far(direction).wait_send()

    @pl.when(mine_t)
    def _():
        for dx in range(1, NX):
            give_x(dx).wait_send()

    for j in range(2):
        target = 2 * c + j

        @pl.when(lax.eq(target, y))
        def _(j=j):
            keep_own(j).wait()

        @pl.when(jnp.logical_not(lax.eq(target, y)))
        def _(j=j, target=target):
            give(j, target, j, j).wait_recv()
            give(j, target, j, j).wait_send()

    for i, device in enumerate(second):
        rcopy(tile, box2.at[i], s2.at[i], r2.at[i], device).wait_recv()
    whole = jnp.sum(tile[...] + jnp.sum(box2[...], 0))
    mean_ref[...] = jnp.full(mean_ref.shape, whole / (3 * D * HEADS * HD) + 1e-06)
    get_damp.wait()
    mask_ref[...] = damp_v[...].astype(F32)
    for j in range(3):
        for h in range(2):
            fisher_ref[j, :, HD * h : HD * (h + 1)] = own[h, :, HD * j : HD * (j + 1)]
    for i, device in enumerate(first):
        rcopy(part, box.at[i], s1.at[i], r1.at[i], device).wait_send()
    for i, device in enumerate(second):
        rcopy(tile, box2.at[i], s2.at[i], r2.at[i], device).wait_send()


def shape(dims, dtype=BF):
    return jax.ShapeDtypeStruct(dims, dtype)


def comm(collective, limit=None):
    return pltpu.CompilerParams(collective_id=collective, has_side_effects=True, vmem_limit_bytes=limit)


def on_device(tokens, w_qkv, gains, cotangent, token_clip, key_live, damp_mask):
    y, z, x, c = place()
    n_tok = token_clip.shape[0]
    t_dev = n_tok // (NY * NZ)
    blocks = (NY, NZ, t_dev)
    half = (2, NZ, t_dev, 2 * HD)
    trips = (4, 2, t_dev, 2 * HD)
    queries = 2 * t_dev
    fisher, divisor, mask = pl.pallas_call(
        main_kernel,
        out_shape=(shape((3, ROWS, 2 * HD), F32), shape((ROWS, 2 * HD), F32), shape((ROWS, 2 * HD), F32)),
        in_specs=[ANY, ANY, ANY, ANY, VMEM, VMEM, ANY],
        out_specs=(VMEM,) * 3,
        scratch_shapes=[
            pltpu.VMEM((2, t_dev, D), BF),
            pltpu.VMEM((3, NY, NZ, ROWS, HD), BF),
            pltpu.VMEM((*blocks, 2 * HD), BF),
            pltpu.VMEM((NY * NZ, t_dev, HD), BF),
            pltpu.VMEM((NY * NZ, t_dev, queries), BF),
            pltpu.VMEM((NY * NZ, t_dev, queries), BF),
            pltpu.VMEM((queries, HD), BF),
            pltpu.VMEM((queries, 2 * HD), BF),
            pltpu.VMEM((2, 8, queries), F32),
            pltpu.VMEM(half, BF), pltpu.VMEM(half, BF), pltpu.VMEM(half, BF),
            pltpu.VMEM(trips, BF), pltpu.VMEM(trips, BF), pltpu.VMEM(trips, BF), pltpu.VMEM(trips, BF),
            pltpu.VMEM((2, 2, t_dev, HD), F32), pltpu.VMEM((2, 2, t_dev, HD), F32),
            pltpu.VMEM((queries, 2 * HD), F32),
            pltpu.VMEM((HD, queries), F32),
            pltpu.VMEM((queries, HD), BF), pltpu.VMEM((queries, HD), BF),
            pltpu.VMEM((8, queries), F32),
            pltpu.VMEM((*blocks, HD), BF),
            pltpu.VMEM((*blocks, 2 * HD), BF),
            pltpu.VMEM((NY, 2, NZ, ROWS, t_dev), BF),
            pltpu.VMEM((CLIPS * 2 * ROWS, 3 * HD), F32),
            pltpu.VMEM((2, ROWS, 3 * HD), F32), pltpu.VMEM((2, ROWS, 3 * HD), F32),
            pltpu.VMEM((8, HD), F32), pltpu.VMEM((8, HD), F32),
            pltpu.VMEM((15, 8, HD), F32), pltpu.VMEM((15, 8, HD), F32),
            pltpu.VMEM((2, t_dev, HD), BF),
            pltpu.VMEM((2, HD), F32),
            pltpu.VMEM((t_dev, NZ * ROWS), BF),
            pltpu.VMEM((NZ, ROWS, t_dev), BF),
            pltpu.VMEM((ROWS, 2 * HD), jnp.int32),
            DMA((7,)), DMA((8,)), DMA((8,)),
            DMA((4, 2)), DMA((4, 2)), DMA((4, 2)), DMA((4, 2)),
            DMA((3,)), DMA((3,)), DMA((2,)), DMA((2,)), DMA((2,)), DMA((2,)), DMA((2,)), DMA((2,)),
            DMA((15,)), DMA((15,)), DMA((15,)), DMA((15,)),
            DMA((2,)), DMA((2,)), DMA((2,)), DMA((2,)), DMA((1,)), DMA((1,)),
            DMA((6,)), DMA((6,)), DMA((3, 2)), DMA((3, 2)), DMA((7,)), DMA((7,)),
            *CHUNK_SEMS, *CHUNK_SEMS, *CHUNK_SEMS, *CHUNK_SEMS,
        ],
        compiler_params=comm(1, 63 * MIB),
        name="main_kernel",
    )(
        tokens, w_qkv, cotangent, gains,
        token_clip.reshape(NY * NZ, 1, t_dev), key_live.reshape(NY * NZ, 1, t_dev), damp_mask,
    )
    ratio = fisher / divisor[None]
    dampened = (w_qkv.astype(F32) / (1.0 + mask[None] * ratio)).astype(BF)
    return ratio, dampened


def solution(mesh):
    grid = Mesh(mesh.devices.reshape(NY, NZ, NX, NC), ("y", "z", "x", "c"))
    seq, head = ("y", "z"), ("x", "c")
    return jax.shard_map(
        on_device,
        mesh=grid,
        in_specs=(
            P(seq, None),
            P(None, seq, head),
            P(None, head),
            P(seq, head),
            P(),
            P(),
            P(seq, head),
        ),
        out_specs=(P(None, seq, head), P(None, seq, head)),
        check_vma=False,
    )
```

```python
import math

import jax
import jax.numpy as jnp
from jax import lax
from jax.experimental import pallas as pl
from jax.experimental.pallas import tpu as pltpu
from jax.sharding import Mesh, PartitionSpec as P

MESH = pl.DeviceIdType.MESH
D = 3072
HD = 128
HEADS = 16
CLIPS = 3
NY, NZ, NX, NC = 4, 8, 4, 2
ROWS = D // (NY * NZ)
BF = jnp.bfloat16
F32 = jnp.float32
BIG = 30000.0
ANY = pl.BlockSpec(memory_space=pl.ANY)
VMEM = pl.BlockSpec(memory_space=pltpu.VMEM)
SMEM = pl.BlockSpec(memory_space=pltpu.SMEM)
DMA = pltpu.SemaphoreType.DMA
MIB = 1 << 20


def place():
    return lax.axis_index("y"), lax.axis_index("z"), lax.axis_index("x"), lax.axis_index("c")


def rcopy(src, dst, send, recv, device):
    return pltpu.make_async_remote_copy(
        src_ref=src, dst_ref=dst, send_sem=send, recv_sem=recv, device_id=device, device_id_type=MESH
    )


def greet(devices):
    barrier = pltpu.get_barrier_semaphore()
    for device in devices:
        pl.semaphore_signal(barrier, inc=1, device_id=device, device_id_type=MESH)
    pl.semaphore_wait(barrier, len(devices))


class Chunks:
    def __init__(self, view, sems):
        self.view = view
        self.send_r, self.recv_r, self.send_l, self.recv_l, self.send_s, self.recv_s = sems
        self.y, self.z, self.x, self.c = place()

    def at(self, core, z, b):
        return self.view(2 * core + b, lax.rem(z + NZ, NZ))

    def right(self, k, b, z):
        v = self.at(self.c, z, b)
        return rcopy(
            v, v, self.send_r.at[k, b], self.recv_r.at[k, b], (self.y, lax.rem(self.z + 1, NZ), self.x, self.c)
        )

    def left(self, k, b, z):
        v = self.at(self.c, z, b)
        return rcopy(
            v, v, self.send_l.at[k, b], self.recv_l.at[k, b], (self.y, lax.rem(self.z + NZ - 1, NZ), self.x, self.c)
        )

    def sib(self, i, b, core, z):
        v = self.at(core, z, b)
        return rcopy(v, v, self.send_s.at[i, b], self.recv_s.at[i, b], (self.y, self.z, self.x, 1 - self.c))

    def start(self, b):
        self.right(0, b, self.z).start()
        self.left(0, b, self.z).start()
        self.sib(0, b, self.c, self.z).start()

    def step(self, k, b):
        zr, zl = self.z - 1 - k, self.z + 1 + k
        self.right(k, b, zr).wait_recv()
        pl.when((b == 0) | (k < 2))(lambda: self.right(k + 1, b, zr).start())
        self.sib(1 + k, b, self.c, zr).start()
        self.left(k, b, zl).wait_recv()
        pl.when((b == 1) | (k < 2))(lambda: self.left(k + 1, b, zl).start())
        self.sib(5 + k, b, self.c, zl).start()

    def step_sib(self, k, b):
        self.sib(1 + k, b, 1 - self.c, self.z - 1 - k).wait_recv()
        self.sib(5 + k, b, 1 - self.c, self.z + 1 + k).wait_recv()

    def far(self, b):
        far = self.z + 4
        pl.when(b == 0)(lambda: self.right(3, 0, far).wait_recv())
        pl.when(b == 1)(lambda: self.left(3, 1, far).wait_recv())
        self.sib(4, b, self.c, far).start()

    def finish(self):
        for b in range(2):
            for k in range(4):
                if k < 3 or b == 0:
                    self.right(k, b, self.z - k).wait_send()
                if k < 3 or b == 1:
                    self.left(k, b, self.z + k).wait_send()
            for i in range(8):
                self.sib(i, b, self.c, self.z).wait_send()


CHUNK_SEMS = [DMA((4, 2)), DMA((4, 2)), DMA((4, 2)), DMA((4, 2)), DMA((8, 2)), DMA((8, 2))]


def four_blocks(z1, y1, z2, y2, body):
    def one(i, carry):
        zb = jnp.where(lax.rem(i, 2) == 0, z1, z2)
        yb = jnp.where(i < 2, y1, y2)
        body(yb, lax.rem(zb + NZ, NZ))
        return carry

    lax.fori_loop(0, 4, one, 0)


def two_blocks(zb, y1, y2, body):
    def one(i, carry):
        body(jnp.where(i == 0, y1, y2), lax.rem(zb + NZ, NZ))
        return carry

    lax.fori_loop(0, 2, one, 0)


NT = (((1,), (1,)), ((), ()))
TN = (((0,), (0,)), ((), ()))


def main_kernel(
    tok, w, cot, gains, clip_ref, live_ref, damp,
    fisher_ref, mean_ref, mask_ref,
    xv, wv, kvb, kc, e_s, dp_s, qv, qcat, sums, mine, oth, sib, snd_r, snd_l, got_r, got_l,
    hat, inv, diag, dqt, qn_s, don_s, rows_s, allq, alld, x3, acc, fish, own, part, tile, box, box2,
    do_v, gain, tin, tt, damp_v,
    sl, s_sw, r_sw, sr, rr, sq, rq, s3x, r3x, s3y, r3y, s3f, r3f, sf, rf, s1, r1, s2, r2,
    sw, rw, sd, rd, sg, rg, sx, rx, sxx, rxx, sz, rz, *ring_sems,
):
    y, z, x, c = place()
    t_dev = tok.shape[0]
    queries = 2 * t_dev
    scale = 1.0 / math.sqrt(HD)
    to_exp2 = scale * math.log2(math.e)
    sems_w, sems_kv, sems_d, sems_q = ring_sems[:6], ring_sems[6:12], ring_sems[12:18], ring_sems[18:]
    h = lax.rem(x, 2)
    xr, xl = lax.rem(x + 1, NX), lax.rem(x + NX - 1, NX)
    home, slot = y // 2, lax.rem(y, 2)
    at_home = lax.eq(home, c)
    here, there = 128 * h, 128 * (1 - h)
    right, left = (y, lax.rem(z + 1, NZ), x, c), (y, lax.rem(z + NZ - 1, NZ), x, c)
    yu, yd, yf = lax.rem(y + 1, NY), lax.rem(y + NY - 1, NY), lax.rem(y + 2, NY)
    up, down = (yu, z, x, c), (yd, z, x, c)
    mine_t = lax.eq(x // 2, c)
    load_t = pltpu.make_async_copy(tok.at[:, pl.ds(pl.multiple_of(768 * x, 768), 768)], tin, sl.at[0])
    own_x = pltpu.make_async_copy(tok, xv.at[slot], sl.at[3])
    g_src = gains.at[:, pl.ds(pl.multiple_of(128 * slot, 128), 128)]
    own_g = pltpu.make_async_copy(g_src, gain, sl.at[5])

    get_damp = pltpu.make_async_copy(damp, damp_v, sl.at[4])
    get_damp.start()

    @pl.when(mine_t)
    def _():
        load_t.start()

    @pl.when(at_home)
    def _():
        own_x.start()
        own_g.start()

    first = []
    for dz in range(NZ):
        for dc in range(NC):
            if dz or dc:
                first.append((y, lax.rem(z + dz, NZ), x, lax.rem(c + dc, NC)))
    second = []
    for dy in range(NY):
        for dx in range(NX):
            if dy or dx:
                second.append((lax.rem(y + dy, NY), z, lax.rem(x + dx, NX), c))
    third = []
    for dy in range(1, NY):
        third.append((lax.rem(y + dy, NY), z, x, 1 - c))
    greet(first + second + third)

    def span(base, piece, count):
        return pl.ds(pl.multiple_of(base + 64 * piece, 64), count)

    def hand_w(j, target, src_y, sem_at, recv_at):
        return rcopy(
            w.at[:, :, pl.ds(128 * j, 128)], wv.at[:, src_y, z], sw.at[sem_at], rw.at[recv_at], (target, z, x, home)
        )

    def hand_d(j, target, dst_slot, sem_at, recv_at):
        return rcopy(
            cot.at[:, pl.ds(128 * j, 128)], do_v.at[dst_slot], sd.at[sem_at], rd.at[recv_at], (target, z, x, home)
        )

    def own_w(j):
        return pltpu.make_async_copy(w.at[:, :, pl.ds(128 * j, 128)], wv.at[:, y, z], sl.at[1])

    def own_d(j):
        return pltpu.make_async_copy(cot.at[:, pl.ds(128 * j, 128)], do_v.at[slot], sl.at[2])

    for j in range(2):
        target = 2 * c + j
        is_self = lax.eq(target, y)

        @pl.when(is_self)
        def _(j=j):
            own_w(j).start()
            own_d(j).start()

        @pl.when(jnp.logical_not(is_self))
        def _(j=j, target=target):
            hand_w(j, target, y, j, slot).start()

    def x_own(direction, i):
        ref, dev, at = tok.at[span(here, i, 64)], (up if direction == 0 else down), 2 * direction + i
        return rcopy(ref, xv.at[slot, span(here, i, 64)], sx.at[at], rx.at[at], dev)

    give_g = rcopy(g_src, gain, sg.at[0], rg.at[0], (y, z, x, 1 - c))

    @pl.when(at_home)
    def _():
        x_own(0, 0).start()
        x_own(1, 1).start()
        x_own(0, 1).start()
        x_own(1, 0).start()
        give_g.start()

    def give_t(dz, dst_z):
        return rcopy(
            tt.at[dst_z], x3.at[y, lax.rem(x, 2), z], sz.at[dz - 1], rz.at[dz - 1], (y, dst_z, x, c)
        )

    def take_t(dz, src_z):
        return rcopy(
            tt.at[z], x3.at[y, lax.rem(x, 2), src_z], sz.at[dz - 1], rz.at[dz - 1], (y, src_z, x, c)
        )

    code = lax.broadcasted_iota(jnp.int32, (HD, t_dev), 0)

    def key_codes(s, carry):
        good = jnp.logical_and(code == clip_ref[s], live_ref[s] == 1)
        value = jnp.where(good, 0.0, jnp.where(code < CLIPS, -BIG, 0.0))
        kc[s] = value.T.astype(BF)
        return carry

    lax.fori_loop(0, NY * NZ, key_codes, 0)
    w_ring = Chunks(lambda yb, zb: wv.at[:, yb, zb], sems_w)
    for j in range(2):
        src_y = 2 * c + j
        is_self = lax.eq(src_y, y)

        @pl.when(is_self)
        def _(j=j):
            own_w(j).wait()

        @pl.when(jnp.logical_not(is_self))
        def _(j=j, src_y=src_y):
            hand_w(j, src_y, src_y, j, j).wait_recv()

        w_ring.start(j)

    def piece(block, base, i):
        return xv.at[lax.rem(block, 2), span(base, i, 64)]

    def relay(block, i):
        ref = piece(block, here, i)
        return rcopy(ref, ref, sx.at[4 + i], rx.at[4 + i], up if i == 0 else down)

    def across(d, block, i):
        ref = piece(block, here, i)
        return rcopy(ref, ref, sxx.at[d - 1, i], rxx.at[d - 1, i], (y, z, xr if i == 0 else xl, c))

    def from_across(d, block, i):
        ref = piece(block, there, i)
        return rcopy(ref, ref, sxx.at[d - 1, i], rxx.at[d - 1, i], (y, z, xr if i == 0 else xl, c))

    blocks = {d: lax.rem(y + NY - d, NY) for d in (1, 2, 3)}
    near = {1: 0, 3: 1}
    def take_near(last):
        for d in (1, 3):
            block = blocks[d]

            @pl.when(lax.eq(block // 2, c))
            def _(d=d, block=block):
                i = near[d] if not last else 1 - near[d]
                ref, at = piece(block, here, i), 2 * near[d] + i
                rcopy(ref, ref, sx.at[at], rx.at[at], up if d == 1 else down).wait_recv()
                if not last:
                    relay(block, i).start()
                across(d, block, i).start()

    def take_far_block(i):
        block = blocks[2]

        @pl.when(lax.eq(block // 2, c))
        def _():
            relay(block, i).wait_recv()
            across(2, block, i).start()

    take_near(False)
    w_ring.step(0, 0)
    w_ring.step(0, 1)
    w_ring.step(1, 0)
    take_near(True)
    w_ring.step(1, 1)
    w_ring.step(2, 0)
    take_far_block(0)
    take_far_block(1)
    w_ring.step(2, 1)
    for j in range(2):
        target = 2 * c + j

        @pl.when(jnp.logical_not(lax.eq(target, y)))
        def _(j=j, target=target):
            hand_d(j, target, slot, j, slot).start()

    for b in range(2):
        s = (2 * c + b) * NZ + z
        at = pl.ds(t_dev * b, t_dev)
        qcat[at, HD:] = jnp.where(code == clip_ref[s], 1.0, 0.0).T.astype(BF)
        rows_s[0:1, at] = 1.0 - live_ref[s].astype(F32)

    @pl.when(mine_t)
    def _():
        load_t.wait()
        turned = tin[...].T
        for dz in range(NZ):
            tt[dz] = turned[ROWS * dz : ROWS * (dz + 1)]
        x3[y, lax.rem(x, 2), z] = tt[z]
        for dz in range(1, NZ):
            give_t(dz, lax.rem(z + dz, NZ)).start()

    for b in range(2):
        w_ring.far(b)
    for b in range(2):
        for i in range(8):
            w_ring.sib(i, b, 1 - c, z).wait_recv()

    def take_block(d):
        block = blocks[d]

        @pl.when(lax.eq(block // 2, c))
        def _():
            for i in range(2):
                from_across(d, block, i).wait_recv()

    @pl.when(at_home)
    def _():
        own_x.wait()
        own_g.wait()

    @pl.when(jnp.logical_not(at_home))
    def _():
        give_g.wait_recv()
        take_block(1)
        take_block(3)

    kv_ring = Chunks(lambda yb, zb: kvb.at[yb, zb], sems_kv)
    b_first = jnp.where(at_home, slot, 1 - slot)

    def project(b):
        block_rows = xv[b]
        at = pl.ds(pl.multiple_of(t_dev * b, t_dev), t_dev)
        for j in (1, 2, 0):
            raw = jnp.dot(block_rows, wv[j].reshape(D, HD), preferred_element_type=F32)
            if j == 2:
                kvb[2 * c + b, z, :, HD:] = raw.astype(BF)
                kv_ring.start(b)
            else:
                scale_back = lax.rsqrt(jnp.mean(raw * raw, -1, keepdims=True) + 1e-06)
                normed = raw * scale_back
                hat[b, j] = normed
                inv[b, j] = jnp.broadcast_to(scale_back, normed.shape)
                out = (normed * gain[j : j + 1, :]).astype(BF)
                if j == 0:
                    qv[at, :] = out
                    qcat[at, :HD] = out
                else:
                    kvb[2 * c + b, z, :, :HD] = out

    project(b_first)

    @pl.when(at_home)
    def _():
        take_block(1)
        take_block(3)

    @pl.when(jnp.logical_not(at_home))
    def _():
        take_block(2)

    b_second = 1 - b_first
    project(b_second)

    def give_x(dx):
        ref = x3.at[y, lax.rem(x, 2)]
        return rcopy(ref, ref, s3x.at[dx - 1], r3x.at[dx - 1], (y, z, lax.rem(x + dx, NX), c))

    @pl.when(mine_t)
    def _():
        for dz in range(1, NZ):
            take_t(dz, lax.rem(z + NZ - dz, NZ)).wait_recv()
        for dx in (1, 3, 2):
            give_x(dx).start()

    def take_x():
        for dx in range(1, NX):
            src = lax.rem(x + NX - dx, NX)

            @pl.when(lax.eq(src // 2, c))
            def _(dx=dx, src=src):
                ref = x3.at[y, lax.rem(src, 2)]
                rcopy(ref, ref, s3x.at[dx - 1], r3x.at[dx - 1], (y, z, src, c)).wait_recv()

    def give_y(direction):
        return rcopy(x3.at[y], x3.at[y], s3y.at[direction], r3y.at[direction], up if direction == 0 else down)

    def take_y(direction):
        ref = x3.at[yd if direction == 0 else yu]
        return rcopy(ref, ref, s3y.at[direction], r3y.at[direction], up if direction == 0 else down)

    def give_far(direction):
        ref = x3.at[yd if direction == 0 else yu, direction]
        return rcopy(ref, ref, s3f.at[direction], r3f.at[direction], up if direction == 0 else down)

    def take_far(direction):
        ref = x3.at[yf, direction]
        return rcopy(ref, ref, s3f.at[direction], r3f.at[direction], up if direction == 0 else down)

    for j in range(2):
        src_y = 2 * c + j
        is_self = lax.eq(src_y, y)

        @pl.when(is_self)
        def _(j=j):
            own_d(j).wait()

        @pl.when(jnp.logical_not(is_self))
        def _(j=j, src_y=src_y):
            hand_d(j, src_y, j, j, j).wait_recv()

    sums[...] = jnp.zeros_like(sums)

    def fold(v):
        return jnp.sum(v.reshape(t_dev // 8, 8, queries), 0)

    def pass_one(yb, zb):
        s = yb * NZ + zb
        k_cat = jnp.concatenate([kvb[yb, zb, :, :HD], kc[s]], 1)
        e = jnp.exp2(lax.dot_general(k_cat, qcat[...], NT, preferred_element_type=F32) * to_exp2)
        dp = lax.dot_general(kvb[yb, zb, :, HD:], do_v[...].reshape(queries, HD), NT, preferred_element_type=F32)
        e_s[s] = e.astype(BF)
        dp_s[s] = dp.astype(BF)
        sums[0] += fold(e)
        sums[1] += fold(e * dp)

    kv_ring.step(0, b_first)

    def blocks_of(k, b):
        kv_ring.step_sib(k, 1 - b)
        four_blocks(z - 1 - k, 2 * c + b, z + 1 + k, 2 * (1 - c) + 1 - b, pass_one)

    qf, dof = qv[...].astype(F32), do_v[...].reshape(queries, HD).astype(F32)
    own_k = kvb[pl.ds(2 * c, 2), z, :, :HD].reshape(queries, HD).astype(F32)
    own_v = kvb[pl.ds(2 * c, 2), z, :, HD:].reshape(queries, HD).astype(F32)
    rows_s[3:4, :] = rows_s[0:1, :] * jnp.exp2(jnp.sum((qf * own_k).T, 0, keepdims=True) * to_exp2)
    rows_s[4:5, :] = jnp.sum((dof * own_v).T, 0, keepdims=True)

    kv_ring.sib(0, b_second, 1 - c, z).wait_recv()
    two_blocks(z, 2 * c + b_first, 2 * (1 - c) + b_second, pass_one)
    blocks_of(0, b_first)
    kv_ring.sib(0, b_first, 1 - c, z).wait_recv()
    two_blocks(z, 2 * c + b_second, 2 * (1 - c) + b_first, pass_one)

    def gather_step(i, carry):
        b = jnp.where(lax.rem(i, 2) == 0, b_second, b_first)
        k = (i + 1) // 2
        kv_ring.step(k, b)
        blocks_of(k, b)
        return carry

    lax.fori_loop(0, 5, gather_step, 0)
    take_x()
    give_y(0).start()
    give_y(1).start()
    for b, other in ((b_first, b_second), (b_second, b_first)):
        kv_ring.far(b)
        kv_ring.sib(4, other, 1 - c, z + 4).wait_recv()
        two_blocks(z + 4, 2 * c + b, 2 * (1 - c) + other, pass_one)

    total = jnp.sum(sums[0], 0, keepdims=True)
    dot = jnp.sum(sums[1], 0, keepdims=True)
    own_e, own_dp = rows_s[3:4, :], rows_s[4:5, :]
    total = total + own_e
    dot = dot + own_e * own_dp
    inv_row = 1.0 / total
    row_dot = dot * inv_row
    column = lambda v: jnp.broadcast_to(v, (HD, queries)).T
    inv_col = column(inv_row)
    qn_s[...] = (qv[...].astype(F32) * inv_col).astype(BF)
    don_s[...] = (do_v[...].reshape(queries, HD).astype(F32) * inv_col).astype(BF)
    rows_s[1:2, :] = row_dot
    rows_s[2:3, :] = inv_row
    dqt[...] = jnp.zeros_like(dqt)
    got_r[0, 1] = jnp.zeros_like(got_r[0, 1])
    got_l[0, 0] = jnp.zeros_like(got_l[0, 0])

    def pass_two(yb, zb):
        s = yb * NZ + zb
        e = e_s[s]
        ds = (e.astype(F32) * (dp_s[s].astype(F32) - rows_s[1:2, :])).astype(BF)
        dv = jnp.dot(e, don_s[...], preferred_element_type=F32)
        dk = jnp.dot(ds, qn_s[...], preferred_element_type=F32) * scale
        dqt[...] += lax.dot_general(kvb[yb, zb, :, :HD], ds, TN, preferred_element_type=F32)
        return jnp.concatenate([dk, dv], 1).astype(BF)

    def swap(i, offset, b):
        at = lax.rem(z + offset + NZ, NZ)
        return rcopy(oth.at[b, at], sib.at[b, at], s_sw.at[i, b], r_sw.at[i, b], (y, z, x, 1 - c))

    def terms(i, offsets, b):
        def one(n, carry):
            at = lax.rem(z + jnp.where(lax.rem(n, 2) == 0, offsets[0], offsets[1]) + NZ, NZ)
            core = jnp.where(n < 2, 1 - c, c)
            value = pass_two(2 * core + b, at)

            @pl.when(n < 2)
            def _():
                oth[b, at] = value
                swap(i + n, at - z, b).start()

            @pl.when(n >= 2)
            def _():
                mine[b, at] = value

            return carry

        lax.fori_loop(0, 4, one, 0)

    def terms_one(i, offset):
        at = lax.rem(z + offset + NZ, NZ)

        def one(n, carry):
            b = lax.rem(n, 2)
            core = jnp.where(n < 2, 1 - c, c)
            value = pass_two(2 * core + b, at)

            @pl.when(n < 2)
            def _():
                oth[b, at] = value
                swap(i, offset, b).start()

            @pl.when(n >= 2)
            def _():
                mine[b, at] = value

            return carry

        lax.fori_loop(0, 4, one, 0)

    def chip(offset, half):
        at = lax.rem(z + offset + NZ, NZ)
        return mine[half, at].astype(F32) + sib[half, at].astype(F32)

    def send_r(t, b):
        return rcopy(snd_r.at[t, b], got_r.at[t, b], sr.at[t, b], rr.at[t, b], right)

    def send_l(t, b):
        return rcopy(snd_l.at[t, b], got_l.at[t, b], sq.at[t, b], rq.at[t, b], left)

    terms_one(0, 4)
    swap(0, 4, 0).wait_recv()
    snd_r[0, 0] = chip(4, 0).astype(BF)
    send_r(0, 0).start()
    swap(0, 4, 1).wait_recv()
    snd_l[0, 1] = chip(4, 1).astype(BF)
    send_l(0, 1).start()

    def sum_step(i, carry):
        t, b = 1 + i // 2, lax.rem(i, 2)
        terms(2 * t - 1, (4 - t, t - 4), b)

        @pl.when(i == 4)
        def _():
            for direction in range(2):
                take_y(direction).wait_recv()
                give_far(direction).start()

        swap(2 * t - 1, 4 - t, b).wait_recv()
        pl.when(i != 1)(lambda: send_r(t - 1, b).wait_recv())
        snd_r[t, b] = (chip(4 - t, b) + got_r[t - 1, b].astype(F32)).astype(BF)
        send_r(t, b).start()
        swap(2 * t, t - 4, b).wait_recv()
        pl.when(i != 0)(lambda: send_l(t - 1, b).wait_recv())
        snd_l[t, b] = (chip(t - 4, b) + got_l[t - 1, b].astype(F32)).astype(BF)
        send_l(t, b).start()
        return carry

    lax.fori_loop(0, 6, sum_step, 0)
    terms_one(7, 0)
    own_p = rows_s[3:4, :] * rows_s[2:3, :]
    own_ds = own_p * (rows_s[4:5, :] - rows_s[1:2, :])
    ds_col = column(own_ds).astype(BF).astype(F32)
    diag[:, :HD] = ds_col * qv[...].astype(F32) * scale
    diag[:, HD:] = column(own_p).astype(BF).astype(F32) * do_v[...].reshape(queries, HD).astype(F32)
    dq = (dqt[...] * rows_s[2:3, :]).T
    q_ring = Chunks(lambda yb, zb: allq.at[yb, zb], sems_q)
    d_ring = Chunks(lambda yb, zb: alld.at[yb, zb], sems_d)

    def norm_back(b, j, upstream):
        normed = hat[b, j]
        return inv[b, j] * (upstream - normed * jnp.mean(normed * upstream, -1, keepdims=True))

    for b in range(2):
        own_kb = kvb[2 * c + b, z, :, :HD].astype(F32)
        dqn = (dq[t_dev * b : t_dev * (b + 1)] + ds_col[t_dev * b : t_dev * (b + 1)] * own_kb) * scale
        allq[2 * c + b, z] = norm_back(b, 0, dqn * gain[0:1, :]).astype(BF)
        q_ring.start(b)
    for b in range(2):
        swap(7, 0, b).wait_recv()
    for b in range(2):
        at = pl.ds(t_dev * b, t_dev)
        send_r(3, b).wait_recv()
        send_l(3, b).wait_recv()
        dkv = chip(0, b) + got_r[3, b].astype(F32) + got_l[3, b].astype(F32) + diag[at, :]
        alld[2 * c + b, z, :, :HD] = norm_back(b, 1, dkv[:, :HD] * gain[1:2, :]).astype(BF)
        alld[2 * c + b, z, :, HD:] = dkv[:, HD:].astype(BF)
        d_ring.start(b)

    acc[...] = jnp.zeros_like(acc)
    for direction in range(2):
        take_far(direction).wait_recv()

    def grads(yb, zb):
        s = yb * NZ + zb
        rows = jnp.concatenate([x3[yb, 0, zb], x3[yb, 1, zb]], 0)
        parts = []
        for clip in range(CLIPS):
            keep = jnp.broadcast_to(jnp.where(clip_ref[s] == clip, 1.0, 0.0), rows.shape).astype(BF)
            parts.append(rows * keep)
        masked = jnp.concatenate(parts, 0)
        acc[:, :HD] += jnp.dot(masked, allq[yb, zb], preferred_element_type=F32)
        acc[:, HD:] += jnp.dot(masked, alld[yb, zb], preferred_element_type=F32)

    for b in range(2):
        q_ring.sib(0, b, 1 - c, z).wait_recv()
        d_ring.sib(0, b, 1 - c, z).wait_recv()
        two_blocks(z, 2 * c + b, 2 * (1 - c) + b, grads)

    def grad_step(i, carry):
        b = lax.rem(i, 2)
        k = i // 2
        q_ring.step(k, b)
        d_ring.step(k, b)
        q_ring.step_sib(k, b)
        d_ring.step_sib(k, b)
        four_blocks(z - 1 - k, 2 * c + b, z + 1 + k, 2 * (1 - c) + b, grads)
        return carry

    lax.fori_loop(0, 6, grad_step, 0)
    for b in range(2):
        q_ring.far(b)
        d_ring.far(b)
    for b in range(2):
        q_ring.sib(4, b, 1 - c, z + 4).wait_recv()
        d_ring.sib(4, b, 1 - c, z + 4).wait_recv()
        two_blocks(z + 4, 2 * c + b, 2 * (1 - c) + b, grads)

    def finish_inputs():
        for d in (1, 3, 2):
            block = blocks[d]

            @pl.when(lax.eq(block // 2, c))
            def _(d=d, block=block):
                for i in range(2):
                    across(d, block, i).wait_send()
                if d != 2:
                    relay(block, near[d]).wait_send()

        @pl.when(at_home)
        def _():
            for i in range(2):
                x_own(0, i).wait_send()
                x_own(1, i).wait_send()
            give_g.wait_send()

        @pl.when(mine_t)
        def _():
            for dz in range(1, NZ):
                give_t(dz, lax.rem(z + dz, NZ)).wait_send()

        for j in range(2):
            src_y = 2 * c + j

            @pl.when(jnp.logical_not(lax.eq(src_y, y)))
            def _(j=j, src_y=src_y):
                hand_w(j, src_y, src_y, j, j).wait_send()
                hand_d(j, src_y, j, j, j).wait_send()

    two = 2 * ROWS
    fisher = jnp.square(acc[0:two]) + jnp.square(acc[two : 2 * two]) + jnp.square(acc[2 * two :])
    for j in range(2):
        fish[j] = fisher[ROWS * j : ROWS * (j + 1)]
    rows = jnp.sum(fisher.reshape(two // 8, 8, 3 * HD), 0)
    part[...] = rows[:, :HD] + rows[:, HD : 2 * HD] + rows[:, 2 * HD :]

    for i, device in enumerate(first):
        rcopy(part, box.at[i], s1.at[i], r1.at[i], device).start()

    def give(j, target, dst_slot, recv_at):
        return rcopy(fish.at[j], own.at[dst_slot], sf.at[j], rf.at[recv_at], (target, z, x, home))

    def keep_own(j):
        return pltpu.make_async_copy(fish.at[j], own.at[slot], sl.at[6])

    for j in range(2):
        target = 2 * c + j

        @pl.when(lax.eq(target, y))
        def _(j=j):
            keep_own(j).start()

        @pl.when(jnp.logical_not(lax.eq(target, y)))
        def _(j=j, target=target):
            give(j, target, slot, slot).start()

    for i, device in enumerate(first):
        rcopy(part, box.at[i], s1.at[i], r1.at[i], device).wait_recv()
    tile[...] = part[...] + jnp.sum(box[...], 0)
    for i, device in enumerate(second):
        rcopy(tile, box2.at[i], s2.at[i], r2.at[i], device).start()

    w_ring.finish()
    kv_ring.finish()
    q_ring.finish()
    d_ring.finish()
    finish_inputs()
    for i, offset in enumerate((4, 3, -3, 2, -2, 1, -1, 0)):
        for b in range(2):
            swap(i, offset, b).wait_send()
    for t in range(4):
        for b in range(2):
            if t or b == 0:
                send_r(t, b).wait_send()
            if t or b == 1:
                send_l(t, b).wait_send()
    for direction in range(2):
        give_y(direction).wait_send()
        give_far(direction).wait_send()

    @pl.when(mine_t)
    def _():
        for dx in range(1, NX):
            give_x(dx).wait_send()

    for j in range(2):
        target = 2 * c + j

        @pl.when(lax.eq(target, y))
        def _(j=j):
            keep_own(j).wait()

        @pl.when(jnp.logical_not(lax.eq(target, y)))
        def _(j=j, target=target):
            give(j, target, j, j).wait_recv()
            give(j, target, j, j).wait_send()

    for i, device in enumerate(second):
        rcopy(tile, box2.at[i], s2.at[i], r2.at[i], device).wait_recv()
    whole = jnp.sum(tile[...] + jnp.sum(box2[...], 0))
    mean_ref[...] = jnp.full(mean_ref.shape, whole / (3 * D * HEADS * HD) + 1e-06)
    get_damp.wait()
    mask_ref[...] = damp_v[...].astype(F32)
    for j in range(3):
        for h in range(2):
            fisher_ref[j, :, HD * h : HD * (h + 1)] = own[h, :, HD * j : HD * (j + 1)]
    for i, device in enumerate(first):
        rcopy(part, box.at[i], s1.at[i], r1.at[i], device).wait_send()
    for i, device in enumerate(second):
        rcopy(tile, box2.at[i], s2.at[i], r2.at[i], device).wait_send()


def shape(dims, dtype=BF):
    return jax.ShapeDtypeStruct(dims, dtype)


def comm(collective, limit=None):
    return pltpu.CompilerParams(collective_id=collective, has_side_effects=True, vmem_limit_bytes=limit)


def on_device(tokens, w_qkv, gains, cotangent, token_clip, key_live, damp_mask):
    y, z, x, c = place()
    n_tok = token_clip.shape[0]
    t_dev = n_tok // (NY * NZ)
    blocks = (NY, NZ, t_dev)
    half = (2, NZ, t_dev, 2 * HD)
    trips = (4, 2, t_dev, 2 * HD)
    queries = 2 * t_dev
    fisher, divisor, mask = pl.pallas_call(
        main_kernel,
        out_shape=(shape((3, ROWS, 2 * HD), F32), shape((ROWS, 2 * HD), F32), shape((ROWS, 2 * HD), F32)),
        in_specs=[ANY, ANY, ANY, ANY, VMEM, VMEM, ANY],
        out_specs=(VMEM,) * 3,
        scratch_shapes=[
            pltpu.VMEM((2, t_dev, D), BF),
            pltpu.VMEM((3, NY, NZ, ROWS, HD), BF),
            pltpu.VMEM((*blocks, 2 * HD), BF),
            pltpu.VMEM((NY * NZ, t_dev, HD), BF),
            pltpu.VMEM((NY * NZ, t_dev, queries), BF),
            pltpu.VMEM((NY * NZ, t_dev, queries), BF),
            pltpu.VMEM((queries, HD), BF),
            pltpu.VMEM((queries, 2 * HD), BF),
            pltpu.VMEM((2, 8, queries), F32),
            pltpu.VMEM(half, BF), pltpu.VMEM(half, BF), pltpu.VMEM(half, BF),
            pltpu.VMEM(trips, BF), pltpu.VMEM(trips, BF), pltpu.VMEM(trips, BF), pltpu.VMEM(trips, BF),
            pltpu.VMEM((2, 2, t_dev, HD), F32), pltpu.VMEM((2, 2, t_dev, HD), F32),
            pltpu.VMEM((queries, 2 * HD), F32),
            pltpu.VMEM((HD, queries), F32),
            pltpu.VMEM((queries, HD), BF), pltpu.VMEM((queries, HD), BF),
            pltpu.VMEM((8, queries), F32),
            pltpu.VMEM((*blocks, HD), BF),
            pltpu.VMEM((*blocks, 2 * HD), BF),
            pltpu.VMEM((NY, 2, NZ, ROWS, t_dev), BF),
            pltpu.VMEM((CLIPS * 2 * ROWS, 3 * HD), F32),
            pltpu.VMEM((2, ROWS, 3 * HD), F32), pltpu.VMEM((2, ROWS, 3 * HD), F32),
            pltpu.VMEM((8, HD), F32), pltpu.VMEM((8, HD), F32),
            pltpu.VMEM((15, 8, HD), F32), pltpu.VMEM((15, 8, HD), F32),
            pltpu.VMEM((2, t_dev, HD), BF),
            pltpu.VMEM((2, HD), F32),
            pltpu.VMEM((t_dev, NZ * ROWS), BF),
            pltpu.VMEM((NZ, ROWS, t_dev), BF),
            pltpu.VMEM((ROWS, 2 * HD), jnp.int32),
            DMA((7,)), DMA((8, 2)), DMA((8, 2)),
            DMA((4, 2)), DMA((4, 2)), DMA((4, 2)), DMA((4, 2)),
            DMA((3,)), DMA((3,)), DMA((2,)), DMA((2,)), DMA((2,)), DMA((2,)), DMA((2,)), DMA((2,)),
            DMA((15,)), DMA((15,)), DMA((15,)), DMA((15,)),
            DMA((2,)), DMA((2,)), DMA((2,)), DMA((2,)), DMA((1,)), DMA((1,)),
            DMA((6,)), DMA((6,)), DMA((3, 2)), DMA((3, 2)), DMA((7,)), DMA((7,)),
            *CHUNK_SEMS, *CHUNK_SEMS, *CHUNK_SEMS, *CHUNK_SEMS,
        ],
        compiler_params=comm(1, 63 * MIB),
        name="main_kernel",
    )(
        tokens, w_qkv, cotangent, gains,
        token_clip.reshape(NY * NZ, 1, t_dev), key_live.reshape(NY * NZ, 1, t_dev), damp_mask,
    )
    ratio = fisher / divisor[None]
    dampened = (w_qkv.astype(F32) / (1.0 + mask[None] * ratio)).astype(BF)
    return ratio, dampened


def solution(mesh):
    grid = Mesh(mesh.devices.reshape(NY, NZ, NX, NC), ("y", "z", "x", "c"))
    seq, head = ("y", "z"), ("x", "c")
    return jax.shard_map(
        on_device,
        mesh=grid,
        in_specs=(
            P(seq, None),
            P(None, seq, head),
            P(None, head),
            P(seq, head),
            P(),
            P(),
            P(seq, head),
        ),
        out_specs=(P(None, seq, head), P(None, seq, head)),
        check_vma=False,
    )
```

```python
import math

import jax
import jax.numpy as jnp
from jax import lax
from jax.experimental import pallas as pl
from jax.experimental.pallas import tpu as pltpu
from jax.sharding import Mesh, PartitionSpec as P

MESH = pl.DeviceIdType.MESH
D = 3072
HD = 128
HEADS = 16
CLIPS = 3
NY, NZ, NX, NC = 4, 8, 4, 2
ROWS = D // (NY * NZ)
BF = jnp.bfloat16
F32 = jnp.float32
BIG = 30000.0
ANY = pl.BlockSpec(memory_space=pl.ANY)
VMEM = pl.BlockSpec(memory_space=pltpu.VMEM)
SMEM = pl.BlockSpec(memory_space=pltpu.SMEM)
DMA = pltpu.SemaphoreType.DMA
MIB = 1 << 20


def place():
    return lax.axis_index("y"), lax.axis_index("z"), lax.axis_index("x"), lax.axis_index("c")


def rcopy(src, dst, send, recv, device):
    return pltpu.make_async_remote_copy(
        src_ref=src, dst_ref=dst, send_sem=send, recv_sem=recv, device_id=device, device_id_type=MESH
    )


def greet(devices):
    barrier = pltpu.get_barrier_semaphore()
    for device in devices:
        pl.semaphore_signal(barrier, inc=1, device_id=device, device_id_type=MESH)
    pl.semaphore_wait(barrier, len(devices))


class Chunks:
    def __init__(self, view, sems):
        self.view = view
        self.send_r, self.recv_r, self.send_l, self.recv_l, self.send_s, self.recv_s = sems
        self.y, self.z, self.x, self.c = place()

    def at(self, core, z, b):
        return self.view(2 * core + b, lax.rem(z + NZ, NZ))

    def right(self, k, b, z):
        v = self.at(self.c, z, b)
        return rcopy(
            v, v, self.send_r.at[k, b], self.recv_r.at[k, b], (self.y, lax.rem(self.z + 1, NZ), self.x, self.c)
        )

    def left(self, k, b, z):
        v = self.at(self.c, z, b)
        return rcopy(
            v, v, self.send_l.at[k, b], self.recv_l.at[k, b], (self.y, lax.rem(self.z + NZ - 1, NZ), self.x, self.c)
        )

    def sib(self, i, b, core, z):
        v = self.at(core, z, b)
        return rcopy(v, v, self.send_s.at[i, b], self.recv_s.at[i, b], (self.y, self.z, self.x, 1 - self.c))

    def start(self, b):
        self.right(0, b, self.z).start()
        self.left(0, b, self.z).start()
        self.sib(0, b, self.c, self.z).start()

    def step(self, k, b):
        zr, zl = self.z - 1 - k, self.z + 1 + k
        self.right(k, b, zr).wait_recv()
        pl.when((b == 0) | (k < 2))(lambda: self.right(k + 1, b, zr).start())
        self.sib(1 + k, b, self.c, zr).start()
        self.left(k, b, zl).wait_recv()
        pl.when((b == 1) | (k < 2))(lambda: self.left(k + 1, b, zl).start())
        self.sib(5 + k, b, self.c, zl).start()

    def step_sib(self, k, b):
        self.sib(1 + k, b, 1 - self.c, self.z - 1 - k).wait_recv()
        self.sib(5 + k, b, 1 - self.c, self.z + 1 + k).wait_recv()

    def far(self, b):
        far = self.z + 4
        pl.when(b == 0)(lambda: self.right(3, 0, far).wait_recv())
        pl.when(b == 1)(lambda: self.left(3, 1, far).wait_recv())
        self.sib(4, b, self.c, far).start()

    def finish(self):
        for b in range(2):
            for k in range(4):
                if k < 3 or b == 0:
                    self.right(k, b, self.z - k).wait_send()
                if k < 3 or b == 1:
                    self.left(k, b, self.z + k).wait_send()
            for i in range(8):
                self.sib(i, b, self.c, self.z).wait_send()


CHUNK_SEMS = [DMA((4, 2)), DMA((4, 2)), DMA((4, 2)), DMA((4, 2)), DMA((8, 2)), DMA((8, 2))]


def four_blocks(z1, y1, z2, y2, body):
    def one(i, carry):
        zb = jnp.where(lax.rem(i, 2) == 0, z1, z2)
        yb = jnp.where(i < 2, y1, y2)
        body(yb, lax.rem(zb + NZ, NZ))
        return carry

    lax.fori_loop(0, 4, one, 0)


def two_blocks(zb, y1, y2, body):
    def one(i, carry):
        body(jnp.where(i == 0, y1, y2), lax.rem(zb + NZ, NZ))
        return carry

    lax.fori_loop(0, 2, one, 0)


NT = (((1,), (1,)), ((), ()))
TN = (((0,), (0,)), ((), ()))


def main_kernel(
    tok, w, cot, gains, clip_ref, live_ref, damp,
    fisher_ref, mean_ref, mask_ref,
    xv, wv, kvb, kc, e_s, dp_s, qv, qcat, sums, mine, oth, sib, snd_r, snd_l, got_r, got_l,
    hat, inv, diag, dqt, qn_s, don_s, rows_s, allq, alld, x3, acc, fish, own, part, tile, box, box2,
    do_v, gain, tin, tt, damp_v,
    sl, s_sw, r_sw, sr, rr, sq, rq, s3x, r3x, s3y, r3y, s3f, r3f, sf, rf, s1, r1, s2, r2,
    sw, rw, sd, rd, sg, rg, sx, rx, sxx, rxx, sz, rz, *ring_sems,
):
    y, z, x, c = place()
    t_dev = tok.shape[0]
    queries = 2 * t_dev
    scale = 1.0 / math.sqrt(HD)
    to_exp2 = scale * math.log2(math.e)
    sems_w, sems_kv, sems_d, sems_q = ring_sems[:6], ring_sems[6:12], ring_sems[12:18], ring_sems[18:]
    h = lax.rem(x, 2)
    xr, xl = lax.rem(x + 1, NX), lax.rem(x + NX - 1, NX)
    home, slot = y // 2, lax.rem(y, 2)
    at_home = lax.eq(home, c)
    here, there = 128 * h, 128 * (1 - h)
    right, left = (y, lax.rem(z + 1, NZ), x, c), (y, lax.rem(z + NZ - 1, NZ), x, c)
    yu, yd, yf = lax.rem(y + 1, NY), lax.rem(y + NY - 1, NY), lax.rem(y + 2, NY)
    up, down = (yu, z, x, c), (yd, z, x, c)
    mine_t = lax.eq(x // 2, c)
    load_t = pltpu.make_async_copy(tok.at[:, pl.ds(pl.multiple_of(768 * x, 768), 768)], tin, sl.at[0])
    own_x = pltpu.make_async_copy(tok, xv.at[slot], sl.at[3])
    g_src = gains.at[:, pl.ds(pl.multiple_of(128 * slot, 128), 128)]
    own_g = pltpu.make_async_copy(g_src, gain, sl.at[5])

    get_damp = pltpu.make_async_copy(damp, damp_v, sl.at[4])
    get_damp.start()

    @pl.when(mine_t)
    def _():
        load_t.start()

    @pl.when(at_home)
    def _():
        own_x.start()
        own_g.start()

    first = []
    for dz in range(NZ):
        for dc in range(NC):
            if dz or dc:
                first.append((y, lax.rem(z + dz, NZ), x, lax.rem(c + dc, NC)))
    second = []
    for dy in range(NY):
        for dx in range(NX):
            if dy or dx:
                second.append((lax.rem(y + dy, NY), z, lax.rem(x + dx, NX), c))
    third = []
    for dy in range(1, NY):
        third.append((lax.rem(y + dy, NY), z, x, 1 - c))
    greet(first + second + third)

    def span(base, piece, count):
        return pl.ds(pl.multiple_of(base + 64 * piece, 64), count)

    def hand_w(j, target, src_y, sem_at, recv_at):
        return rcopy(
            w.at[:, :, pl.ds(128 * j, 128)], wv.at[:, src_y, z], sw.at[sem_at], rw.at[recv_at], (target, z, x, home)
        )

    def hand_d(j, target, dst_slot, sem_at, recv_at):
        return rcopy(
            cot.at[:, pl.ds(128 * j, 128)], do_v.at[dst_slot], sd.at[sem_at], rd.at[recv_at], (target, z, x, home)
        )

    def own_w(j):
        return pltpu.make_async_copy(w.at[:, :, pl.ds(128 * j, 128)], wv.at[:, y, z], sl.at[1])

    def own_d(j):
        return pltpu.make_async_copy(cot.at[:, pl.ds(128 * j, 128)], do_v.at[slot], sl.at[2])

    for j in range(2):
        target = 2 * c + j
        is_self = lax.eq(target, y)

        @pl.when(is_self)
        def _(j=j):
            own_w(j).start()
            own_d(j).start()

        @pl.when(jnp.logical_not(is_self))
        def _(j=j, target=target):
            hand_w(j, target, y, j, slot).start()

    def x_own(direction, i):
        ref, dev, at = tok.at[span(here, i, 64)], (up if direction == 0 else down), 2 * direction + i
        return rcopy(ref, xv.at[slot, span(here, i, 64)], sx.at[at], rx.at[at], dev)

    give_g = rcopy(g_src, gain, sg.at[0], rg.at[0], (y, z, x, 1 - c))

    @pl.when(at_home)
    def _():
        x_own(0, 0).start()
        x_own(1, 1).start()
        x_own(0, 1).start()
        x_own(1, 0).start()
        give_g.start()

    def give_t(dz, dst_z):
        return rcopy(
            tt.at[dst_z], x3.at[y, lax.rem(x, 2), z], sz.at[dz - 1], rz.at[dz - 1], (y, dst_z, x, c)
        )

    def take_t(dz, src_z):
        return rcopy(
            tt.at[z], x3.at[y, lax.rem(x, 2), src_z], sz.at[dz - 1], rz.at[dz - 1], (y, src_z, x, c)
        )

    code = lax.broadcasted_iota(jnp.int32, (HD, t_dev), 0)

    def key_codes(s, carry):
        good = jnp.logical_and(code == clip_ref[s], live_ref[s] == 1)
        value = jnp.where(good, 0.0, jnp.where(code < CLIPS, -BIG, 0.0))
        kc[s] = value.T.astype(BF)
        return carry

    lax.fori_loop(0, NY * NZ, key_codes, 0)
    w_ring = Chunks(lambda yb, zb: wv.at[:, yb, zb], sems_w)
    for j in range(2):
        src_y = 2 * c + j
        is_self = lax.eq(src_y, y)

        @pl.when(is_self)
        def _(j=j):
            own_w(j).wait()

        @pl.when(jnp.logical_not(is_self))
        def _(j=j, src_y=src_y):
            hand_w(j, src_y, src_y, j, j).wait_recv()

        w_ring.start(j)

    def piece(block, base, i):
        return xv.at[lax.rem(block, 2), span(base, i, 64)]

    def relay(block, i):
        ref = piece(block, here, i)
        return rcopy(ref, ref, sx.at[4 + i], rx.at[4 + i], up if i == 0 else down)

    def across(d, block, i):
        ref = piece(block, here, i)
        return rcopy(ref, ref, sxx.at[d - 1, i], rxx.at[d - 1, i], (y, z, xr if i == 0 else xl, c))

    def from_across(d, block, i):
        ref = piece(block, there, i)
        return rcopy(ref, ref, sxx.at[d - 1, i], rxx.at[d - 1, i], (y, z, xr if i == 0 else xl, c))

    blocks = {d: lax.rem(y + NY - d, NY) for d in (1, 2, 3)}
    near = {1: 0, 3: 1}
    def take_near(last):
        for d in (1, 3):
            block = blocks[d]

            @pl.when(lax.eq(block // 2, c))
            def _(d=d, block=block):
                i = near[d] if not last else 1 - near[d]
                ref, at = piece(block, here, i), 2 * near[d] + i
                rcopy(ref, ref, sx.at[at], rx.at[at], up if d == 1 else down).wait_recv()
                if not last:
                    relay(block, i).start()
                across(d, block, i).start()

    def take_far_block(i):
        block = blocks[2]

        @pl.when(lax.eq(block // 2, c))
        def _():
            relay(block, i).wait_recv()
            across(2, block, i).start()

    take_near(False)
    w_ring.step(0, 0)
    w_ring.step(0, 1)
    w_ring.step(1, 0)
    take_near(True)
    w_ring.step(1, 1)
    w_ring.step(2, 0)
    take_far_block(0)
    take_far_block(1)
    w_ring.step(2, 1)
    for j in range(2):
        target = 2 * c + j

        @pl.when(jnp.logical_not(lax.eq(target, y)))
        def _(j=j, target=target):
            hand_d(j, target, slot, j, slot).start()

    for b in range(2):
        s = (2 * c + b) * NZ + z
        at = pl.ds(t_dev * b, t_dev)
        qcat[at, HD:] = jnp.where(code == clip_ref[s], 1.0, 0.0).T.astype(BF)
        rows_s[0:1, at] = 1.0 - live_ref[s].astype(F32)

    @pl.when(mine_t)
    def _():
        load_t.wait()
        turned = tin[...].T
        for dz in range(NZ):
            tt[dz] = turned[ROWS * dz : ROWS * (dz + 1)]
        x3[y, lax.rem(x, 2), z] = tt[z]
        for dz in range(1, NZ):
            give_t(dz, lax.rem(z + dz, NZ)).start()

    for b in range(2):
        w_ring.far(b)
    for b in range(2):
        for i in range(8):
            w_ring.sib(i, b, 1 - c, z).wait_recv()

    def take_block(d):
        block = blocks[d]

        @pl.when(lax.eq(block // 2, c))
        def _():
            for i in range(2):
                from_across(d, block, i).wait_recv()

    @pl.when(at_home)
    def _():
        own_x.wait()
        own_g.wait()

    @pl.when(jnp.logical_not(at_home))
    def _():
        give_g.wait_recv()
        take_block(1)
        take_block(3)

    kv_ring = Chunks(lambda yb, zb: kvb.at[yb, zb], sems_kv)
    b_first = jnp.where(at_home, slot, 1 - slot)

    def project(b):
        block_rows = xv[b]
        at = pl.ds(pl.multiple_of(t_dev * b, t_dev), t_dev)
        for j in (1, 2, 0):
            raw = jnp.dot(block_rows, wv[j].reshape(D, HD), preferred_element_type=F32)
            if j == 2:
                kvb[2 * c + b, z, :, HD:] = raw.astype(BF)
                kv_ring.start(b)
            else:
                scale_back = lax.rsqrt(jnp.mean(raw * raw, -1, keepdims=True) + 1e-06)
                normed = raw * scale_back
                hat[b, j] = normed
                inv[b, j] = jnp.broadcast_to(scale_back, normed.shape)
                out = (normed * gain[j : j + 1, :]).astype(BF)
                if j == 0:
                    qv[at, :] = out
                    qcat[at, :HD] = out
                else:
                    kvb[2 * c + b, z, :, :HD] = out

    project(b_first)

    @pl.when(at_home)
    def _():
        take_block(1)
        take_block(3)

    @pl.when(jnp.logical_not(at_home))
    def _():
        take_block(2)

    b_second = 1 - b_first
    project(b_second)

    def give_x(dx):
        ref = x3.at[y, lax.rem(x, 2)]
        return rcopy(ref, ref, s3x.at[dx - 1], r3x.at[dx - 1], (y, z, lax.rem(x + dx, NX), c))

    @pl.when(mine_t)
    def _():
        for dz in range(1, NZ):
            take_t(dz, lax.rem(z + NZ - dz, NZ)).wait_recv()
        for dx in (1, 3, 2):
            give_x(dx).start()

    def take_x():
        for dx in range(1, NX):
            src = lax.rem(x + NX - dx, NX)

            @pl.when(lax.eq(src // 2, c))
            def _(dx=dx, src=src):
                ref = x3.at[y, lax.rem(src, 2)]
                rcopy(ref, ref, s3x.at[dx - 1], r3x.at[dx - 1], (y, z, src, c)).wait_recv()

    def give_y(direction):
        return rcopy(x3.at[y], x3.at[y], s3y.at[direction], r3y.at[direction], up if direction == 0 else down)

    def take_y(direction):
        ref = x3.at[yd if direction == 0 else yu]
        return rcopy(ref, ref, s3y.at[direction], r3y.at[direction], up if direction == 0 else down)

    def give_far(direction):
        ref = x3.at[yd if direction == 0 else yu, direction]
        return rcopy(ref, ref, s3f.at[direction], r3f.at[direction], up if direction == 0 else down)

    def take_far(direction):
        ref = x3.at[yf, direction]
        return rcopy(ref, ref, s3f.at[direction], r3f.at[direction], up if direction == 0 else down)

    for j in range(2):
        src_y = 2 * c + j
        is_self = lax.eq(src_y, y)

        @pl.when(is_self)
        def _(j=j):
            own_d(j).wait()

        @pl.when(jnp.logical_not(is_self))
        def _(j=j, src_y=src_y):
            hand_d(j, src_y, j, j, j).wait_recv()

    sums[...] = jnp.zeros_like(sums)

    def fold(v):
        return jnp.sum(v.reshape(t_dev // 8, 8, queries), 0)

    def pass_one(yb, zb):
        s = yb * NZ + zb
        k_cat = jnp.concatenate([kvb[yb, zb, :, :HD], kc[s]], 1)
        e = jnp.exp2(lax.dot_general(k_cat, qcat[...], NT, preferred_element_type=F32) * to_exp2)
        dp = lax.dot_general(kvb[yb, zb, :, HD:], do_v[...].reshape(queries, HD), NT, preferred_element_type=F32)
        e_s[s] = e.astype(BF)
        dp_s[s] = dp.astype(BF)
        sums[0] += fold(e)
        sums[1] += fold(e * dp)

    kv_ring.step(0, b_first)

    def blocks_of(k, b):
        kv_ring.step_sib(k, 1 - b)
        four_blocks(z - 1 - k, 2 * c + b, z + 1 + k, 2 * (1 - c) + 1 - b, pass_one)

    kv_ring.sib(0, b_second, 1 - c, z).wait_recv()
    two_blocks(z, 2 * c + b_first, 2 * (1 - c) + b_second, pass_one)
    blocks_of(0, b_first)
    kv_ring.sib(0, b_first, 1 - c, z).wait_recv()
    two_blocks(z, 2 * c + b_second, 2 * (1 - c) + b_first, pass_one)

    def gather_step(i, carry):
        b = jnp.where(lax.rem(i, 2) == 0, b_second, b_first)
        k = (i + 1) // 2
        kv_ring.step(k, b)
        blocks_of(k, b)
        return carry

    lax.fori_loop(0, 2, gather_step, 0)
    qf, dof = qv[...].astype(F32), do_v[...].reshape(queries, HD).astype(F32)
    own_k = kvb[pl.ds(2 * c, 2), z, :, :HD].reshape(queries, HD).astype(F32)
    own_v = kvb[pl.ds(2 * c, 2), z, :, HD:].reshape(queries, HD).astype(F32)
    rows_s[3:4, :] = rows_s[0:1, :] * jnp.exp2(jnp.sum((qf * own_k).T, 0, keepdims=True) * to_exp2)
    rows_s[4:5, :] = jnp.sum((dof * own_v).T, 0, keepdims=True)

    lax.fori_loop(2, 5, gather_step, 0)
    take_x()
    give_y(0).start()
    give_y(1).start()
    for b, other in ((b_first, b_second), (b_second, b_first)):
        kv_ring.far(b)
        kv_ring.sib(4, other, 1 - c, z + 4).wait_recv()
        two_blocks(z + 4, 2 * c + b, 2 * (1 - c) + other, pass_one)

    total = jnp.sum(sums[0], 0, keepdims=True)
    dot = jnp.sum(sums[1], 0, keepdims=True)
    own_e, own_dp = rows_s[3:4, :], rows_s[4:5, :]
    total = total + own_e
    dot = dot + own_e * own_dp
    inv_row = 1.0 / total
    row_dot = dot * inv_row
    column = lambda v: jnp.broadcast_to(v, (HD, queries)).T
    inv_col = column(inv_row)
    qn_s[...] = (qv[...].astype(F32) * inv_col).astype(BF)
    don_s[...] = (do_v[...].reshape(queries, HD).astype(F32) * inv_col).astype(BF)
    rows_s[1:2, :] = row_dot
    rows_s[2:3, :] = inv_row
    dqt[...] = jnp.zeros_like(dqt)
    got_r[0, 1] = jnp.zeros_like(got_r[0, 1])
    got_l[0, 0] = jnp.zeros_like(got_l[0, 0])

    def pass_two(yb, zb):
        s = yb * NZ + zb
        e = e_s[s]
        ds = (e.astype(F32) * (dp_s[s].astype(F32) - rows_s[1:2, :])).astype(BF)
        dv = jnp.dot(e, don_s[...], preferred_element_type=F32)
        dk = jnp.dot(ds, qn_s[...], preferred_element_type=F32) * scale
        dqt[...] += lax.dot_general(kvb[yb, zb, :, :HD], ds, TN, preferred_element_type=F32)
        return jnp.concatenate([dk, dv], 1).astype(BF)

    def swap(i, offset, b):
        at = lax.rem(z + offset + NZ, NZ)
        return rcopy(oth.at[b, at], sib.at[b, at], s_sw.at[i, b], r_sw.at[i, b], (y, z, x, 1 - c))

    def terms(i, offsets, b):
        def one(n, carry):
            at = lax.rem(z + jnp.where(lax.rem(n, 2) == 0, offsets[0], offsets[1]) + NZ, NZ)
            core = jnp.where(n < 2, 1 - c, c)
            value = pass_two(2 * core + b, at)

            @pl.when(n < 2)
            def _():
                oth[b, at] = value
                swap(i + n, at - z, b).start()

            @pl.when(n >= 2)
            def _():
                mine[b, at] = value

            return carry

        lax.fori_loop(0, 4, one, 0)

    def terms_one(i, offset):
        at = lax.rem(z + offset + NZ, NZ)

        def one(n, carry):
            b = lax.rem(n, 2)
            core = jnp.where(n < 2, 1 - c, c)
            value = pass_two(2 * core + b, at)

            @pl.when(n < 2)
            def _():
                oth[b, at] = value
                swap(i, offset, b).start()

            @pl.when(n >= 2)
            def _():
                mine[b, at] = value

            return carry

        lax.fori_loop(0, 4, one, 0)

    def chip(offset, half):
        at = lax.rem(z + offset + NZ, NZ)
        return mine[half, at].astype(F32) + sib[half, at].astype(F32)

    def send_r(t, b):
        return rcopy(snd_r.at[t, b], got_r.at[t, b], sr.at[t, b], rr.at[t, b], right)

    def send_l(t, b):
        return rcopy(snd_l.at[t, b], got_l.at[t, b], sq.at[t, b], rq.at[t, b], left)

    terms_one(0, 4)
    swap(0, 4, 0).wait_recv()
    snd_r[0, 0] = chip(4, 0).astype(BF)
    send_r(0, 0).start()
    swap(0, 4, 1).wait_recv()
    snd_l[0, 1] = chip(4, 1).astype(BF)
    send_l(0, 1).start()

    def sum_step(i, carry):
        t, b = 1 + i // 2, lax.rem(i, 2)
        terms(2 * t - 1, (4 - t, t - 4), b)

        @pl.when(i == 4)
        def _():
            for direction in range(2):
                take_y(direction).wait_recv()
                give_far(direction).start()

        swap(2 * t - 1, 4 - t, b).wait_recv()
        pl.when(i != 1)(lambda: send_r(t - 1, b).wait_recv())
        snd_r[t, b] = (chip(4 - t, b) + got_r[t - 1, b].astype(F32)).astype(BF)
        send_r(t, b).start()
        swap(2 * t, t - 4, b).wait_recv()
        pl.when(i != 0)(lambda: send_l(t - 1, b).wait_recv())
        snd_l[t, b] = (chip(t - 4, b) + got_l[t - 1, b].astype(F32)).astype(BF)
        send_l(t, b).start()
        return carry

    lax.fori_loop(0, 6, sum_step, 0)
    terms_one(7, 0)
    own_p = rows_s[3:4, :] * rows_s[2:3, :]
    own_ds = own_p * (rows_s[4:5, :] - rows_s[1:2, :])
    ds_col = column(own_ds).astype(BF).astype(F32)
    diag[:, :HD] = ds_col * qv[...].astype(F32) * scale
    diag[:, HD:] = column(own_p).astype(BF).astype(F32) * do_v[...].reshape(queries, HD).astype(F32)
    dq = (dqt[...] * rows_s[2:3, :]).T
    q_ring = Chunks(lambda yb, zb: allq.at[yb, zb], sems_q)
    d_ring = Chunks(lambda yb, zb: alld.at[yb, zb], sems_d)

    def norm_back(b, j, upstream):
        normed = hat[b, j]
        return inv[b, j] * (upstream - normed * jnp.mean(normed * upstream, -1, keepdims=True))

    for b in range(2):
        own_kb = kvb[2 * c + b, z, :, :HD].astype(F32)
        dqn = (dq[t_dev * b : t_dev * (b + 1)] + ds_col[t_dev * b : t_dev * (b + 1)] * own_kb) * scale
        allq[2 * c + b, z] = norm_back(b, 0, dqn * gain[0:1, :]).astype(BF)
        q_ring.start(b)
    for b in range(2):
        swap(7, 0, b).wait_recv()
    for b in range(2):
        at = pl.ds(t_dev * b, t_dev)
        send_r(3, b).wait_recv()
        send_l(3, b).wait_recv()
        dkv = chip(0, b) + got_r[3, b].astype(F32) + got_l[3, b].astype(F32) + diag[at, :]
        alld[2 * c + b, z, :, :HD] = norm_back(b, 1, dkv[:, :HD] * gain[1:2, :]).astype(BF)
        alld[2 * c + b, z, :, HD:] = dkv[:, HD:].astype(BF)
        d_ring.start(b)

    acc[...] = jnp.zeros_like(acc)
    for direction in range(2):
        take_far(direction).wait_recv()

    def grads(yb, zb):
        s = yb * NZ + zb
        rows = jnp.concatenate([x3[yb, 0, zb], x3[yb, 1, zb]], 0)
        parts = []
        for clip in range(CLIPS):
            keep = jnp.broadcast_to(jnp.where(clip_ref[s] == clip, 1.0, 0.0), rows.shape).astype(BF)
            parts.append(rows * keep)
        masked = jnp.concatenate(parts, 0)
        acc[:, :HD] += jnp.dot(masked, allq[yb, zb], preferred_element_type=F32)
        acc[:, HD:] += jnp.dot(masked, alld[yb, zb], preferred_element_type=F32)

    for b in range(2):
        q_ring.sib(0, b, 1 - c, z).wait_recv()
        d_ring.sib(0, b, 1 - c, z).wait_recv()
        two_blocks(z, 2 * c + b, 2 * (1 - c) + b, grads)

    def finish_inputs():
        for d in (1, 3, 2):
            block = blocks[d]

            @pl.when(lax.eq(block // 2, c))
            def _(d=d, block=block):
                for i in range(2):
                    across(d, block, i).wait_send()
                if d != 2:
                    relay(block, near[d]).wait_send()

        @pl.when(at_home)
        def _():
            for i in range(2):
                x_own(0, i).wait_send()
                x_own(1, i).wait_send()
            give_g.wait_send()

        @pl.when(mine_t)
        def _():
            for dz in range(1, NZ):
                give_t(dz, lax.rem(z + dz, NZ)).wait_send()

        for j in range(2):
            src_y = 2 * c + j

            @pl.when(jnp.logical_not(lax.eq(src_y, y)))
            def _(j=j, src_y=src_y):
                hand_w(j, src_y, src_y, j, j).wait_send()
                hand_d(j, src_y, j, j, j).wait_send()

    finish_inputs()
    w_ring.finish()
    kv_ring.finish()
    for i, offset in enumerate((4, 3, -3, 2, -2, 1, -1, 0)):
        for b in range(2):
            swap(i, offset, b).wait_send()
    for t in range(4):
        for b in range(2):
            if t or b == 0:
                send_r(t, b).wait_send()
            if t or b == 1:
                send_l(t, b).wait_send()
    for direction in range(2):
        give_y(direction).wait_send()

    @pl.when(mine_t)
    def _():
        for dx in range(1, NX):
            give_x(dx).wait_send()

    def grad_step(k, carry):
        for b in range(2):
            q_ring.step(k, b)
            d_ring.step(k, b)

        def one(b, carry):
            q_ring.step_sib(k, b)
            d_ring.step_sib(k, b)
            four_blocks(z - 1 - k, 2 * c + b, z + 1 + k, 2 * (1 - c) + b, grads)
            return carry

        return lax.fori_loop(0, 2, one, carry)

    lax.fori_loop(0, 3, grad_step, 0)
    for b in range(2):
        q_ring.far(b)
        d_ring.far(b)
    for b in range(2):
        q_ring.sib(4, b, 1 - c, z + 4).wait_recv()
        d_ring.sib(4, b, 1 - c, z + 4).wait_recv()
        two_blocks(z + 4, 2 * c + b, 2 * (1 - c) + b, grads)

    two = 2 * ROWS
    fisher = jnp.square(acc[0:two]) + jnp.square(acc[two : 2 * two]) + jnp.square(acc[2 * two :])
    for j in range(2):
        fish[j] = fisher[ROWS * j : ROWS * (j + 1)]
    rows = jnp.sum(fisher.reshape(two // 8, 8, 3 * HD), 0)
    part[...] = rows[:, :HD] + rows[:, HD : 2 * HD] + rows[:, 2 * HD :]

    for i, device in enumerate(first):
        rcopy(part, box.at[i], s1.at[i], r1.at[i], device).start()

    def give(j, target, dst_slot, recv_at):
        return rcopy(fish.at[j], own.at[dst_slot], sf.at[j], rf.at[recv_at], (target, z, x, home))

    def keep_own(j):
        return pltpu.make_async_copy(fish.at[j], own.at[slot], sl.at[6])

    for j in range(2):
        target = 2 * c + j

        @pl.when(lax.eq(target, y))
        def _(j=j):
            keep_own(j).start()

        @pl.when(jnp.logical_not(lax.eq(target, y)))
        def _(j=j, target=target):
            give(j, target, slot, slot).start()

    for i, device in enumerate(first):
        rcopy(part, box.at[i], s1.at[i], r1.at[i], device).wait_recv()
    tile[...] = part[...] + jnp.sum(box[...], 0)
    for i, device in enumerate(second):
        rcopy(tile, box2.at[i], s2.at[i], r2.at[i], device).start()

    q_ring.finish()
    d_ring.finish()
    for direction in range(2):
        give_far(direction).wait_send()

    for j in range(2):
        target = 2 * c + j

        @pl.when(lax.eq(target, y))
        def _(j=j):
            keep_own(j).wait()

        @pl.when(jnp.logical_not(lax.eq(target, y)))
        def _(j=j, target=target):
            give(j, target, j, j).wait_recv()
            give(j, target, j, j).wait_send()

    for i, device in enumerate(second):
        rcopy(tile, box2.at[i], s2.at[i], r2.at[i], device).wait_recv()
    whole = jnp.sum(tile[...] + jnp.sum(box2[...], 0))
    mean_ref[...] = jnp.full(mean_ref.shape, whole / (3 * D * HEADS * HD) + 1e-06)
    get_damp.wait()
    mask_ref[...] = damp_v[...].astype(F32)
    for j in range(3):
        for h in range(2):
            fisher_ref[j, :, HD * h : HD * (h + 1)] = own[h, :, HD * j : HD * (j + 1)]
    for i, device in enumerate(first):
        rcopy(part, box.at[i], s1.at[i], r1.at[i], device).wait_send()
    for i, device in enumerate(second):
        rcopy(tile, box2.at[i], s2.at[i], r2.at[i], device).wait_send()


def shape(dims, dtype=BF):
    return jax.ShapeDtypeStruct(dims, dtype)


def comm(collective, limit=None):
    return pltpu.CompilerParams(collective_id=collective, has_side_effects=True, vmem_limit_bytes=limit)


def on_device(tokens, w_qkv, gains, cotangent, token_clip, key_live, damp_mask):
    y, z, x, c = place()
    n_tok = token_clip.shape[0]
    t_dev = n_tok // (NY * NZ)
    blocks = (NY, NZ, t_dev)
    half = (2, NZ, t_dev, 2 * HD)
    trips = (4, 2, t_dev, 2 * HD)
    queries = 2 * t_dev
    fisher, divisor, mask = pl.pallas_call(
        main_kernel,
        out_shape=(shape((3, ROWS, 2 * HD), F32), shape((ROWS, 2 * HD), F32), shape((ROWS, 2 * HD), F32)),
        in_specs=[ANY, ANY, ANY, ANY, VMEM, VMEM, ANY],
        out_specs=(VMEM,) * 3,
        scratch_shapes=[
            pltpu.VMEM((2, t_dev, D), BF),
            pltpu.VMEM((3, NY, NZ, ROWS, HD), BF),
            pltpu.VMEM((*blocks, 2 * HD), BF),
            pltpu.VMEM((NY * NZ, t_dev, HD), BF),
            pltpu.VMEM((NY * NZ, t_dev, queries), BF),
            pltpu.VMEM((NY * NZ, t_dev, queries), BF),
            pltpu.VMEM((queries, HD), BF),
            pltpu.VMEM((queries, 2 * HD), BF),
            pltpu.VMEM((2, 8, queries), F32),
            pltpu.VMEM(half, BF), pltpu.VMEM(half, BF), pltpu.VMEM(half, BF),
            pltpu.VMEM(trips, BF), pltpu.VMEM(trips, BF), pltpu.VMEM(trips, BF), pltpu.VMEM(trips, BF),
            pltpu.VMEM((2, 2, t_dev, HD), F32), pltpu.VMEM((2, 2, t_dev, HD), F32),
            pltpu.VMEM((queries, 2 * HD), F32),
            pltpu.VMEM((HD, queries), F32),
            pltpu.VMEM((queries, HD), BF), pltpu.VMEM((queries, HD), BF),
            pltpu.VMEM((8, queries), F32),
            pltpu.VMEM((*blocks, HD), BF),
            pltpu.VMEM((*blocks, 2 * HD), BF),
            pltpu.VMEM((NY, 2, NZ, ROWS, t_dev), BF),
            pltpu.VMEM((CLIPS * 2 * ROWS, 3 * HD), F32),
            pltpu.VMEM((2, ROWS, 3 * HD), F32), pltpu.VMEM((2, ROWS, 3 * HD), F32),
            pltpu.VMEM((8, HD), F32), pltpu.VMEM((8, HD), F32),
            pltpu.VMEM((15, 8, HD), F32), pltpu.VMEM((15, 8, HD), F32),
            pltpu.VMEM((2, t_dev, HD), BF),
            pltpu.VMEM((2, HD), F32),
            pltpu.VMEM((t_dev, NZ * ROWS), BF),
            pltpu.VMEM((NZ, ROWS, t_dev), BF),
            pltpu.VMEM((ROWS, 2 * HD), jnp.int32),
            DMA((7,)), DMA((8, 2)), DMA((8, 2)),
            DMA((4, 2)), DMA((4, 2)), DMA((4, 2)), DMA((4, 2)),
            DMA((3,)), DMA((3,)), DMA((2,)), DMA((2,)), DMA((2,)), DMA((2,)), DMA((2,)), DMA((2,)),
            DMA((15,)), DMA((15,)), DMA((15,)), DMA((15,)),
            DMA((2,)), DMA((2,)), DMA((2,)), DMA((2,)), DMA((1,)), DMA((1,)),
            DMA((6,)), DMA((6,)), DMA((3, 2)), DMA((3, 2)), DMA((7,)), DMA((7,)),
            *CHUNK_SEMS, *CHUNK_SEMS, *CHUNK_SEMS, *CHUNK_SEMS,
        ],
        compiler_params=comm(1, 63 * MIB),
        name="main_kernel",
    )(
        tokens, w_qkv, cotangent, gains,
        token_clip.reshape(NY * NZ, 1, t_dev), key_live.reshape(NY * NZ, 1, t_dev), damp_mask,
    )
    ratio = fisher / divisor[None]
    dampened = (w_qkv.astype(F32) / (1.0 + mask[None] * ratio)).astype(BF)
    return ratio, dampened


def solution(mesh):
    grid = Mesh(mesh.devices.reshape(NY, NZ, NX, NC), ("y", "z", "x", "c"))
    seq, head = ("y", "z"), ("x", "c")
    return jax.shard_map(
        on_device,
        mesh=grid,
        in_specs=(
            P(seq, None),
            P(None, seq, head),
            P(None, head),
            P(seq, head),
            P(),
            P(),
            P(seq, head),
        ),
        out_specs=(P(None, seq, head), P(None, seq, head)),
        check_vma=False,
    )
```

```python
import math

import jax
import jax.numpy as jnp
from jax import lax
from jax.experimental import pallas as pl
from jax.experimental.pallas import tpu as pltpu
from jax.sharding import Mesh, PartitionSpec as P

MESH = pl.DeviceIdType.MESH
D = 3072
HD = 128
HEADS = 16
CLIPS = 3
NY, NZ, NX, NC = 4, 8, 4, 2
ROWS = D // (NY * NZ)
BF = jnp.bfloat16
F32 = jnp.float32
BIG = 30000.0
ANY = pl.BlockSpec(memory_space=pl.ANY)
VMEM = pl.BlockSpec(memory_space=pltpu.VMEM)
SMEM = pl.BlockSpec(memory_space=pltpu.SMEM)
DMA = pltpu.SemaphoreType.DMA
MIB = 1 << 20


def place():
    return lax.axis_index("y"), lax.axis_index("z"), lax.axis_index("x"), lax.axis_index("c")


def rcopy(src, dst, send, recv, device):
    return pltpu.make_async_remote_copy(
        src_ref=src, dst_ref=dst, send_sem=send, recv_sem=recv, device_id=device, device_id_type=MESH
    )


def greet(devices):
    barrier = pltpu.get_barrier_semaphore()
    for device in devices:
        pl.semaphore_signal(barrier, inc=1, device_id=device, device_id_type=MESH)
    pl.semaphore_wait(barrier, len(devices))


class Chunks:
    def __init__(self, view, sems):
        self.view = view
        self.send_r, self.recv_r, self.send_l, self.recv_l, self.send_s, self.recv_s = sems
        self.y, self.z, self.x, self.c = place()

    def at(self, core, z, b):
        return self.view(2 * core + b, lax.rem(z + NZ, NZ))

    def right(self, k, b, z):
        v = self.at(self.c, z, b)
        return rcopy(
            v, v, self.send_r.at[k, b], self.recv_r.at[k, b], (self.y, lax.rem(self.z + 1, NZ), self.x, self.c)
        )

    def left(self, k, b, z):
        v = self.at(self.c, z, b)
        return rcopy(
            v, v, self.send_l.at[k, b], self.recv_l.at[k, b], (self.y, lax.rem(self.z + NZ - 1, NZ), self.x, self.c)
        )

    def sib(self, i, b, core, z):
        v = self.at(core, z, b)
        return rcopy(v, v, self.send_s.at[i, b], self.recv_s.at[i, b], (self.y, self.z, self.x, 1 - self.c))

    def start(self, b):
        self.right(0, b, self.z).start()
        self.left(0, b, self.z).start()
        self.sib(0, b, self.c, self.z).start()

    def step(self, k, b):
        zr, zl = self.z - 1 - k, self.z + 1 + k
        self.right(k, b, zr).wait_recv()
        pl.when((b == 0) | (k < 2))(lambda: self.right(k + 1, b, zr).start())
        self.sib(1 + k, b, self.c, zr).start()
        self.left(k, b, zl).wait_recv()
        pl.when((b == 1) | (k < 2))(lambda: self.left(k + 1, b, zl).start())
        self.sib(5 + k, b, self.c, zl).start()

    def step_sib(self, k, b):
        self.sib(1 + k, b, 1 - self.c, self.z - 1 - k).wait_recv()
        self.sib(5 + k, b, 1 - self.c, self.z + 1 + k).wait_recv()

    def far(self, b):
        far = self.z + 4
        pl.when(b == 0)(lambda: self.right(3, 0, far).wait_recv())
        pl.when(b == 1)(lambda: self.left(3, 1, far).wait_recv())
        self.sib(4, b, self.c, far).start()

    def finish(self):
        for b in range(2):
            for k in range(4):
                if k < 3 or b == 0:
                    self.right(k, b, self.z - k).wait_send()
                if k < 3 or b == 1:
                    self.left(k, b, self.z + k).wait_send()
            for i in range(8):
                self.sib(i, b, self.c, self.z).wait_send()


CHUNK_SEMS = [DMA((4, 2)), DMA((4, 2)), DMA((4, 2)), DMA((4, 2)), DMA((8, 2)), DMA((8, 2))]


def four_blocks(z1, y1, z2, y2, body):
    def one(i, carry):
        zb = jnp.where(lax.rem(i, 2) == 0, z1, z2)
        yb = jnp.where(i < 2, y1, y2)
        body(yb, lax.rem(zb + NZ, NZ))
        return carry

    lax.fori_loop(0, 4, one, 0)


def two_blocks(zb, y1, y2, body):
    def one(i, carry):
        body(jnp.where(i == 0, y1, y2), lax.rem(zb + NZ, NZ))
        return carry

    lax.fori_loop(0, 2, one, 0)


NT = (((1,), (1,)), ((), ()))
TN = (((0,), (0,)), ((), ()))


def main_kernel(
    tok, w, cot, gains, clip_ref, live_ref, damp,
    fisher_ref, mean_ref, mask_ref,
    xv, wv, kvb, kc, e_s, dp_s, qv, qcat, sums, mine, oth, sib, snd_r, snd_l, got_r, got_l,
    hat, inv, diag, dqt, qn_s, don_s, rows_s, allq, alld, x3, acc, fish, own, part, tile, box, box2,
    do_v, gain, tin, tt, damp_v,
    sl, s_sw, r_sw, sr, rr, sq, rq, s3x, r3x, s3y, r3y, s3f, r3f, sf, rf, s1, r1, s2, r2,
    sw, rw, sd, rd, sg, rg, sx, rx, sxx, rxx, sz, rz, *ring_sems,
):
    y, z, x, c = place()
    t_dev = tok.shape[0]
    queries = 2 * t_dev
    scale = 1.0 / math.sqrt(HD)
    to_exp2 = scale * math.log2(math.e)
    sems_w, sems_kv, sems_d, sems_q = ring_sems[:6], ring_sems[6:12], ring_sems[12:18], ring_sems[18:]
    h = lax.rem(x, 2)
    xr, xl = lax.rem(x + 1, NX), lax.rem(x + NX - 1, NX)
    home, slot = y // 2, lax.rem(y, 2)
    at_home = lax.eq(home, c)
    here, there = 128 * h, 128 * (1 - h)
    right, left = (y, lax.rem(z + 1, NZ), x, c), (y, lax.rem(z + NZ - 1, NZ), x, c)
    yu, yd, yf = lax.rem(y + 1, NY), lax.rem(y + NY - 1, NY), lax.rem(y + 2, NY)
    up, down = (yu, z, x, c), (yd, z, x, c)
    mine_t = lax.eq(x // 2, c)
    load_t = pltpu.make_async_copy(tok.at[:, pl.ds(pl.multiple_of(768 * x, 768), 768)], tin, sl.at[0])
    own_x = pltpu.make_async_copy(tok, xv.at[slot], sl.at[3])
    g_src = gains.at[:, pl.ds(pl.multiple_of(128 * slot, 128), 128)]
    own_g = pltpu.make_async_copy(g_src, gain, sl.at[5])

    get_damp = pltpu.make_async_copy(damp, damp_v, sl.at[4])
    get_damp.start()

    @pl.when(mine_t)
    def _():
        load_t.start()

    @pl.when(at_home)
    def _():
        own_x.start()
        own_g.start()

    first = []
    for dz in range(NZ):
        for dc in range(NC):
            if dz or dc:
                first.append((y, lax.rem(z + dz, NZ), x, lax.rem(c + dc, NC)))
    second = []
    for dy in range(NY):
        for dx in range(NX):
            if dy or dx:
                second.append((lax.rem(y + dy, NY), z, lax.rem(x + dx, NX), c))
    third = []
    for dy in range(1, NY):
        third.append((lax.rem(y + dy, NY), z, x, 1 - c))
    greet(first + second + third)

    def span(base, piece, count):
        return pl.ds(pl.multiple_of(base + 64 * piece, 64), count)

    def hand_w(j, target, src_y, sem_at, recv_at):
        return rcopy(
            w.at[:, :, pl.ds(128 * j, 128)], wv.at[:, src_y, z], sw.at[sem_at], rw.at[recv_at], (target, z, x, home)
        )

    def hand_d(j, target, dst_slot, sem_at, recv_at):
        return rcopy(
            cot.at[:, pl.ds(128 * j, 128)], do_v.at[dst_slot], sd.at[sem_at], rd.at[recv_at], (target, z, x, home)
        )

    def own_w(j):
        return pltpu.make_async_copy(w.at[:, :, pl.ds(128 * j, 128)], wv.at[:, y, z], sl.at[1])

    def own_d(j):
        return pltpu.make_async_copy(cot.at[:, pl.ds(128 * j, 128)], do_v.at[slot], sl.at[2])

    for j in range(2):
        target = 2 * c + j
        is_self = lax.eq(target, y)

        @pl.when(is_self)
        def _(j=j):
            own_w(j).start()
            own_d(j).start()

        @pl.when(jnp.logical_not(is_self))
        def _(j=j, target=target):
            hand_w(j, target, y, j, slot).start()

    def x_own(direction, i):
        ref, dev, at = tok.at[span(here, i, 64)], (up if direction == 0 else down), 2 * direction + i
        return rcopy(ref, xv.at[slot, span(here, i, 64)], sx.at[at], rx.at[at], dev)

    give_g = rcopy(g_src, gain, sg.at[0], rg.at[0], (y, z, x, 1 - c))

    @pl.when(at_home)
    def _():
        x_own(0, 0).start()
        x_own(1, 1).start()
        x_own(0, 1).start()
        x_own(1, 0).start()
        give_g.start()

    def give_t(dz, dst_z):
        return rcopy(
            tt.at[dst_z], x3.at[y, lax.rem(x, 2), z], sz.at[dz - 1], rz.at[dz - 1], (y, dst_z, x, c)
        )

    def take_t(dz, src_z):
        return rcopy(
            tt.at[z], x3.at[y, lax.rem(x, 2), src_z], sz.at[dz - 1], rz.at[dz - 1], (y, src_z, x, c)
        )

    code = lax.broadcasted_iota(jnp.int32, (HD, t_dev), 0)

    def key_codes(s, carry):
        good = jnp.logical_and(code == clip_ref[s], live_ref[s] == 1)
        value = jnp.where(good, 0.0, jnp.where(code < CLIPS, -BIG, 0.0))
        kc[s] = value.T.astype(BF)
        return carry

    lax.fori_loop(0, NY * NZ, key_codes, 0)
    w_ring = Chunks(lambda yb, zb: wv.at[:, yb, zb], sems_w)
    for j in range(2):
        src_y = 2 * c + j
        is_self = lax.eq(src_y, y)

        @pl.when(is_self)
        def _(j=j):
            own_w(j).wait()

        @pl.when(jnp.logical_not(is_self))
        def _(j=j, src_y=src_y):
            hand_w(j, src_y, src_y, j, j).wait_recv()

        w_ring.start(j)

    def piece(block, base, i):
        return xv.at[lax.rem(block, 2), span(base, i, 64)]

    def relay(block, i):
        ref = piece(block, here, i)
        return rcopy(ref, ref, sx.at[4 + i], rx.at[4 + i], up if i == 0 else down)

    def across(d, block, i):
        ref = piece(block, here, i)
        return rcopy(ref, ref, sxx.at[d - 1, i], rxx.at[d - 1, i], (y, z, xr if i == 0 else xl, c))

    def from_across(d, block, i):
        ref = piece(block, there, i)
        return rcopy(ref, ref, sxx.at[d - 1, i], rxx.at[d - 1, i], (y, z, xr if i == 0 else xl, c))

    blocks = {d: lax.rem(y + NY - d, NY) for d in (1, 2, 3)}
    near = {1: 0, 3: 1}
    def take_near(last):
        for d in (1, 3):
            block = blocks[d]

            @pl.when(lax.eq(block // 2, c))
            def _(d=d, block=block):
                i = near[d] if not last else 1 - near[d]
                ref, at = piece(block, here, i), 2 * near[d] + i
                rcopy(ref, ref, sx.at[at], rx.at[at], up if d == 1 else down).wait_recv()
                if not last:
                    relay(block, i).start()
                across(d, block, i).start()

    def take_far_block(i):
        block = blocks[2]

        @pl.when(lax.eq(block // 2, c))
        def _():
            relay(block, i).wait_recv()
            across(2, block, i).start()

    take_near(False)
    w_ring.step(0, 0)
    w_ring.step(0, 1)
    w_ring.step(1, 0)
    take_near(True)
    w_ring.step(1, 1)
    w_ring.step(2, 0)
    take_far_block(0)
    take_far_block(1)
    w_ring.step(2, 1)
    for j in range(2):
        target = 2 * c + j

        @pl.when(jnp.logical_not(lax.eq(target, y)))
        def _(j=j, target=target):
            hand_d(j, target, slot, j, slot).start()

    for b in range(2):
        s = (2 * c + b) * NZ + z
        at = pl.ds(t_dev * b, t_dev)
        qcat[at, HD:] = jnp.where(code == clip_ref[s], 1.0, 0.0).T.astype(BF)
        rows_s[0:1, at] = 1.0 - live_ref[s].astype(F32)

    @pl.when(mine_t)
    def _():
        load_t.wait()
        turned = tin[...].T
        for dz in range(NZ):
            tt[dz] = turned[ROWS * dz : ROWS * (dz + 1)]
        x3[y, lax.rem(x, 2), z] = tt[z]
        for dz in range(1, NZ):
            give_t(dz, lax.rem(z + dz, NZ)).start()

    for b in range(2):
        w_ring.far(b)
    for b in range(2):
        for i in range(8):
            w_ring.sib(i, b, 1 - c, z).wait_recv()

    def take_block(d):
        block = blocks[d]

        @pl.when(lax.eq(block // 2, c))
        def _():
            for i in range(2):
                from_across(d, block, i).wait_recv()

    @pl.when(at_home)
    def _():
        own_x.wait()
        own_g.wait()

    @pl.when(jnp.logical_not(at_home))
    def _():
        give_g.wait_recv()
        take_block(1)
        take_block(3)

    kv_ring = Chunks(lambda yb, zb: kvb.at[yb, zb], sems_kv)
    b_first = jnp.where(at_home, slot, 1 - slot)

    def project(b):
        block_rows = xv[b]
        at = pl.ds(pl.multiple_of(t_dev * b, t_dev), t_dev)
        for j in (1, 2, 0):
            raw = jnp.dot(block_rows, wv[j].reshape(D, HD), preferred_element_type=F32)
            if j == 2:
                kvb[2 * c + b, z, :, HD:] = raw.astype(BF)
                kv_ring.start(b)
            else:
                scale_back = lax.rsqrt(jnp.mean(raw * raw, -1, keepdims=True) + 1e-06)
                normed = raw * scale_back
                hat[b, j] = normed
                inv[b, j] = jnp.broadcast_to(scale_back, normed.shape)
                out = (normed * gain[j : j + 1, :]).astype(BF)
                if j == 0:
                    qv[at, :] = out
                    qcat[at, :HD] = out
                else:
                    kvb[2 * c + b, z, :, :HD] = out

    project(b_first)

    @pl.when(at_home)
    def _():
        take_block(1)
        take_block(3)

    @pl.when(jnp.logical_not(at_home))
    def _():
        take_block(2)

    b_second = 1 - b_first
    project(b_second)

    def give_x(dx):
        ref = x3.at[y, lax.rem(x, 2)]
        return rcopy(ref, ref, s3x.at[dx - 1], r3x.at[dx - 1], (y, z, lax.rem(x + dx, NX), c))

    @pl.when(mine_t)
    def _():
        for dz in range(1, NZ):
            take_t(dz, lax.rem(z + NZ - dz, NZ)).wait_recv()
        for dx in (1, 3, 2):
            give_x(dx).start()

    def take_x():
        for dx in range(1, NX):
            src = lax.rem(x + NX - dx, NX)

            @pl.when(lax.eq(src // 2, c))
            def _(dx=dx, src=src):
                ref = x3.at[y, lax.rem(src, 2)]
                rcopy(ref, ref, s3x.at[dx - 1], r3x.at[dx - 1], (y, z, src, c)).wait_recv()

    def give_y(direction):
        return rcopy(x3.at[y], x3.at[y], s3y.at[direction], r3y.at[direction], up if direction == 0 else down)

    def take_y(direction):
        ref = x3.at[yd if direction == 0 else yu]
        return rcopy(ref, ref, s3y.at[direction], r3y.at[direction], up if direction == 0 else down)

    def give_far(direction):
        ref = x3.at[yd if direction == 0 else yu, direction]
        return rcopy(ref, ref, s3f.at[direction], r3f.at[direction], up if direction == 0 else down)

    def take_far(direction):
        ref = x3.at[yf, direction]
        return rcopy(ref, ref, s3f.at[direction], r3f.at[direction], up if direction == 0 else down)

    for j in range(2):
        src_y = 2 * c + j
        is_self = lax.eq(src_y, y)

        @pl.when(is_self)
        def _(j=j):
            own_d(j).wait()

        @pl.when(jnp.logical_not(is_self))
        def _(j=j, src_y=src_y):
            hand_d(j, src_y, j, j, j).wait_recv()

    sums[...] = jnp.zeros_like(sums)

    def fold(v):
        return jnp.sum(v.reshape(t_dev // 8, 8, queries), 0)

    def pass_one(yb, zb):
        s = yb * NZ + zb
        k_cat = jnp.concatenate([kvb[yb, zb, :, :HD], kc[s]], 1)
        e = jnp.exp2(lax.dot_general(k_cat, qcat[...], NT, preferred_element_type=F32) * to_exp2)
        dp = lax.dot_general(kvb[yb, zb, :, HD:], do_v[...].reshape(queries, HD), NT, preferred_element_type=F32)
        e_s[s] = e.astype(BF)
        dp_s[s] = dp.astype(BF)
        sums[0] += fold(e)
        sums[1] += fold(e * dp)

    kv_ring.step(0, b_first)

    def blocks_of(k, b):
        kv_ring.step_sib(k, 1 - b)
        four_blocks(z - 1 - k, 2 * c + b, z + 1 + k, 2 * (1 - c) + 1 - b, pass_one)

    qf, dof = qv[...].astype(F32), do_v[...].reshape(queries, HD).astype(F32)
    own_k = kvb[pl.ds(2 * c, 2), z, :, :HD].reshape(queries, HD).astype(F32)
    own_v = kvb[pl.ds(2 * c, 2), z, :, HD:].reshape(queries, HD).astype(F32)
    rows_s[3:4, :] = rows_s[0:1, :] * jnp.exp2(jnp.sum((qf * own_k).T, 0, keepdims=True) * to_exp2)
    rows_s[4:5, :] = jnp.sum((dof * own_v).T, 0, keepdims=True)

    kv_ring.sib(0, b_second, 1 - c, z).wait_recv()
    two_blocks(z, 2 * c + b_first, 2 * (1 - c) + b_second, pass_one)
    blocks_of(0, b_first)
    kv_ring.sib(0, b_first, 1 - c, z).wait_recv()
    two_blocks(z, 2 * c + b_second, 2 * (1 - c) + b_first, pass_one)

    dqt[...] = jnp.zeros_like(dqt)
    got_r[0, 1] = jnp.zeros_like(got_r[0, 1])
    got_l[0, 0] = jnp.zeros_like(got_l[0, 0])
    acc[...] = jnp.zeros_like(acc)

    def gather_step(i, carry):
        b = jnp.where(lax.rem(i, 2) == 0, b_second, b_first)
        k = (i + 1) // 2
        kv_ring.step(k, b)
        blocks_of(k, b)
        return carry

    lax.fori_loop(0, 5, gather_step, 0)
    take_x()
    give_y(0).start()
    give_y(1).start()
    for b, other in ((b_first, b_second), (b_second, b_first)):
        kv_ring.far(b)
        kv_ring.sib(4, other, 1 - c, z + 4).wait_recv()
        two_blocks(z + 4, 2 * c + b, 2 * (1 - c) + other, pass_one)

    total = jnp.sum(sums[0], 0, keepdims=True)
    dot = jnp.sum(sums[1], 0, keepdims=True)
    own_e, own_dp = rows_s[3:4, :], rows_s[4:5, :]
    total = total + own_e
    dot = dot + own_e * own_dp
    inv_row = 1.0 / total
    row_dot = dot * inv_row
    column = lambda v: jnp.broadcast_to(v, (HD, queries)).T
    inv_col = column(inv_row)
    qn_s[...] = (qv[...].astype(F32) * inv_col).astype(BF)
    don_s[...] = (do_v[...].reshape(queries, HD).astype(F32) * inv_col).astype(BF)
    rows_s[1:2, :] = row_dot
    rows_s[2:3, :] = inv_row

    def pass_two(yb, zb):
        s = yb * NZ + zb
        e = e_s[s]
        ds = (e.astype(F32) * (dp_s[s].astype(F32) - rows_s[1:2, :])).astype(BF)
        dv = jnp.dot(e, don_s[...], preferred_element_type=F32)
        dk = jnp.dot(ds, qn_s[...], preferred_element_type=F32) * scale
        dqt[...] += lax.dot_general(kvb[yb, zb, :, :HD], ds, TN, preferred_element_type=F32)
        return jnp.concatenate([dk, dv], 1).astype(BF)

    def swap(i, offset, b):
        at = lax.rem(z + offset + NZ, NZ)
        return rcopy(oth.at[b, at], sib.at[b, at], s_sw.at[i, b], r_sw.at[i, b], (y, z, x, 1 - c))

    def terms(i, offsets, b):
        def one(n, carry):
            at = lax.rem(z + jnp.where(lax.rem(n, 2) == 0, offsets[0], offsets[1]) + NZ, NZ)
            core = jnp.where(n < 2, 1 - c, c)
            value = pass_two(2 * core + b, at)

            @pl.when(n < 2)
            def _():
                oth[b, at] = value
                swap(i + n, at - z, b).start()

            @pl.when(n >= 2)
            def _():
                mine[b, at] = value

            return carry

        lax.fori_loop(0, 4, one, 0)

    def terms_one(i, offset, ready=lambda b: None):
        at = lax.rem(z + offset + NZ, NZ)

        def one(n, carry):
            b = lax.rem(n, 2)
            core = jnp.where(n < 2, 1 - c, c)
            value = pass_two(2 * core + b, at)

            @pl.when(n < 2)
            def _():
                oth[b, at] = value
                swap(i, offset, b).start()

            @pl.when(n >= 2)
            def _():
                mine[b, at] = value
                ready(b)

            return carry

        lax.fori_loop(0, 4, one, 0)

    def chip(offset, half):
        at = lax.rem(z + offset + NZ, NZ)
        return mine[half, at].astype(F32) + sib[half, at].astype(F32)

    def send_r(t, b):
        return rcopy(snd_r.at[t, b], got_r.at[t, b], sr.at[t, b], rr.at[t, b], right)

    def send_l(t, b):
        return rcopy(snd_l.at[t, b], got_l.at[t, b], sq.at[t, b], rq.at[t, b], left)

    def first_sum(b):
        swap(0, 4, b).wait_recv()

        @pl.when(b == 0)
        def _():
            snd_r[0, 0] = chip(4, 0).astype(BF)
            send_r(0, 0).start()

        @pl.when(b == 1)
        def _():
            snd_l[0, 1] = chip(4, 1).astype(BF)
            send_l(0, 1).start()

    terms_one(0, 4, first_sum)

    def sum_step(i, carry):
        t, b = 1 + i // 2, lax.rem(i, 2)
        terms(2 * t - 1, (4 - t, t - 4), b)

        @pl.when(i == 4)
        def _():
            for direction in range(2):
                take_y(direction).wait_recv()
                give_far(direction).start()

        swap(2 * t - 1, 4 - t, b).wait_recv()
        pl.when(i != 1)(lambda: send_r(t - 1, b).wait_recv())
        snd_r[t, b] = (chip(4 - t, b) + got_r[t - 1, b].astype(F32)).astype(BF)
        send_r(t, b).start()
        swap(2 * t, t - 4, b).wait_recv()
        pl.when(i != 0)(lambda: send_l(t - 1, b).wait_recv())
        snd_l[t, b] = (chip(t - 4, b) + got_l[t - 1, b].astype(F32)).astype(BF)
        send_l(t, b).start()
        return carry

    lax.fori_loop(0, 6, sum_step, 0)
    terms_one(7, 0)
    own_p = rows_s[3:4, :] * rows_s[2:3, :]
    own_ds = own_p * (rows_s[4:5, :] - rows_s[1:2, :])
    ds_col = column(own_ds).astype(BF).astype(F32)
    diag[:, :HD] = ds_col * qv[...].astype(F32) * scale
    diag[:, HD:] = column(own_p).astype(BF).astype(F32) * do_v[...].reshape(queries, HD).astype(F32)
    dq = (dqt[...] * rows_s[2:3, :]).T
    q_ring = Chunks(lambda yb, zb: allq.at[yb, zb], sems_q)
    d_ring = Chunks(lambda yb, zb: alld.at[yb, zb], sems_d)

    def norm_back(b, j, upstream):
        normed = hat[b, j]
        return inv[b, j] * (upstream - normed * jnp.mean(normed * upstream, -1, keepdims=True))

    for b in range(2):
        own_kb = kvb[2 * c + b, z, :, :HD].astype(F32)
        dqn = (dq[t_dev * b : t_dev * (b + 1)] + ds_col[t_dev * b : t_dev * (b + 1)] * own_kb) * scale
        allq[2 * c + b, z] = norm_back(b, 0, dqn * gain[0:1, :]).astype(BF)
        q_ring.start(b)
    for b in range(2):
        swap(7, 0, b).wait_recv()
    for b in range(2):
        at = pl.ds(t_dev * b, t_dev)
        send_r(3, b).wait_recv()
        send_l(3, b).wait_recv()
        dkv = chip(0, b) + got_r[3, b].astype(F32) + got_l[3, b].astype(F32) + diag[at, :]
        alld[2 * c + b, z, :, :HD] = norm_back(b, 1, dkv[:, :HD] * gain[1:2, :]).astype(BF)
        alld[2 * c + b, z, :, HD:] = dkv[:, HD:].astype(BF)
        d_ring.start(b)

    for direction in range(2):
        take_far(direction).wait_recv()

    def grads(yb, zb):
        s = yb * NZ + zb
        rows = jnp.concatenate([x3[yb, 0, zb], x3[yb, 1, zb]], 0)
        parts = []
        for clip in range(CLIPS):
            keep = jnp.broadcast_to(jnp.where(clip_ref[s] == clip, 1.0, 0.0), rows.shape).astype(BF)
            parts.append(rows * keep)
        masked = jnp.concatenate(parts, 0)
        acc[:, :HD] += jnp.dot(masked, allq[yb, zb], preferred_element_type=F32)
        acc[:, HD:] += jnp.dot(masked, alld[yb, zb], preferred_element_type=F32)

    for b in range(2):
        q_ring.sib(0, b, 1 - c, z).wait_recv()
        d_ring.sib(0, b, 1 - c, z).wait_recv()
        two_blocks(z, 2 * c + b, 2 * (1 - c) + b, grads)

    def grad_step(i, carry):
        b = lax.rem(i, 2)
        k = i // 2
        q_ring.step(k, b)
        d_ring.step(k, b)
        q_ring.step_sib(k, b)
        d_ring.step_sib(k, b)
        four_blocks(z - 1 - k, 2 * c + b, z + 1 + k, 2 * (1 - c) + b, grads)
        return carry

    lax.fori_loop(0, 6, grad_step, 0)
    for b in range(2):
        q_ring.far(b)
        d_ring.far(b)
    for b in range(2):
        q_ring.sib(4, b, 1 - c, z + 4).wait_recv()
        d_ring.sib(4, b, 1 - c, z + 4).wait_recv()
        two_blocks(z + 4, 2 * c + b, 2 * (1 - c) + b, grads)

    def finish_inputs():
        for d in (1, 3, 2):
            block = blocks[d]

            @pl.when(lax.eq(block // 2, c))
            def _(d=d, block=block):
                for i in range(2):
                    across(d, block, i).wait_send()
                if d != 2:
                    relay(block, near[d]).wait_send()

        @pl.when(at_home)
        def _():
            for i in range(2):
                x_own(0, i).wait_send()
                x_own(1, i).wait_send()
            give_g.wait_send()

        @pl.when(mine_t)
        def _():
            for dz in range(1, NZ):
                give_t(dz, lax.rem(z + dz, NZ)).wait_send()

        for j in range(2):
            src_y = 2 * c + j

            @pl.when(jnp.logical_not(lax.eq(src_y, y)))
            def _(j=j, src_y=src_y):
                hand_w(j, src_y, src_y, j, j).wait_send()
                hand_d(j, src_y, j, j, j).wait_send()

    two = 2 * ROWS
    fisher = jnp.square(acc[0:two]) + jnp.square(acc[two : 2 * two]) + jnp.square(acc[2 * two :])
    for j in range(2):
        fish[j] = fisher[ROWS * j : ROWS * (j + 1)]
    rows = jnp.sum(fisher.reshape(two // 8, 8, 3 * HD), 0)
    part[...] = rows[:, :HD] + rows[:, HD : 2 * HD] + rows[:, 2 * HD :]

    for i, device in enumerate(first):
        rcopy(part, box.at[i], s1.at[i], r1.at[i], device).start()

    def give(j, target, dst_slot, recv_at):
        return rcopy(fish.at[j], own.at[dst_slot], sf.at[j], rf.at[recv_at], (target, z, x, home))

    def keep_own(j):
        return pltpu.make_async_copy(fish.at[j], own.at[slot], sl.at[6])

    for j in range(2):
        target = 2 * c + j

        @pl.when(lax.eq(target, y))
        def _(j=j):
            keep_own(j).start()

        @pl.when(jnp.logical_not(lax.eq(target, y)))
        def _(j=j, target=target):
            give(j, target, slot, slot).start()

    for i, device in enumerate(first):
        rcopy(part, box.at[i], s1.at[i], r1.at[i], device).wait_recv()
    tile[...] = part[...] + jnp.sum(box[...], 0)
    for i, device in enumerate(second):
        rcopy(tile, box2.at[i], s2.at[i], r2.at[i], device).start()

    w_ring.finish()
    kv_ring.finish()
    q_ring.finish()
    d_ring.finish()
    finish_inputs()
    for i, offset in enumerate((4, 3, -3, 2, -2, 1, -1, 0)):
        for b in range(2):
            swap(i, offset, b).wait_send()
    for t in range(4):
        for b in range(2):
            if t or b == 0:
                send_r(t, b).wait_send()
            if t or b == 1:
                send_l(t, b).wait_send()
    for direction in range(2):
        give_y(direction).wait_send()
        give_far(direction).wait_send()

    @pl.when(mine_t)
    def _():
        for dx in range(1, NX):
            give_x(dx).wait_send()

    for j in range(2):
        target = 2 * c + j

        @pl.when(lax.eq(target, y))
        def _(j=j):
            keep_own(j).wait()

        @pl.when(jnp.logical_not(lax.eq(target, y)))
        def _(j=j, target=target):
            give(j, target, j, j).wait_recv()
            give(j, target, j, j).wait_send()

    for i, device in enumerate(second):
        rcopy(tile, box2.at[i], s2.at[i], r2.at[i], device).wait_recv()
    whole = jnp.sum(tile[...] + jnp.sum(box2[...], 0))
    mean_ref[...] = jnp.full(mean_ref.shape, whole / (3 * D * HEADS * HD) + 1e-06)
    get_damp.wait()
    mask_ref[...] = damp_v[...].astype(F32)
    for j in range(3):
        for h in range(2):
            fisher_ref[j, :, HD * h : HD * (h + 1)] = own[h, :, HD * j : HD * (j + 1)]
    for i, device in enumerate(first):
        rcopy(part, box.at[i], s1.at[i], r1.at[i], device).wait_send()
    for i, device in enumerate(second):
        rcopy(tile, box2.at[i], s2.at[i], r2.at[i], device).wait_send()


def shape(dims, dtype=BF):
    return jax.ShapeDtypeStruct(dims, dtype)


def comm(collective, limit=None):
    return pltpu.CompilerParams(collective_id=collective, has_side_effects=True, vmem_limit_bytes=limit)


def on_device(tokens, w_qkv, gains, cotangent, token_clip, key_live, damp_mask):
    y, z, x, c = place()
    n_tok = token_clip.shape[0]
    t_dev = n_tok // (NY * NZ)
    blocks = (NY, NZ, t_dev)
    half = (2, NZ, t_dev, 2 * HD)
    trips = (4, 2, t_dev, 2 * HD)
    queries = 2 * t_dev
    fisher, divisor, mask = pl.pallas_call(
        main_kernel,
        out_shape=(shape((3, ROWS, 2 * HD), F32), shape((ROWS, 2 * HD), F32), shape((ROWS, 2 * HD), F32)),
        in_specs=[ANY, ANY, ANY, ANY, VMEM, VMEM, ANY],
        out_specs=(VMEM,) * 3,
        scratch_shapes=[
            pltpu.VMEM((2, t_dev, D), BF),
            pltpu.VMEM((3, NY, NZ, ROWS, HD), BF),
            pltpu.VMEM((*blocks, 2 * HD), BF),
            pltpu.VMEM((NY * NZ, t_dev, HD), BF),
            pltpu.VMEM((NY * NZ, t_dev, queries), BF),
            pltpu.VMEM((NY * NZ, t_dev, queries), BF),
            pltpu.VMEM((queries, HD), BF),
            pltpu.VMEM((queries, 2 * HD), BF),
            pltpu.VMEM((2, 8, queries), F32),
            pltpu.VMEM(half, BF), pltpu.VMEM(half, BF), pltpu.VMEM(half, BF),
            pltpu.VMEM(trips, BF), pltpu.VMEM(trips, BF), pltpu.VMEM(trips, BF), pltpu.VMEM(trips, BF),
            pltpu.VMEM((2, 2, t_dev, HD), F32), pltpu.VMEM((2, 2, t_dev, HD), F32),
            pltpu.VMEM((queries, 2 * HD), F32),
            pltpu.VMEM((HD, queries), F32),
            pltpu.VMEM((queries, HD), BF), pltpu.VMEM((queries, HD), BF),
            pltpu.VMEM((8, queries), F32),
            pltpu.VMEM((*blocks, HD), BF),
            pltpu.VMEM((*blocks, 2 * HD), BF),
            pltpu.VMEM((NY, 2, NZ, ROWS, t_dev), BF),
            pltpu.VMEM((CLIPS * 2 * ROWS, 3 * HD), F32),
            pltpu.VMEM((2, ROWS, 3 * HD), F32), pltpu.VMEM((2, ROWS, 3 * HD), F32),
            pltpu.VMEM((8, HD), F32), pltpu.VMEM((8, HD), F32),
            pltpu.VMEM((15, 8, HD), F32), pltpu.VMEM((15, 8, HD), F32),
            pltpu.VMEM((2, t_dev, HD), BF),
            pltpu.VMEM((2, HD), F32),
            pltpu.VMEM((t_dev, NZ * ROWS), BF),
            pltpu.VMEM((NZ, ROWS, t_dev), BF),
            pltpu.VMEM((ROWS, 2 * HD), jnp.int32),
            DMA((7,)), DMA((8, 2)), DMA((8, 2)),
            DMA((4, 2)), DMA((4, 2)), DMA((4, 2)), DMA((4, 2)),
            DMA((3,)), DMA((3,)), DMA((2,)), DMA((2,)), DMA((2,)), DMA((2,)), DMA((2,)), DMA((2,)),
            DMA((15,)), DMA((15,)), DMA((15,)), DMA((15,)),
            DMA((2,)), DMA((2,)), DMA((2,)), DMA((2,)), DMA((1,)), DMA((1,)),
            DMA((6,)), DMA((6,)), DMA((3, 2)), DMA((3, 2)), DMA((7,)), DMA((7,)),
            *CHUNK_SEMS, *CHUNK_SEMS, *CHUNK_SEMS, *CHUNK_SEMS,
        ],
        compiler_params=comm(1, 63 * MIB),
        name="main_kernel",
    )(
        tokens, w_qkv, cotangent, gains,
        token_clip.reshape(NY * NZ, 1, t_dev), key_live.reshape(NY * NZ, 1, t_dev), damp_mask,
    )
    ratio = fisher / divisor[None]
    dampened = (w_qkv.astype(F32) / (1.0 + mask[None] * ratio)).astype(BF)
    return ratio, dampened


def solution(mesh):
    grid = Mesh(mesh.devices.reshape(NY, NZ, NX, NC), ("y", "z", "x", "c"))
    seq, head = ("y", "z"), ("x", "c")
    return jax.shard_map(
        on_device,
        mesh=grid,
        in_specs=(
            P(seq, None),
            P(None, seq, head),
            P(None, head),
            P(seq, head),
            P(),
            P(),
            P(seq, head),
        ),
        out_specs=(P(None, seq, head), P(None, seq, head)),
        check_vma=False,
    )
```
